32 devices in a mesh: groups: 2 (over y), ctx: 4 (over z), mp: 4 (over x, core).
Axes of the slice: x: 2, y: 2, z: 4, core: 2. Of those that a mesh axis runs over, the one named last changes fastest.
Arguments:
- block_entry_input: bfloat16 [1536, 2048], P('mp', ('groups', 'ctx')), parts along dimension 1, may hold values from -6 to 6
- first_conv_taps: bfloat16 [3, 768, 1536], P(None, 'mp'), may hold values from -0.09375 to 0.09375
- first_pointwise_weight: bfloat16 [1536, 768], P(None, 'mp'), may hold values from -0.21875 to 0.21875
- second_conv_taps: bfloat16 [3, 768, 1536], P(None, 'mp'), may hold values from -0.09375 to 0.09375
- second_pointwise_weight: bfloat16 [1536, 768], P(None, 'mp'), may hold values from -0.21875 to 0.21875
- grad_heads: bfloat16 [8, 192, 2048], P('mp', 'ctx', 'groups'), parts along dimension 2, may hold values from -6 to 6
Outputs:
- second_block_output: bfloat16 [1536, 2048], P('mp', ('groups', 'ctx')), parts along dimension 1
- entry_input_gradient: bfloat16 [1536, 2048], P('mp', ('groups', 'ctx')), parts along dimension 1
- first_taps_gradient: float32 [6, 768, 1536], P('groups', 'mp', 'ctx'), parts along dimension 0
- first_projection_gradient: float32 [3072, 768], P(('groups', 'ctx'), 'mp'), parts along dimension 0
- second_taps_gradient: float32 [6, 768, 1536], P('groups', 'mp', 'ctx'), parts along dimension 0
- second_projection_gradient: float32 [3072, 768], P(('groups', 'ctx'), 'mp'), parts along dimension 0
The draws below stay inside these ranges and needn't reach their ends.
There are 2 independent parts, one for each index of `groups`. The reference program is written for one: setup_inputs(seed, part) draws one part's arguments, and reference() takes and returns one part's arrays. A program takes and returns all parts, laid end to end along the dimension named above; an argument that names none is the same for every part. Nothing has to cross between parts.
All inputs are finite; a program needn't handle non-finite values.
Results may differ from the reference program's by a relative error of at most 0.034.
Values may be sent and summed in bfloat16 or wider, within the bound.
No kernel may reach another device: no remote copies, remote signals or barrier semaphores. Data moves between devices by JAX's collectives and lax.ppermute only.
A program may use at most 192 MiB of HBM per device.

```python
import jax
import jax.numpy as jnp

HEADS = 8
VAL = 192
H = 768
FIRST_DILATION = 1024
SECOND_DILATION = 2048
C = 1536
BINS = 1024


def raised(values, stream_key, source, target, parts, factor):
    def block_of(dim):
        return (jnp.arange(values.shape[dim]) // (values.shape[dim] // parts)).reshape((-1,) + (1,) * (values.ndim - 1 - dim))

    first = jax.random.permutation(stream_key, parts)[block_of(target)]
    other_side = (block_of(target) + parts // 2) % parts
    return jnp.where((block_of(source) == first) | (block_of(source) == other_side), factor * values, values)


def level_of(stream_key, shape, pieces, low, high):
    def one(axis_at, shards_of):
        draws = jax.random.uniform(jax.random.fold_in(jax.random.fold_in(stream_key, 6), axis_at), (shards_of,), jnp.float32, low / len(pieces), high / len(pieces))
        return jnp.repeat(jnp.exp(draws), shape[axis_at] // shards_of).reshape((-1,) + (1,) * (len(shape) - axis_at - 1))

    level = one(*pieces[0])
    for cut in pieces[1:]:
        level = level * one(*cut)
    return level


def normal_values(key, extent, deviation, limit, cuts=(), dtype=jnp.bfloat16):
    values = jax.random.normal(key, extent, jnp.float32) * deviation
    if len(cuts) > 0:
        values = level_of(key, extent, cuts, -0.22, 0.18) * values
    return jnp.clip(values, min=-limit, max=limit).astype(dtype)


def noise_with(stream_key, extent, deviation, reach, cuts, heavy, dtype=jnp.bfloat16):
    array = deviation * jax.random.normal(stream_key, extent, jnp.float32)
    if cuts:
        array = array * level_of(stream_key, extent, cuts, -0.22, 0.18)
    return jnp.clip(raised(array, jax.random.fold_in(stream_key, 3), *heavy), -reach, reach).astype(dtype)


def setup_inputs(seed: int = 0, part: int = 0) -> dict:
    streams_of = jax.random.split(jax.random.key(seed), 7)
    part_splits = jax.random.split(jax.random.fold_in(streams_of[6], part), 7)
    block_entry_input = noise_with(part_splits[0], (C, BINS), 1.0, 6.0, ((0, 4), (1, 4)), (1, 0, 4, 2.0))
    first_conv_taps = normal_values(streams_of[1], (3, H, C), (3 * C) ** -0.5, 0.09375, ((1, 4),))
    first_pointwise_weight = normal_values(streams_of[2], (C, H), H ** -0.5, 0.21875, ((1, 4),))
    second_conv_taps = normal_values(streams_of[3], (3, H, C), (3 * C) ** -0.5, 0.09375, ((1, 4),))
    second_pointwise_weight = normal_values(streams_of[4], (C, H), H ** -0.5, 0.21875, ((1, 4),))
    grad_heads = normal_values(part_splits[5], (HEADS, VAL, BINS), 1.0, 6.0, ((0, 4), (1, 4)))
    return dict(block_entry_input=block_entry_input, first_conv_taps=first_conv_taps, first_pointwise_weight=first_pointwise_weight, second_conv_taps=second_conv_taps, second_pointwise_weight=second_pointwise_weight, grad_heads=grad_heads)


def gelu_slope(values):
    return jax.jvp(jax.nn.gelu, (values,), (jnp.ones_like(values),))[1]


def displaced(field, offset):
    width = field.shape[1]
    margin = abs(offset)
    padded = jnp.pad(field, ((0, 0), (margin, margin)))
    return padded[:, margin + offset: margin + offset + width]


def residual_block_forward(activations, conv_weight, point_weight, dilation):
    squashed = jax.nn.gelu(activations.astype(jnp.float32)).astype(jnp.bfloat16)
    pre_act = jnp.zeros((conv_weight.shape[1], activations.shape[1]), jnp.float32)
    for position in range(3):
        pre_act = pre_act + jnp.dot(conv_weight[position], displaced(squashed, (position - 1) * dilation), preferred_element_type=jnp.float32)
    hidden = jax.nn.gelu(pre_act).astype(jnp.bfloat16)
    mixed = jnp.dot(point_weight, hidden, preferred_element_type=jnp.float32)
    result = (activations.astype(jnp.float32) + mixed).astype(jnp.bfloat16)
    return result, squashed, pre_act, hidden


def residual_block_backward(incoming_gradient, activations, squashed, pre_act, hidden, conv_weight, point_weight, dilation):
    grad_hidden = jnp.dot(point_weight.T, incoming_gradient, preferred_element_type=jnp.float32)
    grad_pre = (grad_hidden * gelu_slope(pre_act)).astype(jnp.bfloat16)
    moved = [displaced(grad_pre, -(position - 1) * dilation) for position in range(3)]
    grad_conv = jnp.stack([jnp.dot(moved[position], squashed.T, preferred_element_type=jnp.float32) for position in range(3)])
    grad_point = jnp.dot(incoming_gradient, hidden.T, preferred_element_type=jnp.float32)
    grad_squash = jnp.zeros((conv_weight.shape[2], incoming_gradient.shape[1]), jnp.float32)
    for position in range(3):
        grad_squash = grad_squash + jnp.dot(conv_weight[position].T, moved[position], preferred_element_type=jnp.float32)
    previous = (incoming_gradient.astype(jnp.float32) + grad_squash * gelu_slope(activations.astype(jnp.float32))).astype(jnp.bfloat16)
    return previous, grad_conv, grad_point


def reference(block_entry_input, first_conv_taps, first_pointwise_weight, second_conv_taps, second_pointwise_weight, grad_heads):
    between_blocks_state, first_gelu_output, first_preactivation, first_hidden_state = residual_block_forward(block_entry_input, first_conv_taps, first_pointwise_weight, FIRST_DILATION)
    second_block_output, second_gelu_output, second_preactivation, second_hidden_state = residual_block_forward(between_blocks_state, second_conv_taps, second_pointwise_weight, SECOND_DILATION)
    incoming_gradient = grad_heads.reshape(HEADS * VAL, BINS)
    incoming_gradient, second_taps_gradient, second_projection_gradient = residual_block_backward(incoming_gradient, between_blocks_state, second_gelu_output, second_preactivation, second_hidden_state, second_conv_taps, second_pointwise_weight, SECOND_DILATION)
    entry_input_gradient, first_taps_gradient, first_projection_gradient = residual_block_backward(incoming_gradient, block_entry_input, first_gelu_output, first_preactivation, first_hidden_state, first_conv_taps, first_pointwise_weight, FIRST_DILATION)
    return second_block_output, entry_input_gradient, first_taps_gradient, first_projection_gradient, second_taps_gradient, second_projection_gradient
```

```python
import jax
import jax.numpy as jnp
from jax import lax
from jax.experimental import pallas as pl
from jax.experimental.pallas import tpu as pltpu
from jax.sharding import PartitionSpec as P

FIRST_DILATION = 1024
SECOND_DILATION = 2048
F32 = jnp.float32
BF16 = jnp.bfloat16
ROOT = 0.7978845608028654
CUBIC = 0.044715


def shifted(value, axis, by):
    length = lax.axis_size(axis)
    pairs = [(i, i + by) for i in range(length) if 0 <= i + by < length]
    return lax.ppermute(value, axis, pairs)


def gelu_slope(values):
    return jax.jvp(jax.nn.gelu, (values,), (jnp.ones_like(values),))[1]


def contract_first(left, right):
    return lax.dot_general(
        left, right, (((0,), (0,)), ((), ())), preferred_element_type=jnp.float32
    )


def contract_last(left, right):
    return lax.dot_general(
        left, right, (((1,), (1,)), ((), ())), preferred_element_type=jnp.float32
    )


def hop_steps(activations, dilation):
    return dilation // activations.shape[1]


def residual_block_forward(activations, conv_weight, point_weight, dilation):
    hop_count = hop_steps(activations, dilation)
    squash_part = jax.nn.gelu(activations.astype(jnp.float32)).astype(jnp.bfloat16)
    squashed = lax.all_gather(squash_part, "mp", axis=0, tiled=True)
    earlier = shifted(squashed, "ctx", hop_count)
    later = shifted(squashed, "ctx", -hop_count)
    pre_act = jnp.dot(conv_weight[0], earlier, preferred_element_type=jnp.float32)
    pre_act = pre_act + jnp.dot(conv_weight[1], squashed, preferred_element_type=jnp.float32)
    pre_act = pre_act + jnp.dot(conv_weight[2], later, preferred_element_type=jnp.float32)
    hidden = jax.nn.gelu(pre_act).astype(jnp.bfloat16)
    mixed = lax.psum_scatter(
        jnp.dot(point_weight, hidden, preferred_element_type=jnp.float32).astype(jnp.bfloat16),
        "mp",
        scatter_dimension=0,
        tiled=True,
    ).astype(jnp.float32)
    result = (activations.astype(jnp.float32) + mixed).astype(jnp.bfloat16)
    return (result, squashed, pre_act, hidden)


def residual_block_backward(
    incoming_gradient, activations, squashed, pre_act, hidden, conv_weight, point_weight, dilation
):
    hop_count = hop_steps(activations, dilation)
    upstream_full = lax.all_gather(incoming_gradient, "mp", axis=0, tiled=True)
    grad_hidden = contract_first(point_weight, upstream_full)
    grad_pre = (grad_hidden * gelu_slope(pre_act)).astype(jnp.bfloat16)
    grad_later = shifted(grad_pre, "ctx", -hop_count)
    grad_earlier = shifted(grad_pre, "ctx", hop_count)
    moved = (grad_later, grad_pre, grad_earlier)
    grad_conv = jnp.stack([contract_last(part, squashed) for part in moved])
    grad_point = contract_last(upstream_full, hidden)
    total = contract_first(conv_weight[0], moved[0])
    total = total + contract_first(conv_weight[1], moved[1])
    grad_squash = lax.psum_scatter(
        (total + contract_first(conv_weight[2], moved[2])).astype(jnp.bfloat16),
        "mp",
        scatter_dimension=0,
        tiled=True,
    ).astype(jnp.float32)
    previous = (
        incoming_gradient.astype(jnp.float32)
        + grad_squash * gelu_slope(activations.astype(jnp.float32))
    ).astype(jnp.bfloat16)
    return (previous, grad_conv, grad_point)


def reduce_block(grad_conv, grad_point):
    return (
        lax.psum_scatter(
            grad_conv.astype(jnp.bfloat16), "ctx", scatter_dimension=2, tiled=True
        ).astype(jnp.float32),
        lax.psum_scatter(
            grad_point.astype(jnp.bfloat16), "ctx", scatter_dimension=0, tiled=True
        ).astype(jnp.float32),
    )


def general_shards(x, taps_a, point_a, taps_b, point_b, grad_heads):
    regrouped = lax.all_to_all(grad_heads, "ctx", split_axis=2, concat_axis=1, tiled=True)
    gradient = regrouped.reshape(regrouped.shape[0] * regrouped.shape[1], regrouped.shape[2])
    middle, z_a, u_a, v_a = residual_block_forward(x, taps_a, point_a, FIRST_DILATION)
    result, z_b, u_b, v_b = residual_block_forward(middle, taps_b, point_b, SECOND_DILATION)
    gradient, conv_b, proj_b = residual_block_backward(
        gradient, middle, z_b, u_b, v_b, taps_b, point_b, SECOND_DILATION
    )
    conv_b, proj_b = reduce_block(conv_b, proj_b)
    gradient, conv_a, proj_a = residual_block_backward(
        gradient, x, z_a, u_a, v_a, taps_a, point_a, FIRST_DILATION
    )
    conv_a, proj_a = reduce_block(conv_a, proj_a)
    return result, gradient, conv_a, proj_a, conv_b, proj_b


def swap(value, axis, bits):
    size = lax.axis_size(axis)
    return lax.ppermute(value, axis, [(i, i ^ bits) for i in range(size)])


def dot(left, right, dims=((1,), (0,))):
    return lax.dot_general(left, right, (dims, ((), ())), preferred_element_type=F32)


def gelu(s):
    return 0.5 * s * (1.0 + jnp.tanh(ROOT * (s + CUBIC * (s * s * s))))


def gelu_and_slope(s):
    sq = s * s
    t = jnp.tanh(ROOT * (s + CUBIC * (s * sq)))
    half = 0.5 * (1.0 + t)
    slope = half + 0.5 * s * (1.0 - t * t) * (ROOT * (1.0 + 3.0 * CUBIC * sq))
    return s * half, slope


def slope_of(s):
    return gelu_and_slope(s)[1]


def call(body, outs, args, name, specs=None, scratch=()):
    return pl.pallas_call(
        body,
        out_shape=[jax.ShapeDtypeStruct(s, d) for s, d in outs],
        in_specs=specs or [whole(a.shape) for a in args],
        out_specs=[whole(s) for s, _ in outs],
        grid=(1,),
        scratch_shapes=scratch,
        name=name,
    )(*args)


def whole(shape):
    return pl.BlockSpec(shape, lambda _: (0,) * len(shape))


def fast_shards(x, taps_a, point_a, taps_b, point_b, grad_heads):
    rows, bins = x.shape
    hid, chans = taps_a.shape[1], taps_a.shape[2]
    heads, val, _ = grad_heads.shape
    tap = pl.BlockSpec((None, hid, chans), lambda _: (1, 0, 0))
    tile = whole((rows, bins))
    pair = whole((2, rows, bins))
    point = whole(point_a.shape)

    def block(m, j):
        return pl.ds(pl.multiple_of((m ^ j) * rows, rows), rows)

    def split_body(g_ref, *outs):
        c = lax.axis_index("ctx")
        for k in range(4):
            outs[k][...] = g_ref[:, :, pl.ds(pl.multiple_of((c ^ k) * bins, bins), bins)]

    pieces = call(split_body, [((heads, val, bins), BF16)] * 4, (grad_heads,), "split_grad")
    pieces = [pieces[0]] + [swap(pieces[k], "ctx", k) for k in (1, 2, 3)]

    def join_body(*refs):
        c = lax.axis_index("ctx")
        out = refs[4]
        for k in range(4):
            out[:, c ^ k] = refs[k][...]

    (g_own,) = call(join_body, [((heads, 4, val, bins), BF16)], pieces, "join_grad")
    g_own = g_own.reshape(rows, bins)
    g_far = swap(g_own, "mp", 2)
    g_near = swap(g_own, "mp", 1)
    g_cross = swap(g_far, "mp", 1)

    x_far = swap(x, "mp", 2)
    x_near = swap(x, "mp", 1)
    x_cross = swap(x_far, "mp", 1)

    def first_body(x0, x1, x2, x3, k_ref, p_ref, z_ref, v_ref, s_ref, keep_ref, send_ref):
        m = lax.axis_index("mp")
        u = jnp.zeros((hid, bins), F32)
        for j, ref in enumerate((x0, x1, x2, x3)):
            z = gelu(ref[...].astype(F32)).astype(BF16)
            z_ref[j] = z
            u = u + dot(k_ref[:, block(m, j)], z)
        v, slope = gelu_and_slope(u)
        v = v.astype(BF16)
        v_ref[...] = v
        s_ref[...] = slope
        for i, j in enumerate((1, 3)):
            send_ref[i] = dot(p_ref[block(m, j), :], v).astype(BF16)
        for i, j in enumerate((0, 2)):
            keep_ref[i] = dot(p_ref[block(m, j), :], v)

    z_a, v_a, slope_a, keep, send = call(
        first_body,
        [
            ((4, rows, bins), BF16),
            ((hid, bins), BF16),
            ((hid, bins), F32),
            ((2, rows, bins), F32),
            ((2, rows, bins), BF16),
        ],
        (x, x_near, x_far, x_cross, taps_a, point_a),
        "first_forward",
        [tile, tile, tile, tile, tap, point],
    )
    got = swap(send, "mp", 1)

    def near_body(keep_ref, got_ref, out_ref):
        out_ref[...] = (keep_ref[...] + got_ref[...].astype(F32)).astype(BF16)

    def near_sum(keep, got, name):
        return call(near_body, [((2, rows, bins), BF16)], (keep, got), name)[0]

    chip = near_sum(keep, got, "mix_sum")
    other = swap(chip, "mp", 2)

    def middle_body(x0, x2, chip_ref, other_ref, out_ref):
        for i, ref in enumerate((x0, x2)):
            mixed = chip_ref[i].astype(F32) + other_ref[1 - i].astype(F32)
            out_ref[i] = (ref[...].astype(F32) + mixed).astype(BF16)

    (mid,) = call(
        middle_body, [((2, rows, bins), BF16)], (x, x_far, chip, other), "middle"
    )
    mid_near = swap(mid, "mp", 1)

    def second_body(
        a_ref, b_ref, g0, g1, g2, g3, k_ref, p_ref,
        z_ref, v_ref, gu_ref, keep_ref, send_ref, ykeep_ref, ysend_ref,
    ):
        m = lax.axis_index("mp")
        u = jnp.zeros((hid, bins), F32)
        for j in range(4):
            part = (a_ref, b_ref)[j & 1][j >> 1]
            z = gelu(part.astype(F32)).astype(BF16)
            z_ref[j] = z
            u = u + dot(k_ref[:, block(m, j)], z)
        v, slope = gelu_and_slope(u)
        v = v.astype(BF16)
        v_ref[...] = v
        gv = jnp.zeros((hid, bins), F32)
        for j, ref in enumerate((g0, g1, g2, g3)):
            gv = gv + dot(p_ref[block(m, j), :], ref[...], ((0,), (0,)))
        gu = (gv * slope).astype(BF16)
        gu_ref[...] = gu
        for i, j in enumerate((1, 3)):
            send_ref[i] = dot(k_ref[:, block(m, j)], gu, ((0,), (0,))).astype(BF16)
        for i, j in enumerate((0, 2)):
            keep_ref[i] = dot(k_ref[:, block(m, j)], gu, ((0,), (0,)))
        for i, j in enumerate((1, 3)):
            ysend_ref[i] = dot(p_ref[block(m, j), :], v).astype(BF16)
        for i, j in enumerate((0, 2)):
            ykeep_ref[i] = dot(p_ref[block(m, j), :], v)

    z_b, v_b, gu_b, keep, send, ykeep, ysend = call(
        second_body,
        [
            ((4, rows, bins), BF16),
            ((hid, bins), BF16),
            ((hid, bins), BF16),
            ((2, rows, bins), F32),
            ((2, rows, bins), BF16),
            ((2, rows, bins), F32),
            ((2, rows, bins), BF16),
        ],
        (mid, mid_near, g_own, g_near, g_far, g_cross, taps_b, point_b),
        "second_block",
        [pair, pair, tile, tile, tile, tile, tap, point],
    )
    got = swap(send, "mp", 1)
    chip = near_sum(keep, got, "squash_sum")
    other = swap(chip, "mp", 2)

    def back_body(g0, g2, mid_ref, chip_ref, other_ref, out_ref):
        for i, ref in enumerate((g0, g2)):
            grad = chip_ref[i].astype(F32) + other_ref[1 - i].astype(F32)
            out_ref[i] = (
                ref[...].astype(F32) + grad * slope_of(mid_ref[i].astype(F32))
            ).astype(BF16)

    (g_mid,) = call(
        back_body, [((2, rows, bins), BF16)], (g_own, g_far, mid, chip, other), "middle_grad"
    )
    g_mid_near = swap(g_mid, "mp", 1)

    ygot = swap(ysend, "mp", 1)

    def last_sum_body(keep_ref, got_ref, own_ref, send_ref):
        own_ref[...] = keep_ref[0] + got_ref[0].astype(F32)
        send_ref[...] = (keep_ref[1] + got_ref[1].astype(F32)).astype(BF16)

    def last_sum(keep, got, name):
        return call(
            last_sum_body, [((rows, bins), F32), ((rows, bins), BF16)], (keep, got), name
        )

    y_own, y_send = last_sum(ykeep, ygot, "out_sum")
    y_got = swap(y_send, "mp", 2)

    def out_body(mid_ref, own_ref, got_ref, out_ref):
        mixed = own_ref[...] + got_ref[...].astype(F32)
        out_ref[...] = (mid_ref[0].astype(F32) + mixed).astype(BF16)

    (second_out,) = call(out_body, [((rows, bins), BF16)], (mid, y_own, y_got), "out")

    def first_back_body(a_ref, b_ref, k_ref, p_ref, s_ref, gu_ref, keep_ref, send_ref):
        m = lax.axis_index("mp")
        gv = jnp.zeros((hid, bins), F32)
        for j in range(4):
            part = (a_ref, b_ref)[j & 1][j >> 1]
            gv = gv + dot(p_ref[block(m, j), :], part, ((0,), (0,)))
        gu = (gv * s_ref[...]).astype(BF16)
        gu_ref[...] = gu
        for i, j in enumerate((1, 3)):
            send_ref[i] = dot(k_ref[:, block(m, j)], gu, ((0,), (0,))).astype(BF16)
        for i, j in enumerate((0, 2)):
            keep_ref[i] = dot(k_ref[:, block(m, j)], gu, ((0,), (0,)))

    gu_a, keep, send = call(
        first_back_body,
        [((hid, bins), BF16), ((2, rows, bins), F32), ((2, rows, bins), BF16)],
        (g_mid, g_mid_near, taps_a, point_a, slope_a),
        "first_backward",
        [pair, pair, tap, point, whole((hid, bins))],
    )
    got = swap(send, "mp", 1)
    e_own, e_send = last_sum(keep, got, "entry_sum")
    e_got = swap(e_send, "mp", 2)

    def entry_body(g_ref, x_ref, own_ref, got_ref, out_ref):
        grad = own_ref[...] + got_ref[...].astype(F32)
        out_ref[...] = (
            g_ref[0].astype(F32) + grad * slope_of(x_ref[...].astype(F32))
        ).astype(BF16)

    (entry,) = call(entry_body, [((rows, bins), BF16)], (g_mid, x, e_own, e_got), "entry")

    def weight_body(z_ref, gu_ref, v_ref, g0, g1, g2, g3, own_ref, *rest):
        outs, g_ref = rest[:3], rest[3]
        m = lax.axis_index("mp")
        c = lax.axis_index("ctx")
        for j, ref in enumerate((g0, g1, g2, g3)):
            g_ref[j] = ref[...]
        for k in (1, 2, 3, 0):
            j = m ^ c ^ k
            taps = dot(gu_ref[...], z_ref[j], ((1,), (1,)))
            proj = dot(v_ref[...], g_ref[j], ((1,), (1,)))
            out = own_ref if k == 0 else outs[k - 1]
            out[:hid, :] = taps.astype(out.dtype)
            out[hid:, :] = proj.astype(out.dtype)

    def weights(z, gu, v, grads, specs, name):
        own, *sends = call(
            weight_body,
            [((2 * hid, rows), F32)] + [((2 * hid, rows), BF16)] * 3,
            (z, gu, v, *grads),
            name,
            [whole(z.shape), whole(gu.shape), whole(v.shape), *specs],
            [pltpu.VMEM((4, rows, bins), BF16)],
        )
        gots = [swap(part, "ctx", k + 1) for k, part in enumerate(sends)]

        def total_body(own_ref, r1, r2, r3, taps_ref, proj_ref):
            def total(part):
                return own_ref[part, :] + (
                    r1[part, :].astype(F32) + r2[part, :].astype(F32) + r3[part, :].astype(F32)
                )

            taps_ref[0] = jnp.zeros((hid, rows), F32)
            taps_ref[1] = total(pl.ds(0, hid))
            taps_ref[2] = jnp.zeros((hid, rows), F32)
            proj_ref[...] = total(pl.ds(hid, hid)).T

        return call(
            total_body,
            [((3, hid, rows), F32), ((rows, hid), F32)],
            (own, *gots),
            name + "_total",
        )

    taps_b_grad, point_b_grad = weights(
        z_b, gu_b, v_b, (g_own, g_near, g_far, g_cross), [tile] * 4, "second_weights"
    )
    upper = [pl.BlockSpec((None, rows, bins), lambda _, i=i: (i, 0, 0)) for i in (0, 1)]
    taps_a_grad, point_a_grad = weights(
        z_a,
        gu_a,
        v_a,
        (g_mid, g_mid_near, g_mid, g_mid_near),
        [upper[0], upper[0], upper[1], upper[1]],
        "first_weights",
    )
    return second_out, entry, taps_a_grad, point_a_grad, taps_b_grad, point_b_grad


def solution(mesh):
    sizes = dict(mesh.shape)

    def shards(x, *rest):
        span = x.shape[1] * sizes["ctx"]
        fast = (
            min(FIRST_DILATION, SECOND_DILATION) >= span
            and sizes["mp"] == 4
            and sizes["ctx"] == 4
        )
        return (fast_shards if fast else general_shards)(x, *rest)

    return jax.shard_map(
        shards,
        mesh=mesh,
        in_specs=(
            P("mp", ("groups", "ctx")),
            P(None, "mp", None),
            P(None, "mp"),
            P(None, "mp", None),
            P(None, "mp"),
            P("mp", "ctx", "groups"),
        ),
        out_specs=(
            P("mp", ("groups", "ctx")),
            P("mp", ("groups", "ctx")),
            P("groups", "mp", "ctx"),
            P(("groups", "ctx"), "mp"),
            P("groups", "mp", "ctx"),
            P(("groups", "ctx"), "mp"),
        ),
        check_vma=False,
    )
```

```python
import functools

import jax
import jax.numpy as jnp
from jax import lax
from jax.experimental import pallas as pl
from jax.experimental.pallas import tpu as pltpu
from jax.sharding import PartitionSpec as P

FIRST_DILATION = 1024
SECOND_DILATION = 2048
F32 = jnp.float32
BF16 = jnp.bfloat16
ROOT = 0.7978845608028654
CUBIC = 0.044715


def shifted(value, axis, by):
    length = lax.axis_size(axis)
    pairs = [(i, i + by) for i in range(length) if 0 <= i + by < length]
    return lax.ppermute(value, axis, pairs)


def gelu_slope(values):
    return jax.jvp(jax.nn.gelu, (values,), (jnp.ones_like(values),))[1]


def contract_first(left, right):
    return lax.dot_general(
        left, right, (((0,), (0,)), ((), ())), preferred_element_type=jnp.float32
    )


def contract_last(left, right):
    return lax.dot_general(
        left, right, (((1,), (1,)), ((), ())), preferred_element_type=jnp.float32
    )


def hop_steps(activations, dilation):
    return dilation // activations.shape[1]


def residual_block_forward(activations, conv_weight, point_weight, dilation):
    hop_count = hop_steps(activations, dilation)
    squash_part = jax.nn.gelu(activations.astype(jnp.float32)).astype(jnp.bfloat16)
    squashed = lax.all_gather(squash_part, "mp", axis=0, tiled=True)
    earlier = shifted(squashed, "ctx", hop_count)
    later = shifted(squashed, "ctx", -hop_count)
    pre_act = jnp.dot(conv_weight[0], earlier, preferred_element_type=jnp.float32)
    pre_act = pre_act + jnp.dot(conv_weight[1], squashed, preferred_element_type=jnp.float32)
    pre_act = pre_act + jnp.dot(conv_weight[2], later, preferred_element_type=jnp.float32)
    hidden = jax.nn.gelu(pre_act).astype(jnp.bfloat16)
    mixed = lax.psum_scatter(
        jnp.dot(point_weight, hidden, preferred_element_type=jnp.float32).astype(jnp.bfloat16),
        "mp",
        scatter_dimension=0,
        tiled=True,
    ).astype(jnp.float32)
    result = (activations.astype(jnp.float32) + mixed).astype(jnp.bfloat16)
    return (result, squashed, pre_act, hidden)


def residual_block_backward(
    incoming_gradient, activations, squashed, pre_act, hidden, conv_weight, point_weight, dilation
):
    hop_count = hop_steps(activations, dilation)
    upstream_full = lax.all_gather(incoming_gradient, "mp", axis=0, tiled=True)
    grad_hidden = contract_first(point_weight, upstream_full)
    grad_pre = (grad_hidden * gelu_slope(pre_act)).astype(jnp.bfloat16)
    grad_later = shifted(grad_pre, "ctx", -hop_count)
    grad_earlier = shifted(grad_pre, "ctx", hop_count)
    moved = (grad_later, grad_pre, grad_earlier)
    grad_conv = jnp.stack([contract_last(part, squashed) for part in moved])
    grad_point = contract_last(upstream_full, hidden)
    total = contract_first(conv_weight[0], moved[0])
    total = total + contract_first(conv_weight[1], moved[1])
    grad_squash = lax.psum_scatter(
        (total + contract_first(conv_weight[2], moved[2])).astype(jnp.bfloat16),
        "mp",
        scatter_dimension=0,
        tiled=True,
    ).astype(jnp.float32)
    previous = (
        incoming_gradient.astype(jnp.float32)
        + grad_squash * gelu_slope(activations.astype(jnp.float32))
    ).astype(jnp.bfloat16)
    return (previous, grad_conv, grad_point)


def reduce_block(grad_conv, grad_point):
    return (
        lax.psum_scatter(
            grad_conv.astype(jnp.bfloat16), "ctx", scatter_dimension=2, tiled=True
        ).astype(jnp.float32),
        lax.psum_scatter(
            grad_point.astype(jnp.bfloat16), "ctx", scatter_dimension=0, tiled=True
        ).astype(jnp.float32),
    )


def general_shards(x, taps_a, point_a, taps_b, point_b, grad_heads):
    regrouped = lax.all_to_all(grad_heads, "ctx", split_axis=2, concat_axis=1, tiled=True)
    gradient = regrouped.reshape(regrouped.shape[0] * regrouped.shape[1], regrouped.shape[2])
    middle, z_a, u_a, v_a = residual_block_forward(x, taps_a, point_a, FIRST_DILATION)
    result, z_b, u_b, v_b = residual_block_forward(middle, taps_b, point_b, SECOND_DILATION)
    gradient, conv_b, proj_b = residual_block_backward(
        gradient, middle, z_b, u_b, v_b, taps_b, point_b, SECOND_DILATION
    )
    conv_b, proj_b = reduce_block(conv_b, proj_b)
    gradient, conv_a, proj_a = residual_block_backward(
        gradient, x, z_a, u_a, v_a, taps_a, point_a, FIRST_DILATION
    )
    conv_a, proj_a = reduce_block(conv_a, proj_a)
    return result, gradient, conv_a, proj_a, conv_b, proj_b


def swap(value, axis, bits):
    size = lax.axis_size(axis)
    return lax.ppermute(value, axis, [(i, i ^ bits) for i in range(size)])


def dot(left, right, dims=((1,), (0,))):
    return lax.dot_general(left, right, (dims, ((), ())), preferred_element_type=F32)


def gelu(s):
    return 0.5 * s * (1.0 + jnp.tanh(ROOT * (s + CUBIC * (s * s * s))))


def gelu_and_slope(s):
    sq = s * s
    t = jnp.tanh(ROOT * (s + CUBIC * (s * sq)))
    half = 0.5 * (1.0 + t)
    slope = half + 0.5 * s * (1.0 - t * t) * (ROOT * (1.0 + 3.0 * CUBIC * sq))
    return s * half, slope


def slope_of(s):
    return gelu_and_slope(s)[1]


VMEM = pl.BlockSpec(memory_space=pltpu.VMEM)


def call(body, outs, args, name, scratch=(), final=False):
    struct = jax.ShapeDtypeStruct if final else pltpu.VMEM
    return pl.pallas_call(
        body,
        out_shape=[struct(s, d) for s, d in outs],
        in_specs=[VMEM] * len(args),
        out_specs=[VMEM] * len(outs),
        scratch_shapes=scratch,
        compiler_params=pltpu.CompilerParams(vmem_limit_bytes=16 << 20),
        name=name,
    )(*[pltpu.with_memory_space_constraint(a, pltpu.VMEM) for a in args])


def fast_shards(x, taps_a, point_a, taps_b, point_b, grad_heads):
    rows, bins = x.shape
    hid, chans = taps_a.shape[1], taps_a.shape[2]
    heads, val, _ = grad_heads.shape
    tap_a, tap_b = taps_a[1], taps_b[1]
    cols_a, cols_b = point_a.T, point_b.T

    def block(m, j):
        return pl.ds(pl.multiple_of((m ^ j) * rows, rows), rows)

    def split_body(g_ref, *outs):
        c = lax.axis_index("ctx")
        for k in range(4):
            outs[k][...] = g_ref[:, :, pl.ds(pl.multiple_of((c ^ k) * bins, bins), bins)]

    pieces = call(split_body, [((heads, val, bins), BF16)] * 4, (grad_heads,), "split_grad")
    pieces = [pieces[0]] + [swap(pieces[k], "ctx", k) for k in (1, 2, 3)]

    def join_body(*refs):
        c = lax.axis_index("ctx")
        out = refs[4]
        for k in range(4):
            out[:, c ^ k] = refs[k][...]

    (g_own,) = call(join_body, [((heads, 4, val, bins), BF16)], pieces, "join_grad")
    g_own = g_own.reshape(rows, bins)
    g_far = swap(g_own, "mp", 2)
    g_near = swap(g_own, "mp", 1)
    g_cross = swap(g_far, "mp", 1)

    x_far = swap(x, "mp", 2)
    x_near = swap(x, "mp", 1)
    x_cross = swap(x_far, "mp", 1)

    def first_body(x0, x1, x2, x3, k_ref, p_ref, z_ref, v_ref, s_ref, keep_ref, send_ref):
        m = lax.axis_index("mp")
        u = jnp.zeros((hid, bins), F32)
        for j, ref in enumerate((x0, x1, x2, x3)):
            z = gelu(ref[...].astype(F32)).astype(BF16)
            z_ref[j] = z
            u = u + dot(k_ref[:, block(m, j)], z)
        v, slope = gelu_and_slope(u)
        v = v.astype(BF16)
        v_ref[...] = v
        s_ref[...] = slope
        for i, j in enumerate((1, 3)):
            send_ref[i] = dot(p_ref[:, block(m, j)], v, ((0,), (0,))).astype(BF16)
        for i, j in enumerate((0, 2)):
            keep_ref[i] = dot(p_ref[:, block(m, j)], v, ((0,), (0,)))

    z_a, v_a, slope_a, keep, send = call(
        first_body,
        [
            ((4, rows, bins), BF16),
            ((hid, bins), BF16),
            ((hid, bins), F32),
            ((2, rows, bins), F32),
            ((2, rows, bins), BF16),
        ],
        (x, x_near, x_far, x_cross, tap_a, cols_a),
        "first_forward",
    )
    got = swap(send, "mp", 1)

    def near_body(keep_ref, got_ref, out_ref):
        out_ref[...] = (keep_ref[...] + got_ref[...].astype(F32)).astype(BF16)

    def near_sum(keep, got, name):
        return call(near_body, [((2, rows, bins), BF16)], (keep, got), name)[0]

    chip = near_sum(keep, got, "mix_sum")
    other = swap(chip, "mp", 2)

    def middle_body(x0, x2, chip_ref, other_ref, out_ref):
        for i, ref in enumerate((x0, x2)):
            mixed = chip_ref[i].astype(F32) + other_ref[1 - i].astype(F32)
            out_ref[i] = (ref[...].astype(F32) + mixed).astype(BF16)

    (mid,) = call(
        middle_body, [((2, rows, bins), BF16)], (x, x_far, chip, other), "middle"
    )
    mid_near = swap(mid, "mp", 1)

    def second_body(
        a_ref, b_ref, g0, g1, g2, g3, k_ref, p_ref,
        z_ref, v_ref, gu_ref, keep_ref, send_ref, ykeep_ref, ysend_ref,
    ):
        m = lax.axis_index("mp")
        u = jnp.zeros((hid, bins), F32)
        for j in range(4):
            part = (a_ref, b_ref)[j & 1][j >> 1]
            z = gelu(part.astype(F32)).astype(BF16)
            z_ref[j] = z
            u = u + dot(k_ref[:, block(m, j)], z)
        v, slope = gelu_and_slope(u)
        v = v.astype(BF16)
        v_ref[...] = v
        gv = jnp.zeros((hid, bins), F32)
        for j, ref in enumerate((g0, g1, g2, g3)):
            gv = gv + dot(p_ref[:, block(m, j)], ref[...])
        gu = (gv * slope).astype(BF16)
        gu_ref[...] = gu
        for i, j in enumerate((1, 3)):
            send_ref[i] = dot(k_ref[:, block(m, j)], gu, ((0,), (0,))).astype(BF16)
        for i, j in enumerate((0, 2)):
            keep_ref[i] = dot(k_ref[:, block(m, j)], gu, ((0,), (0,)))
        for i, j in enumerate((1, 3)):
            ysend_ref[i] = dot(p_ref[:, block(m, j)], v, ((0,), (0,))).astype(BF16)
        for i, j in enumerate((0, 2)):
            ykeep_ref[i] = dot(p_ref[:, block(m, j)], v, ((0,), (0,)))

    z_b, v_b, gu_b, keep, send, ykeep, ysend = call(
        second_body,
        [
            ((4, rows, bins), BF16),
            ((hid, bins), BF16),
            ((hid, bins), BF16),
            ((2, rows, bins), F32),
            ((2, rows, bins), BF16),
            ((2, rows, bins), F32),
            ((2, rows, bins), BF16),
        ],
        (mid, mid_near, g_own, g_near, g_far, g_cross, tap_b, cols_b),
        "second_block",
    )
    got = swap(send, "mp", 1)
    chip = near_sum(keep, got, "squash_sum")
    other = swap(chip, "mp", 2)

    def back_body(g0, g2, mid_ref, chip_ref, other_ref, out_ref):
        for i, ref in enumerate((g0, g2)):
            grad = chip_ref[i].astype(F32) + other_ref[1 - i].astype(F32)
            out_ref[i] = (
                ref[...].astype(F32) + grad * slope_of(mid_ref[i].astype(F32))
            ).astype(BF16)

    (g_mid,) = call(
        back_body, [((2, rows, bins), BF16)], (g_own, g_far, mid, chip, other), "middle_grad"
    )
    g_mid_near = swap(g_mid, "mp", 1)

    ygot = swap(ysend, "mp", 1)

    def last_sum_body(keep_ref, got_ref, own_ref, send_ref):
        own_ref[...] = keep_ref[0] + got_ref[0].astype(F32)
        send_ref[...] = (keep_ref[1] + got_ref[1].astype(F32)).astype(BF16)

    def last_sum(keep, got, name):
        return call(
            last_sum_body, [((rows, bins), F32), ((rows, bins), BF16)], (keep, got), name
        )

    y_own, y_send = last_sum(ykeep, ygot, "out_sum")
    y_got = swap(y_send, "mp", 2)

    def out_body(mid_ref, own_ref, got_ref, out_ref):
        mixed = own_ref[...] + got_ref[...].astype(F32)
        out_ref[...] = (mid_ref[0].astype(F32) + mixed).astype(BF16)

    (second_out,) = call(out_body, [((rows, bins), BF16)], (mid, y_own, y_got), "out", final=True)

    def first_back_body(a_ref, b_ref, k_ref, p_ref, s_ref, gu_ref, keep_ref, send_ref):
        m = lax.axis_index("mp")
        gv = jnp.zeros((hid, bins), F32)
        for j in range(4):
            part = (a_ref, b_ref)[j & 1][j >> 1]
            gv = gv + dot(p_ref[:, block(m, j)], part)
        gu = (gv * s_ref[...]).astype(BF16)
        gu_ref[...] = gu
        for i, j in enumerate((1, 3)):
            send_ref[i] = dot(k_ref[:, block(m, j)], gu, ((0,), (0,))).astype(BF16)
        for i, j in enumerate((0, 2)):
            keep_ref[i] = dot(k_ref[:, block(m, j)], gu, ((0,), (0,)))

    gu_a, keep, send = call(
        first_back_body,
        [((hid, bins), BF16), ((2, rows, bins), F32), ((2, rows, bins), BF16)],
        (g_mid, g_mid_near, tap_a, cols_a, slope_a),
        "first_backward",
    )
    got = swap(send, "mp", 1)
    e_own, e_send = last_sum(keep, got, "entry_sum")
    e_got = swap(e_send, "mp", 2)

    def entry_body(g_ref, x_ref, own_ref, got_ref, out_ref):
        grad = own_ref[...] + got_ref[...].astype(F32)
        out_ref[...] = (
            g_ref[0].astype(F32) + grad * slope_of(x_ref[...].astype(F32))
        ).astype(BF16)

    (entry,) = call(entry_body, [((rows, bins), BF16)], (g_mid, x, e_own, e_got), "entry", final=True)

    def weight_body(fill, z_ref, gu_ref, v_ref, *rest):
        grads, (own_ref, *outs, g_ref) = rest[:-5], rest[-5:]
        m = lax.axis_index("mp")
        c = lax.axis_index("ctx")
        fill(g_ref, grads)
        for k in (1, 2, 3, 0):
            j = m ^ c ^ k
            taps = dot(gu_ref[...], z_ref[j], ((1,), (1,)))
            proj = dot(v_ref[...], g_ref[j], ((1,), (1,)))
            out = own_ref if k == 0 else outs[k - 1]
            out[:hid, :] = taps.astype(out.dtype)
            out[hid:, :] = proj.astype(out.dtype)

    def fill_tiles(g_ref, grads):
        for j, ref in enumerate(grads):
            g_ref[j] = ref[...]

    def fill_pairs(g_ref, grads):
        for j in range(4):
            g_ref[j] = grads[j & 1][j >> 1]

    def weights(z, gu, v, grads, fill, name):
        own, *sends = call(
            functools.partial(weight_body, fill),
            [((2 * hid, rows), F32)] + [((2 * hid, rows), BF16)] * 3,
            (z, gu, v, *grads),
            name,
            [pltpu.VMEM((4, rows, bins), BF16)],
        )
        gots = [swap(part, "ctx", k + 1) for k, part in enumerate(sends)]

        def total_body(own_ref, r1, r2, r3, taps_ref, proj_ref):
            def total(part):
                return own_ref[part, :] + (
                    r1[part, :].astype(F32) + r2[part, :].astype(F32) + r3[part, :].astype(F32)
                )

            taps_ref[0] = jnp.zeros((hid, rows), F32)
            taps_ref[1] = total(pl.ds(0, hid))
            taps_ref[2] = jnp.zeros((hid, rows), F32)
            proj_ref[...] = total(pl.ds(hid, hid))

        taps, proj = call(
            total_body,
            [((3, hid, rows), F32), ((hid, rows), F32)],
            (own, *gots),
            name + "_total",
            final=True,
        )
        return taps, proj.T

    taps_b_grad, point_b_grad = weights(
        z_b, gu_b, v_b, (g_own, g_near, g_far, g_cross), fill_tiles, "second_weights"
    )
    taps_a_grad, point_a_grad = weights(
        z_a, gu_a, v_a, (g_mid, g_mid_near), fill_pairs, "first_weights"
    )
    return second_out, entry, taps_a_grad, point_a_grad, taps_b_grad, point_b_grad


def solution(mesh):
    sizes = dict(mesh.shape)

    def shards(x, *rest):
        span = x.shape[1] * sizes["ctx"]
        fast = (
            min(FIRST_DILATION, SECOND_DILATION) >= span
            and sizes["mp"] == 4
            and sizes["ctx"] == 4
        )
        return (fast_shards if fast else general_shards)(x, *rest)

    return jax.shard_map(
        shards,
        mesh=mesh,
        in_specs=(
            P("mp", ("groups", "ctx")),
            P(None, "mp", None),
            P(None, "mp"),
            P(None, "mp", None),
            P(None, "mp"),
            P("mp", "ctx", "groups"),
        ),
        out_specs=(
            P("mp", ("groups", "ctx")),
            P("mp", ("groups", "ctx")),
            P("groups", "mp", "ctx"),
            P(("groups", "ctx"), "mp"),
            P("groups", "mp", "ctx"),
            P(("groups", "ctx"), "mp"),
        ),
        check_vma=False,
    )
```

```python
import functools

import jax
import jax.numpy as jnp
from jax import lax
from jax.experimental import pallas as pl
from jax.experimental.pallas import tpu as pltpu
from jax.sharding import PartitionSpec as P

FIRST_DILATION = 1024
SECOND_DILATION = 2048
F32 = jnp.float32
BF16 = jnp.bfloat16
ROOT = 0.7978845608028654
CUBIC = 0.044715


def shifted(value, axis, by):
    length = lax.axis_size(axis)
    pairs = [(i, i + by) for i in range(length) if 0 <= i + by < length]
    return lax.ppermute(value, axis, pairs)


def gelu_slope(values):
    return jax.jvp(jax.nn.gelu, (values,), (jnp.ones_like(values),))[1]


def contract_first(left, right):
    return lax.dot_general(
        left, right, (((0,), (0,)), ((), ())), preferred_element_type=jnp.float32
    )


def contract_last(left, right):
    return lax.dot_general(
        left, right, (((1,), (1,)), ((), ())), preferred_element_type=jnp.float32
    )


def hop_steps(activations, dilation):
    return dilation // activations.shape[1]


def residual_block_forward(activations, conv_weight, point_weight, dilation):
    hop_count = hop_steps(activations, dilation)
    squash_part = jax.nn.gelu(activations.astype(jnp.float32)).astype(jnp.bfloat16)
    squashed = lax.all_gather(squash_part, "mp", axis=0, tiled=True)
    earlier = shifted(squashed, "ctx", hop_count)
    later = shifted(squashed, "ctx", -hop_count)
    pre_act = jnp.dot(conv_weight[0], earlier, preferred_element_type=jnp.float32)
    pre_act = pre_act + jnp.dot(conv_weight[1], squashed, preferred_element_type=jnp.float32)
    pre_act = pre_act + jnp.dot(conv_weight[2], later, preferred_element_type=jnp.float32)
    hidden = jax.nn.gelu(pre_act).astype(jnp.bfloat16)
    mixed = lax.psum_scatter(
        jnp.dot(point_weight, hidden, preferred_element_type=jnp.float32).astype(jnp.bfloat16),
        "mp",
        scatter_dimension=0,
        tiled=True,
    ).astype(jnp.float32)
    result = (activations.astype(jnp.float32) + mixed).astype(jnp.bfloat16)
    return (result, squashed, pre_act, hidden)


def residual_block_backward(
    incoming_gradient, activations, squashed, pre_act, hidden, conv_weight, point_weight, dilation
):
    hop_count = hop_steps(activations, dilation)
    upstream_full = lax.all_gather(incoming_gradient, "mp", axis=0, tiled=True)
    grad_hidden = contract_first(point_weight, upstream_full)
    grad_pre = (grad_hidden * gelu_slope(pre_act)).astype(jnp.bfloat16)
    grad_later = shifted(grad_pre, "ctx", -hop_count)
    grad_earlier = shifted(grad_pre, "ctx", hop_count)
    moved = (grad_later, grad_pre, grad_earlier)
    grad_conv = jnp.stack([contract_last(part, squashed) for part in moved])
    grad_point = contract_last(upstream_full, hidden)
    total = contract_first(conv_weight[0], moved[0])
    total = total + contract_first(conv_weight[1], moved[1])
    grad_squash = lax.psum_scatter(
        (total + contract_first(conv_weight[2], moved[2])).astype(jnp.bfloat16),
        "mp",
        scatter_dimension=0,
        tiled=True,
    ).astype(jnp.float32)
    previous = (
        incoming_gradient.astype(jnp.float32)
        + grad_squash * gelu_slope(activations.astype(jnp.float32))
    ).astype(jnp.bfloat16)
    return (previous, grad_conv, grad_point)


def reduce_block(grad_conv, grad_point):
    return (
        lax.psum_scatter(
            grad_conv.astype(jnp.bfloat16), "ctx", scatter_dimension=2, tiled=True
        ).astype(jnp.float32),
        lax.psum_scatter(
            grad_point.astype(jnp.bfloat16), "ctx", scatter_dimension=0, tiled=True
        ).astype(jnp.float32),
    )


def general_shards(x, taps_a, point_a, taps_b, point_b, grad_heads):
    regrouped = lax.all_to_all(grad_heads, "ctx", split_axis=2, concat_axis=1, tiled=True)
    gradient = regrouped.reshape(regrouped.shape[0] * regrouped.shape[1], regrouped.shape[2])
    middle, z_a, u_a, v_a = residual_block_forward(x, taps_a, point_a, FIRST_DILATION)
    result, z_b, u_b, v_b = residual_block_forward(middle, taps_b, point_b, SECOND_DILATION)
    gradient, conv_b, proj_b = residual_block_backward(
        gradient, middle, z_b, u_b, v_b, taps_b, point_b, SECOND_DILATION
    )
    conv_b, proj_b = reduce_block(conv_b, proj_b)
    gradient, conv_a, proj_a = residual_block_backward(
        gradient, x, z_a, u_a, v_a, taps_a, point_a, FIRST_DILATION
    )
    conv_a, proj_a = reduce_block(conv_a, proj_a)
    return result, gradient, conv_a, proj_a, conv_b, proj_b


def swap(value, axis, bits):
    size = lax.axis_size(axis)
    return lax.ppermute(value, axis, [(i, i ^ bits) for i in range(size)])


def dot(left, right, dims=((1,), (0,))):
    return lax.dot_general(left, right, (dims, ((), ())), preferred_element_type=F32)


def gelu(s):
    return 0.5 * s * (1.0 + jnp.tanh(ROOT * (s + CUBIC * (s * s * s))))


def gelu_and_slope(s):
    sq = s * s
    t = jnp.tanh(ROOT * (s + CUBIC * (s * sq)))
    half = 0.5 * (1.0 + t)
    slope = half + 0.5 * s * (1.0 - t * t) * (ROOT * (1.0 + 3.0 * CUBIC * sq))
    return s * half, slope


def slope_of(s):
    return gelu_and_slope(s)[1]


VMEM = pl.BlockSpec(memory_space=pltpu.VMEM)


def call(body, outs, args, name, scratch=(), final=False):
    struct = jax.ShapeDtypeStruct if final else pltpu.VMEM
    return pl.pallas_call(
        body,
        out_shape=[struct(s, d) for s, d in outs],
        in_specs=[VMEM] * len(args),
        out_specs=[VMEM] * len(outs),
        scratch_shapes=scratch,
        compiler_params=pltpu.CompilerParams(vmem_limit_bytes=16 << 20),
        name=name,
    )(*[pltpu.with_memory_space_constraint(a, pltpu.VMEM) for a in args])


def fast_shards(x, taps_a, point_a, taps_b, point_b, grad_heads):
    rows, bins = x.shape
    hid, chans = taps_a.shape[1], taps_a.shape[2]
    heads, val, _ = grad_heads.shape
    def block(m, j):
        return pl.ds(pl.multiple_of((m ^ j) * rows, rows), rows)

    x_far = swap(x, "mp", 2)
    x_near = swap(x, "mp", 1)

    def load_body(x_ref, ta, tb, ca, cb, g_ref, *rest):
        outs, sems = rest[:-1], rest[-1]
        c = lax.axis_index("ctx")
        sources = [x_ref, ta.at[1], tb.at[1], ca, cb]
        for k in range(4):
            at = pl.multiple_of((c ^ k) * bins, bins)
            sources.append(g_ref.at[:, :, pl.ds(at, bins)])
        copies = [
            pltpu.make_async_copy(source, out, sems.at[i])
            for i, (source, out) in enumerate(zip(sources, outs))
        ]
        for copy in copies:
            copy.start()
        for copy in copies:
            copy.wait()

    weight = ((hid, chans), BF16)
    piece = ((heads, val, bins), BF16)
    x_own, tap_a, tap_b, cols_a, cols_b, *pieces = pl.pallas_call(
        load_body,
        out_shape=[pltpu.VMEM((rows, bins), BF16)]
        + [pltpu.VMEM(*weight)] * 4
        + [pltpu.VMEM(*piece)] * 4,
        in_specs=[pl.BlockSpec(memory_space=pltpu.HBM)] * 6,
        out_specs=[VMEM] * 9,
        scratch_shapes=[pltpu.SemaphoreType.DMA((9,))],
        compiler_params=pltpu.CompilerParams(vmem_limit_bytes=16 << 20),
        name="load",
    )(
        *[
            pltpu.with_memory_space_constraint(source, pltpu.HBM)
            for source in (x, taps_a, taps_b, point_a.T, point_b.T, grad_heads)
        ]
    )
    pieces = [pieces[0]] + [swap(pieces[k], "ctx", k) for k in (1, 2, 3)]
    x_far, x_own = lax.optimization_barrier((x_far, x_own))
    x_cross = swap(x_far, "mp", 1)

    def join_body(*refs):
        c = lax.axis_index("ctx")
        out = refs[4]
        for k in range(4):
            out[:, c ^ k] = refs[k][...]

    (g_own,) = call(join_body, [((heads, 4, val, bins), BF16)], pieces, "join_grad")
    g_own = g_own.reshape(rows, bins)
    g_far = swap(g_own, "mp", 2)
    g_near = swap(g_own, "mp", 1)
    g_cross = swap(g_far, "mp", 1)

    def first_body(x0, x1, x2, x3, k_ref, p_ref, _, z_ref, v_ref, s_ref, keep_ref, send_ref):
        m = lax.axis_index("mp")
        u = jnp.zeros((hid, bins), F32)
        for j, ref in enumerate((x0, x1, x2, x3)):
            z = gelu(ref[...].astype(F32)).astype(BF16)
            z_ref[j] = z
            u = u + dot(k_ref[:, block(m, j)], z)
        v, slope = gelu_and_slope(u)
        v = v.astype(BF16)
        v_ref[...] = v
        s_ref[...] = slope
        for i, j in enumerate((1, 3)):
            send_ref[i] = dot(p_ref[:, block(m, j)], v, ((0,), (0,))).astype(BF16)
        for i, j in enumerate((0, 2)):
            keep_ref[i] = dot(p_ref[:, block(m, j)], v, ((0,), (0,)))

    z_a, v_a, slope_a, keep, send = call(
        first_body,
        [
            ((4, rows, bins), BF16),
            ((hid, bins), BF16),
            ((hid, bins), F32),
            ((2, rows, bins), F32),
            ((2, rows, bins), BF16),
        ],
        (x_own, x_near, x_far, x_cross, tap_a, cols_a, g_own),
        "first_forward",
    )
    got = swap(send, "mp", 1)

    def near_body(keep_ref, got_ref, *rest):
        rest[-1][...] = (keep_ref[...] + got_ref[...].astype(F32)).astype(BF16)

    def near_sum(keep, got, name, after=()):
        return call(near_body, [((2, rows, bins), BF16)], (keep, got, *after), name)[0]

    chip = near_sum(keep, got, "mix_sum")
    other = swap(chip, "mp", 2)

    def middle_body(x0, x2, chip_ref, other_ref, out_ref):
        for i, ref in enumerate((x0, x2)):
            mixed = chip_ref[i].astype(F32) + other_ref[1 - i].astype(F32)
            out_ref[i] = (ref[...].astype(F32) + mixed).astype(BF16)

    (mid,) = call(
        middle_body, [((2, rows, bins), BF16)], (x_own, x_far, chip, other), "middle"
    )
    mid_near = swap(mid, "mp", 1)

    def second_body(
        a_ref, b_ref, g0, g1, g2, g3, k_ref, p_ref,
        z_ref, v_ref, gu_ref, keep_ref, send_ref, ykeep_ref, ysend_ref,
    ):
        m = lax.axis_index("mp")
        u = jnp.zeros((hid, bins), F32)
        for j in range(4):
            part = (a_ref, b_ref)[j & 1][j >> 1]
            z = gelu(part.astype(F32)).astype(BF16)
            z_ref[j] = z
            u = u + dot(k_ref[:, block(m, j)], z)
        v, slope = gelu_and_slope(u)
        v = v.astype(BF16)
        v_ref[...] = v
        gv = jnp.zeros((hid, bins), F32)
        for j, ref in enumerate((g0, g1, g2, g3)):
            gv = gv + dot(p_ref[:, block(m, j)], ref[...])
        gu = (gv * slope).astype(BF16)
        gu_ref[...] = gu
        for i, j in enumerate((1, 3)):
            send_ref[i] = dot(k_ref[:, block(m, j)], gu, ((0,), (0,))).astype(BF16)
        for i, j in enumerate((0, 2)):
            keep_ref[i] = dot(k_ref[:, block(m, j)], gu, ((0,), (0,)))
        for i, j in enumerate((1, 3)):
            ysend_ref[i] = dot(p_ref[:, block(m, j)], v, ((0,), (0,))).astype(BF16)
        for i, j in enumerate((0, 2)):
            ykeep_ref[i] = dot(p_ref[:, block(m, j)], v, ((0,), (0,)))

    z_b, v_b, gu_b, keep, send, ykeep, ysend = call(
        second_body,
        [
            ((4, rows, bins), BF16),
            ((hid, bins), BF16),
            ((hid, bins), BF16),
            ((2, rows, bins), F32),
            ((2, rows, bins), BF16),
            ((2, rows, bins), F32),
            ((2, rows, bins), BF16),
        ],
        (mid, mid_near, g_own, g_near, g_far, g_cross, tap_b, cols_b),
        "second_block",
    )
    def weight_body(fill, z_ref, gu_ref, v_ref, *rest):
        grads, (keep_k, keep_p, send_k, send_p, g_ref) = rest[:-5], rest[-5:]
        j = lax.axis_index("mp") ^ lax.axis_index("ctx")
        fill(g_ref, grads)

        def taps(k):
            return dot(gu_ref[...], z_ref[j ^ k], ((1,), (1,)))

        def proj(k):
            return dot(v_ref[...], g_ref[j ^ k], ((1,), (1,)))

        for i, k in enumerate((1, 3)):
            send_k[i] = taps(k).astype(BF16)
        for i, k in enumerate((2, 3)):
            send_p[i] = proj(k).astype(BF16)
        for i, k in enumerate((0, 2)):
            keep_k[i] = taps(k)
        for i, k in enumerate((0, 1)):
            keep_p[i] = proj(k)

    def fill_tiles(g_ref, grads):
        for j, ref in enumerate(grads):
            g_ref[j] = ref[...]

    def fill_pairs(g_ref, grads):
        for j in range(4):
            g_ref[j] = grads[j & 1][j >> 1]

    two = (2, hid, rows)

    def weights(z, gu, v, grads, fill, name):
        return call(
            functools.partial(weight_body, fill),
            [(two, F32), (two, F32), (two, BF16), (two, BF16)],
            (z, gu, v, *grads),
            name,
            [pltpu.VMEM((4, rows, bins), BF16)],
        )

    def half_body(keep_k, keep_p, got_k, got_p, own_k, own_p, send_k, send_p):
        own_k[...] = keep_k[0] + got_k[0].astype(F32)
        own_p[...] = keep_p[0] + got_p[0].astype(F32)
        send_k[...] = (keep_k[1] + got_k[1].astype(F32)).astype(BF16)
        send_p[...] = (keep_p[1] + got_p[1].astype(F32)).astype(BF16)

    def first_swap(send_k, send_p):
        return swap(send_k, "ctx", 1), swap(send_p, "ctx", 2)

    def half_sum(keep_k, keep_p, got_k, got_p, name):
        one = (hid, rows)
        return call(
            half_body,
            [(one, F32), (one, F32), (one, BF16), (one, BF16)],
            (keep_k, keep_p, got_k, got_p),
            name,
        )

    def total_body(own_k, own_p, got_k, got_p, taps_ref, proj_ref):
        taps_ref[0] = jnp.zeros((hid, rows), F32)
        taps_ref[1] = own_k[...] + got_k[...].astype(F32)
        taps_ref[2] = jnp.zeros((hid, rows), F32)
        proj_ref[...] = own_p[...] + got_p[...].astype(F32)

    def total(own_k, own_p, got_k, got_p, name):
        taps, proj = call(
            total_body,
            [((3, hid, rows), F32), ((hid, rows), F32)],
            (own_k, own_p, got_k, got_p),
            name,
            final=True,
        )
        return taps, proj.T

    parts_b = weights(
        z_b, gu_b, v_b, (g_own, g_near, g_far, g_cross), fill_tiles, "second_weights"
    )
    got = swap(send, "mp", 1)
    chip = near_sum(keep, got, "squash_sum", parts_b[:1])
    other = swap(chip, "mp", 2)
    other, *got_b = lax.optimization_barrier((other, *first_swap(*parts_b[2:])))
    parts_b = half_sum(*parts_b[:2], *got_b, "second_half")
    parts_b = (*parts_b[:2], swap(parts_b[2], "ctx", 2), swap(parts_b[3], "ctx", 1))

    def back_body(g0, g2, mid_ref, chip_ref, other_ref, out_ref):
        for i, ref in enumerate((g0, g2)):
            grad = chip_ref[i].astype(F32) + other_ref[1 - i].astype(F32)
            out_ref[i] = (
                ref[...].astype(F32) + grad * slope_of(mid_ref[i].astype(F32))
            ).astype(BF16)

    (g_mid,) = call(
        back_body, [((2, rows, bins), BF16)], (g_own, g_far, mid, chip, other), "middle_grad"
    )
    g_mid_near = swap(g_mid, "mp", 1)

    ygot = swap(ysend, "mp", 1)

    def last_sum_body(keep_ref, got_ref, own_ref, send_ref):
        own_ref[...] = keep_ref[0] + got_ref[0].astype(F32)
        send_ref[...] = (keep_ref[1] + got_ref[1].astype(F32)).astype(BF16)

    def last_sum(keep, got, name):
        return call(
            last_sum_body, [((rows, bins), F32), ((rows, bins), BF16)], (keep, got), name
        )

    y_own, y_send = last_sum(ykeep, ygot, "out_sum")
    y_got = swap(y_send, "mp", 2)

    def out_body(mid_ref, own_ref, got_ref, out_ref):
        mixed = own_ref[...] + got_ref[...].astype(F32)
        out_ref[...] = (mid_ref[0].astype(F32) + mixed).astype(BF16)

    (second_out,) = call(out_body, [((rows, bins), BF16)], (mid, y_own, y_got), "out", final=True)

    def first_back_body(a_ref, b_ref, k_ref, p_ref, s_ref, _a, _b, gu_ref, keep_ref, send_ref):
        m = lax.axis_index("mp")
        gv = jnp.zeros((hid, bins), F32)
        for j in range(4):
            part = (a_ref, b_ref)[j & 1][j >> 1]
            gv = gv + dot(p_ref[:, block(m, j)], part)
        gu = (gv * s_ref[...]).astype(BF16)
        gu_ref[...] = gu
        for i, j in enumerate((1, 3)):
            send_ref[i] = dot(k_ref[:, block(m, j)], gu, ((0,), (0,))).astype(BF16)
        for i, j in enumerate((0, 2)):
            keep_ref[i] = dot(k_ref[:, block(m, j)], gu, ((0,), (0,)))

    gu_a, keep, send = call(
        first_back_body,
        [((hid, bins), BF16), ((2, rows, bins), F32), ((2, rows, bins), BF16)],
        (g_mid, g_mid_near, tap_a, cols_a, slope_a, *parts_b[2:]),
        "first_backward",
    )
    parts_a = weights(z_a, gu_a, v_a, (g_mid, g_mid_near), fill_pairs, "first_weights")
    got = swap(send, "mp", 1)
    e_own, e_send = last_sum(keep, got, "entry_sum")
    e_got = swap(e_send, "mp", 2)

    def entry_body(g_ref, x_ref, own_ref, got_ref, out_ref):
        grad = own_ref[...] + got_ref[...].astype(F32)
        out_ref[...] = (
            g_ref[0].astype(F32) + grad * slope_of(x_ref[...].astype(F32))
        ).astype(BF16)

    (entry,) = call(entry_body, [((rows, bins), BF16)], (g_mid, x_own, e_own, e_got), "entry", final=True)

    taps_b_grad, point_b_grad = total(*parts_b, "second_total")
    parts_a = half_sum(*parts_a[:2], *first_swap(*parts_a[2:]), "first_half")
    parts_a = (*parts_a[:2], swap(parts_a[2], "ctx", 2), swap(parts_a[3], "ctx", 1))
    taps_a_grad, point_a_grad = total(*parts_a, "first_total")
    return second_out, entry, taps_a_grad, point_a_grad, taps_b_grad, point_b_grad


def solution(mesh):
    sizes = dict(mesh.shape)

    def shards(x, *rest):
        span = x.shape[1] * sizes["ctx"]
        fast = (
            min(FIRST_DILATION, SECOND_DILATION) >= span
            and sizes["mp"] == 4
            and sizes["ctx"] == 4
        )
        return (fast_shards if fast else general_shards)(x, *rest)

    return jax.shard_map(
        shards,
        mesh=mesh,
        in_specs=(
            P("mp", ("groups", "ctx")),
            P(None, "mp", None),
            P(None, "mp"),
            P(None, "mp", None),
            P(None, "mp"),
            P("mp", "ctx", "groups"),
        ),
        out_specs=(
            P("mp", ("groups", "ctx")),
            P("mp", ("groups", "ctx")),
            P("groups", "mp", "ctx"),
            P(("groups", "ctx"), "mp"),
            P("groups", "mp", "ctx"),
            P(("groups", "ctx"), "mp"),
        ),
        check_vma=False,
    )
```

```python
import jax
import jax.numpy as jnp
from jax import lax
from jax.experimental import pallas as pl
from jax.experimental.pallas import tpu as pltpu
from jax.sharding import PartitionSpec as P

FIRST_DILATION = 1024
SECOND_DILATION = 2048
F32 = jnp.float32
BF16 = jnp.bfloat16
ROOT = 0.7978845608028654
CUBIC = 0.044715


def shifted(value, axis, by):
    length = lax.axis_size(axis)
    pairs = [(i, i + by) for i in range(length) if 0 <= i + by < length]
    return lax.ppermute(value, axis, pairs)


def gelu_slope(values):
    return jax.jvp(jax.nn.gelu, (values,), (jnp.ones_like(values),))[1]


def contract_first(left, right):
    return lax.dot_general(
        left, right, (((0,), (0,)), ((), ())), preferred_element_type=jnp.float32
    )


def contract_last(left, right):
    return lax.dot_general(
        left, right, (((1,), (1,)), ((), ())), preferred_element_type=jnp.float32
    )


def hop_steps(activations, dilation):
    return dilation // activations.shape[1]


def residual_block_forward(activations, conv_weight, point_weight, dilation):
    hop_count = hop_steps(activations, dilation)
    squash_part = jax.nn.gelu(activations.astype(jnp.float32)).astype(jnp.bfloat16)
    squashed = lax.all_gather(squash_part, "mp", axis=0, tiled=True)
    earlier = shifted(squashed, "ctx", hop_count)
    later = shifted(squashed, "ctx", -hop_count)
    pre_act = jnp.dot(conv_weight[0], earlier, preferred_element_type=jnp.float32)
    pre_act = pre_act + jnp.dot(conv_weight[1], squashed, preferred_element_type=jnp.float32)
    pre_act = pre_act + jnp.dot(conv_weight[2], later, preferred_element_type=jnp.float32)
    hidden = jax.nn.gelu(pre_act).astype(jnp.bfloat16)
    mixed = lax.psum_scatter(
        jnp.dot(point_weight, hidden, preferred_element_type=jnp.float32).astype(jnp.bfloat16),
        "mp",
        scatter_dimension=0,
        tiled=True,
    ).astype(jnp.float32)
    result = (activations.astype(jnp.float32) + mixed).astype(jnp.bfloat16)
    return (result, squashed, pre_act, hidden)


def residual_block_backward(
    incoming_gradient, activations, squashed, pre_act, hidden, conv_weight, point_weight, dilation
):
    hop_count = hop_steps(activations, dilation)
    upstream_full = lax.all_gather(incoming_gradient, "mp", axis=0, tiled=True)
    grad_hidden = contract_first(point_weight, upstream_full)
    grad_pre = (grad_hidden * gelu_slope(pre_act)).astype(jnp.bfloat16)
    grad_later = shifted(grad_pre, "ctx", -hop_count)
    grad_earlier = shifted(grad_pre, "ctx", hop_count)
    moved = (grad_later, grad_pre, grad_earlier)
    grad_conv = jnp.stack([contract_last(part, squashed) for part in moved])
    grad_point = contract_last(upstream_full, hidden)
    total = contract_first(conv_weight[0], moved[0])
    total = total + contract_first(conv_weight[1], moved[1])
    grad_squash = lax.psum_scatter(
        (total + contract_first(conv_weight[2], moved[2])).astype(jnp.bfloat16),
        "mp",
        scatter_dimension=0,
        tiled=True,
    ).astype(jnp.float32)
    previous = (
        incoming_gradient.astype(jnp.float32)
        + grad_squash * gelu_slope(activations.astype(jnp.float32))
    ).astype(jnp.bfloat16)
    return (previous, grad_conv, grad_point)


def reduce_block(grad_conv, grad_point):
    return (
        lax.psum_scatter(
            grad_conv.astype(jnp.bfloat16), "ctx", scatter_dimension=2, tiled=True
        ).astype(jnp.float32),
        lax.psum_scatter(
            grad_point.astype(jnp.bfloat16), "ctx", scatter_dimension=0, tiled=True
        ).astype(jnp.float32),
    )


def general_shards(x, taps_a, point_a, taps_b, point_b, grad_heads):
    regrouped = lax.all_to_all(grad_heads, "ctx", split_axis=2, concat_axis=1, tiled=True)
    gradient = regrouped.reshape(regrouped.shape[0] * regrouped.shape[1], regrouped.shape[2])
    middle, z_a, u_a, v_a = residual_block_forward(x, taps_a, point_a, FIRST_DILATION)
    result, z_b, u_b, v_b = residual_block_forward(middle, taps_b, point_b, SECOND_DILATION)
    gradient, conv_b, proj_b = residual_block_backward(
        gradient, middle, z_b, u_b, v_b, taps_b, point_b, SECOND_DILATION
    )
    conv_b, proj_b = reduce_block(conv_b, proj_b)
    gradient, conv_a, proj_a = residual_block_backward(
        gradient, x, z_a, u_a, v_a, taps_a, point_a, FIRST_DILATION
    )
    conv_a, proj_a = reduce_block(conv_a, proj_a)
    return result, gradient, conv_a, proj_a, conv_b, proj_b


def swap(value, axis, bits):
    size = lax.axis_size(axis)
    return lax.ppermute(value, axis, [(i, i ^ bits) for i in range(size)])


def dot(left, right, dims=((1,), (0,))):
    return lax.dot_general(left, right, (dims, ((), ())), preferred_element_type=F32)


def gelu(s):
    return 0.5 * s * (1.0 + jnp.tanh(ROOT * (s + CUBIC * (s * s * s))))


def gelu_and_slope(s):
    sq = s * s
    t = jnp.tanh(ROOT * (s + CUBIC * (s * sq)))
    half = 0.5 * (1.0 + t)
    slope = half + 0.5 * s * (1.0 - t * t) * (ROOT * (1.0 + 3.0 * CUBIC * sq))
    return s * half, slope


def slope_of(s):
    return gelu_and_slope(s)[1]


VMEM = pl.BlockSpec(memory_space=pltpu.VMEM)


def call(body, outs, args, name, scratch=(), final=False):
    struct = jax.ShapeDtypeStruct if final else pltpu.VMEM
    return pl.pallas_call(
        body,
        out_shape=[struct(s, d) for s, d in outs],
        in_specs=[VMEM] * len(args),
        out_specs=[VMEM] * len(outs),
        scratch_shapes=scratch,
        compiler_params=pltpu.CompilerParams(vmem_limit_bytes=16 << 20),
        name=name,
    )(*[pltpu.with_memory_space_constraint(a, pltpu.VMEM) for a in args])


def fast_shards(x, taps_a, point_a, taps_b, point_b, grad_heads):
    rows, bins = x.shape
    hid, chans = taps_a.shape[1], taps_a.shape[2]
    heads, val, _ = grad_heads.shape
    def block(m, j):
        return pl.ds(pl.multiple_of((m ^ j) * rows, rows), rows)

    x_far = swap(x, "mp", 2)
    x_near = swap(x, "mp", 1)

    raw_far = swap(grad_heads, "mp", 2)

    def load_body(x_ref, ta, tb, ca, cb, g_ref, *rest):
        outs, sems = rest[:-1], rest[-1]
        sources = [x_ref, ta.at[1], tb.at[1], ca, cb, g_ref]
        copies = [
            pltpu.make_async_copy(source, out, sems.at[i])
            for i, (source, out) in enumerate(zip(sources, outs))
        ]
        for copy in copies:
            copy.start()
        for copy in copies:
            copy.wait()

    x_own, tap_a, tap_b, cols_a, cols_b, raw_own = pl.pallas_call(
        load_body,
        out_shape=[pltpu.VMEM((rows, bins), BF16)]
        + [pltpu.VMEM((hid, chans), BF16)] * 4
        + [pltpu.VMEM(grad_heads.shape, BF16)],
        in_specs=[pl.BlockSpec(memory_space=pltpu.HBM)] * 6,
        out_specs=[VMEM] * 6,
        scratch_shapes=[pltpu.SemaphoreType.DMA((6,))],
        compiler_params=pltpu.CompilerParams(vmem_limit_bytes=16 << 20),
        name="load",
    )(
        *[
            pltpu.with_memory_space_constraint(source, pltpu.HBM)
            for source in (x, taps_a, taps_b, point_a.T, point_b.T, grad_heads)
        ]
    )
    x_far, x_own = lax.optimization_barrier((x_far, x_own))
    x_cross = swap(x_far, "mp", 1)

    def split_body(own_ref, far_ref, *outs):
        c = lax.axis_index("ctx")
        for k in range(4):
            at = pl.ds(pl.multiple_of((c ^ k) * bins, bins), bins)
            for i, ref in enumerate((own_ref, far_ref)):
                outs[k][i] = ref[:, :, at]

    piece = ((2, heads, val, bins), BF16)
    pieces = call(split_body, [piece] * 4, (raw_own, raw_far), "split_grad")
    pieces = [pieces[0]] + [swap(pieces[k], "ctx", k) for k in (1, 2, 3)]

    def join_body(*refs):
        c = lax.axis_index("ctx")
        out = refs[4]
        for k in range(4):
            out[:, :, c ^ k] = refs[k][...]

    (g_pair,) = call(join_body, [((2, heads, 4, val, bins), BF16)], pieces, "join_grad")
    g_pair = g_pair.reshape(2, rows, bins)
    g_near = swap(g_pair, "mp", 1)

    def first_body(x0, x1, x2, x3, k_ref, p_ref, _, z_ref, v_ref, s_ref, keep_ref, send_ref):
        m = lax.axis_index("mp")
        u = jnp.zeros((hid, bins), F32)
        for j, ref in enumerate((x0, x1, x2, x3)):
            z = gelu(ref[...].astype(F32)).astype(BF16)
            z_ref[j] = z
            u = u + dot(k_ref[:, block(m, j)], z)
        v, slope = gelu_and_slope(u)
        v = v.astype(BF16)
        v_ref[...] = v
        s_ref[...] = slope
        for i, j in enumerate((1, 3)):
            send_ref[i] = dot(p_ref[:, block(m, j)], v, ((0,), (0,))).astype(BF16)
        for i, j in enumerate((0, 2)):
            keep_ref[i] = dot(p_ref[:, block(m, j)], v, ((0,), (0,)))

    z_a, v_a, slope_a, keep, send = call(
        first_body,
        [
            ((4, rows, bins), BF16),
            ((hid, bins), BF16),
            ((hid, bins), F32),
            ((2, rows, bins), F32),
            ((2, rows, bins), BF16),
        ],
        (x_own, x_near, x_far, x_cross, tap_a, cols_a, raw_far),
        "first_forward",
    )
    got = swap(send, "mp", 1)

    def near_body(keep_ref, got_ref, *rest):
        rest[-1][...] = (keep_ref[...] + got_ref[...].astype(F32)).astype(BF16)

    def near_sum(keep, got, name, after=()):
        return call(near_body, [((2, rows, bins), BF16)], (keep, got, *after), name)[0]

    chip = near_sum(keep, got, "mix_sum")
    other = swap(chip, "mp", 2)

    def middle_body(x0, x2, chip_ref, other_ref, out_ref):
        for i, ref in enumerate((x0, x2)):
            mixed = chip_ref[i].astype(F32) + other_ref[1 - i].astype(F32)
            out_ref[i] = (ref[...].astype(F32) + mixed).astype(BF16)

    (mid,) = call(
        middle_body, [((2, rows, bins), BF16)], (x_own, x_far, chip, other), "middle"
    )
    mid_near = swap(mid, "mp", 1)

    def second_body(
        a_ref, b_ref, ga_ref, gb_ref, k_ref, p_ref,
        z_ref, v_ref, gu_ref, keep_ref, send_ref, ykeep_ref, ysend_ref,
    ):
        m = lax.axis_index("mp")
        u = jnp.zeros((hid, bins), F32)
        for j in range(4):
            part = (a_ref, b_ref)[j & 1][j >> 1]
            z = gelu(part.astype(F32)).astype(BF16)
            z_ref[j] = z
            u = u + dot(k_ref[:, block(m, j)], z)
        v, slope = gelu_and_slope(u)
        v = v.astype(BF16)
        v_ref[...] = v
        gv = jnp.zeros((hid, bins), F32)
        for j in range(4):
            gv = gv + dot(p_ref[:, block(m, j)], (ga_ref, gb_ref)[j & 1][j >> 1])
        gu = (gv * slope).astype(BF16)
        gu_ref[...] = gu
        for i, j in enumerate((1, 3)):
            send_ref[i] = dot(k_ref[:, block(m, j)], gu, ((0,), (0,))).astype(BF16)
        for i, j in enumerate((0, 2)):
            keep_ref[i] = dot(k_ref[:, block(m, j)], gu, ((0,), (0,)))
        for i, j in enumerate((1, 3)):
            ysend_ref[i] = dot(p_ref[:, block(m, j)], v, ((0,), (0,))).astype(BF16)
        for i, j in enumerate((0, 2)):
            ykeep_ref[i] = dot(p_ref[:, block(m, j)], v, ((0,), (0,)))

    z_b, v_b, gu_b, keep, send, ykeep, ysend = call(
        second_body,
        [
            ((4, rows, bins), BF16),
            ((hid, bins), BF16),
            ((hid, bins), BF16),
            ((2, rows, bins), F32),
            ((2, rows, bins), BF16),
            ((2, rows, bins), F32),
            ((2, rows, bins), BF16),
        ],
        (mid, mid_near, g_pair, g_near, tap_b, cols_b),
        "second_block",
    )
    def weight_body(z_ref, gu_ref, v_ref, *rest):
        grads, (keep_k, keep_p, send_k, send_p, g_ref) = rest[:-5], rest[-5:]
        j = lax.axis_index("mp") ^ lax.axis_index("ctx")
        for i in range(4):
            g_ref[i] = grads[i & 1][i >> 1]

        def taps(k):
            return dot(gu_ref[...], z_ref[j ^ k], ((1,), (1,)))

        def proj(k):
            return dot(v_ref[...], g_ref[j ^ k], ((1,), (1,)))

        for i, k in enumerate((1, 3)):
            send_k[i] = taps(k).astype(BF16)
        for i, k in enumerate((2, 3)):
            send_p[i] = proj(k).astype(BF16)
        for i, k in enumerate((0, 2)):
            keep_k[i] = taps(k)
        for i, k in enumerate((0, 1)):
            keep_p[i] = proj(k)

    two = (2, hid, rows)

    def weights(z, gu, v, grads, name, after=()):
        return call(
            weight_body,
            [(two, F32), (two, F32), (two, BF16), (two, BF16)],
            (z, gu, v, *grads, *after),
            name,
            [pltpu.VMEM((4, rows, bins), BF16)],
        )

    def half_body(keep_k, keep_p, got_k, got_p, own_k, own_p, send_k, send_p):
        own_k[...] = keep_k[0] + got_k[0].astype(F32)
        own_p[...] = keep_p[0] + got_p[0].astype(F32)
        send_k[...] = (keep_k[1] + got_k[1].astype(F32)).astype(BF16)
        send_p[...] = (keep_p[1] + got_p[1].astype(F32)).astype(BF16)

    def first_swap(send_k, send_p):
        return swap(send_k, "ctx", 1), swap(send_p, "ctx", 2)

    def half_sum(keep_k, keep_p, got_k, got_p, name):
        one = (hid, rows)
        return call(
            half_body,
            [(one, F32), (one, F32), (one, BF16), (one, BF16)],
            (keep_k, keep_p, got_k, got_p),
            name,
        )

    def total_body(own_k, own_p, got_k, got_p, taps_ref, proj_ref):
        taps_ref[0] = jnp.zeros((hid, rows), F32)
        taps_ref[1] = own_k[...] + got_k[...].astype(F32)
        taps_ref[2] = jnp.zeros((hid, rows), F32)
        proj_ref[...] = own_p[...] + got_p[...].astype(F32)

    def total(own_k, own_p, got_k, got_p, name):
        taps, proj = call(
            total_body,
            [((3, hid, rows), F32), ((hid, rows), F32)],
            (own_k, own_p, got_k, got_p),
            name,
            final=True,
        )
        return taps, proj.T

    parts_b = weights(z_b, gu_b, v_b, (g_pair, g_near), "second_weights")
    got = swap(send, "mp", 1)
    chip = near_sum(keep, got, "squash_sum", parts_b[:1])
    other = swap(chip, "mp", 2)
    other, *got_b = lax.optimization_barrier((other, *first_swap(*parts_b[2:])))
    parts_b = half_sum(*parts_b[:2], *got_b, "second_half")
    own_b = parts_b[0]
    parts_b = (*parts_b[:2], swap(parts_b[2], "ctx", 2), swap(parts_b[3], "ctx", 1))

    def back_body(g_ref, mid_ref, chip_ref, other_ref, out_ref):
        for i in (0, 1):
            grad = chip_ref[i].astype(F32) + other_ref[1 - i].astype(F32)
            out_ref[i] = (
                g_ref[i].astype(F32) + grad * slope_of(mid_ref[i].astype(F32))
            ).astype(BF16)

    (g_mid,) = call(
        back_body, [((2, rows, bins), BF16)], (g_pair, mid, chip, other), "middle_grad"
    )
    g_mid_near = swap(g_mid, "mp", 1)

    ygot = swap(ysend, "mp", 1)

    def last_sum_body(keep_ref, got_ref, *rest):
        own_ref, send_ref = rest[-2:]
        own_ref[...] = keep_ref[0] + got_ref[0].astype(F32)
        send_ref[...] = (keep_ref[1] + got_ref[1].astype(F32)).astype(BF16)

    def last_sum(keep, got, name, after=()):
        outs = [((rows, bins), F32), ((rows, bins), BF16)]
        return call(last_sum_body, outs, (keep, got, *after), name)

    y_own, y_send = last_sum(ykeep, ygot, "out_sum")
    y_got = swap(y_send, "mp", 2)

    def out_body(mid_ref, own_ref, got_ref, out_ref):
        mixed = own_ref[...] + got_ref[...].astype(F32)
        out_ref[...] = (mid_ref[0].astype(F32) + mixed).astype(BF16)

    (second_out,) = call(out_body, [((rows, bins), BF16)], (mid, y_own, y_got), "out", final=True)

    def first_back_body(a_ref, b_ref, k_ref, p_ref, s_ref, _, gu_ref, keep_ref, send_ref):
        m = lax.axis_index("mp")
        gv = jnp.zeros((hid, bins), F32)
        for j in range(4):
            part = (a_ref, b_ref)[j & 1][j >> 1]
            gv = gv + dot(p_ref[:, block(m, j)], part)
        gu = (gv * s_ref[...]).astype(BF16)
        gu_ref[...] = gu
        for i, j in enumerate((1, 3)):
            send_ref[i] = dot(k_ref[:, block(m, j)], gu, ((0,), (0,))).astype(BF16)
        for i, j in enumerate((0, 2)):
            keep_ref[i] = dot(k_ref[:, block(m, j)], gu, ((0,), (0,)))

    gu_a, keep, send = call(
        first_back_body,
        [((hid, bins), BF16), ((2, rows, bins), F32), ((2, rows, bins), BF16)],
        (g_mid, g_mid_near, tap_a, cols_a, slope_a, own_b),
        "first_backward",
    )
    parts_a = weights(z_a, gu_a, v_a, (g_mid, g_mid_near), "first_weights", parts_b[2:])
    got = swap(send, "mp", 1)
    e_own, e_send = last_sum(keep, got, "entry_sum")
    e_got = swap(e_send, "mp", 2)

    def entry_body(g_ref, x_ref, own_ref, got_ref, out_ref):
        grad = own_ref[...] + got_ref[...].astype(F32)
        out_ref[...] = (
            g_ref[0].astype(F32) + grad * slope_of(x_ref[...].astype(F32))
        ).astype(BF16)

    (entry,) = call(entry_body, [((rows, bins), BF16)], (g_mid, x_own, e_own, e_got), "entry", final=True)

    taps_b_grad, point_b_grad = total(*parts_b, "second_total")
    parts_a = half_sum(*parts_a[:2], *first_swap(*parts_a[2:]), "first_half")
    parts_a = (*parts_a[:2], swap(parts_a[2], "ctx", 2), swap(parts_a[3], "ctx", 1))
    taps_a_grad, point_a_grad = total(*parts_a, "first_total")
    return second_out, entry, taps_a_grad, point_a_grad, taps_b_grad, point_b_grad


def solution(mesh):
    sizes = dict(mesh.shape)

    def shards(x, *rest):
        span = x.shape[1] * sizes["ctx"]
        fast = (
            min(FIRST_DILATION, SECOND_DILATION) >= span
            and sizes["mp"] == 4
            and sizes["ctx"] == 4
        )
        return (fast_shards if fast else general_shards)(x, *rest)

    return jax.shard_map(
        shards,
        mesh=mesh,
        in_specs=(
            P("mp", ("groups", "ctx")),
            P(None, "mp", None),
            P(None, "mp"),
            P(None, "mp", None),
            P(None, "mp"),
            P("mp", "ctx", "groups"),
        ),
        out_specs=(
            P("mp", ("groups", "ctx")),
            P("mp", ("groups", "ctx")),
            P("groups", "mp", "ctx"),
            P(("groups", "ctx"), "mp"),
            P("groups", "mp", "ctx"),
            P(("groups", "ctx"), "mp"),
        ),
        check_vma=False,
    )
```

```python
import functools

import jax
import jax.numpy as jnp
from jax import lax
from jax.experimental import pallas as pl
from jax.experimental.pallas import tpu as pltpu
from jax.sharding import PartitionSpec as P

FIRST_DILATION = 1024
SECOND_DILATION = 2048
F32 = jnp.float32
BF16 = jnp.bfloat16
ROOT = 0.7978845608028654
CUBIC = 0.044715


def shifted(value, axis, by):
    length = lax.axis_size(axis)
    pairs = [(i, i + by) for i in range(length) if 0 <= i + by < length]
    return lax.ppermute(value, axis, pairs)


def gelu_slope(values):
    return jax.jvp(jax.nn.gelu, (values,), (jnp.ones_like(values),))[1]


def contract_first(left, right):
    return lax.dot_general(
        left, right, (((0,), (0,)), ((), ())), preferred_element_type=jnp.float32
    )


def contract_last(left, right):
    return lax.dot_general(
        left, right, (((1,), (1,)), ((), ())), preferred_element_type=jnp.float32
    )


def hop_steps(activations, dilation):
    return dilation // activations.shape[1]


def residual_block_forward(activations, conv_weight, point_weight, dilation):
    hop_count = hop_steps(activations, dilation)
    squash_part = jax.nn.gelu(activations.astype(jnp.float32)).astype(jnp.bfloat16)
    squashed = lax.all_gather(squash_part, "mp", axis=0, tiled=True)
    earlier = shifted(squashed, "ctx", hop_count)
    later = shifted(squashed, "ctx", -hop_count)
    pre_act = jnp.dot(conv_weight[0], earlier, preferred_element_type=jnp.float32)
    pre_act = pre_act + jnp.dot(conv_weight[1], squashed, preferred_element_type=jnp.float32)
    pre_act = pre_act + jnp.dot(conv_weight[2], later, preferred_element_type=jnp.float32)
    hidden = jax.nn.gelu(pre_act).astype(jnp.bfloat16)
    mixed = lax.psum_scatter(
        jnp.dot(point_weight, hidden, preferred_element_type=jnp.float32).astype(jnp.bfloat16),
        "mp",
        scatter_dimension=0,
        tiled=True,
    ).astype(jnp.float32)
    result = (activations.astype(jnp.float32) + mixed).astype(jnp.bfloat16)
    return (result, squashed, pre_act, hidden)


def residual_block_backward(
    incoming_gradient, activations, squashed, pre_act, hidden, conv_weight, point_weight, dilation
):
    hop_count = hop_steps(activations, dilation)
    upstream_full = lax.all_gather(incoming_gradient, "mp", axis=0, tiled=True)
    grad_hidden = contract_first(point_weight, upstream_full)
    grad_pre = (grad_hidden * gelu_slope(pre_act)).astype(jnp.bfloat16)
    grad_later = shifted(grad_pre, "ctx", -hop_count)
    grad_earlier = shifted(grad_pre, "ctx", hop_count)
    moved = (grad_later, grad_pre, grad_earlier)
    grad_conv = jnp.stack([contract_last(part, squashed) for part in moved])
    grad_point = contract_last(upstream_full, hidden)
    total = contract_first(conv_weight[0], moved[0])
    total = total + contract_first(conv_weight[1], moved[1])
    grad_squash = lax.psum_scatter(
        (total + contract_first(conv_weight[2], moved[2])).astype(jnp.bfloat16),
        "mp",
        scatter_dimension=0,
        tiled=True,
    ).astype(jnp.float32)
    previous = (
        incoming_gradient.astype(jnp.float32)
        + grad_squash * gelu_slope(activations.astype(jnp.float32))
    ).astype(jnp.bfloat16)
    return (previous, grad_conv, grad_point)


def reduce_block(grad_conv, grad_point):
    return (
        lax.psum_scatter(
            grad_conv.astype(jnp.bfloat16), "ctx", scatter_dimension=2, tiled=True
        ).astype(jnp.float32),
        lax.psum_scatter(
            grad_point.astype(jnp.bfloat16), "ctx", scatter_dimension=0, tiled=True
        ).astype(jnp.float32),
    )


def general_shards(x, taps_a, point_a, taps_b, point_b, grad_heads):
    regrouped = lax.all_to_all(grad_heads, "ctx", split_axis=2, concat_axis=1, tiled=True)
    gradient = regrouped.reshape(regrouped.shape[0] * regrouped.shape[1], regrouped.shape[2])
    middle, z_a, u_a, v_a = residual_block_forward(x, taps_a, point_a, FIRST_DILATION)
    result, z_b, u_b, v_b = residual_block_forward(middle, taps_b, point_b, SECOND_DILATION)
    gradient, conv_b, proj_b = residual_block_backward(
        gradient, middle, z_b, u_b, v_b, taps_b, point_b, SECOND_DILATION
    )
    conv_b, proj_b = reduce_block(conv_b, proj_b)
    gradient, conv_a, proj_a = residual_block_backward(
        gradient, x, z_a, u_a, v_a, taps_a, point_a, FIRST_DILATION
    )
    conv_a, proj_a = reduce_block(conv_a, proj_a)
    return result, gradient, conv_a, proj_a, conv_b, proj_b


def swap(value, axis, bits):
    size = lax.axis_size(axis)
    return lax.ppermute(value, axis, [(i, i ^ bits) for i in range(size)])


def dot(left, right, dims=((1,), (0,))):
    return lax.dot_general(left, right, (dims, ((), ())), preferred_element_type=F32)


def gelu(s):
    return 0.5 * s * (1.0 + jnp.tanh(ROOT * (s + CUBIC * (s * s * s))))


def gelu_and_slope(s):
    sq = s * s
    t = jnp.tanh(ROOT * (s + CUBIC * (s * sq)))
    half = 0.5 * (1.0 + t)
    slope = half + 0.5 * s * (1.0 - t * t) * (ROOT * (1.0 + 3.0 * CUBIC * sq))
    return s * half, slope


def slope_of(s):
    return gelu_and_slope(s)[1]


VMEM = pl.BlockSpec(memory_space=pltpu.VMEM)


def call(body, outs, args, name, scratch=(), final=False):
    struct = jax.ShapeDtypeStruct if final else pltpu.VMEM
    return pl.pallas_call(
        body,
        out_shape=[struct(s, d) for s, d in outs],
        in_specs=[VMEM] * len(args),
        out_specs=[VMEM] * len(outs),
        scratch_shapes=scratch,
        compiler_params=pltpu.CompilerParams(vmem_limit_bytes=16 << 20),
        name=name,
    )(*[pltpu.with_memory_space_constraint(a, pltpu.VMEM) for a in args])


def fast_shards(x, taps_a, point_a, taps_b, point_b, grad_heads):
    rows, bins = x.shape
    hid, chans = taps_a.shape[1], taps_a.shape[2]
    heads, val, _ = grad_heads.shape
    def block(m, j):
        return pl.ds(pl.multiple_of((m ^ j) * rows, rows), rows)

    x_far = swap(x, "mp", 2)
    x_near = swap(x, "mp", 1)

    raw_far = swap(grad_heads, "mp", 2)

    def load_body(x_ref, ta, tb, ca, cb, g_ref, *rest):
        outs, sems = rest[:-1], rest[-1]
        sources = [x_ref, ta.at[1], tb.at[1], ca, cb, g_ref]
        copies = [
            pltpu.make_async_copy(source, out, sems.at[i])
            for i, (source, out) in enumerate(zip(sources, outs))
        ]
        for copy in copies:
            copy.start()
        for copy in copies:
            copy.wait()

    x_own, tap_a, tap_b, cols_a, cols_b, raw_own = pl.pallas_call(
        load_body,
        out_shape=[pltpu.VMEM((rows, bins), BF16)]
        + [pltpu.VMEM((hid, chans), BF16)] * 4
        + [pltpu.VMEM(grad_heads.shape, BF16)],
        in_specs=[pl.BlockSpec(memory_space=pltpu.HBM)] * 6,
        out_specs=[VMEM] * 6,
        scratch_shapes=[pltpu.SemaphoreType.DMA((6,))],
        compiler_params=pltpu.CompilerParams(vmem_limit_bytes=16 << 20),
        name="load",
    )(
        *[
            pltpu.with_memory_space_constraint(source, pltpu.HBM)
            for source in (x, taps_a, taps_b, point_a.T, point_b.T, grad_heads)
        ]
    )
    x_far, x_own = lax.optimization_barrier((x_far, x_own))
    x_cross = swap(x_far, "mp", 1)

    def split_body(own_ref, far_ref, *outs):
        c = lax.axis_index("ctx")
        for k in range(4):
            at = pl.ds(pl.multiple_of((c ^ k) * bins, bins), bins)
            for i, ref in enumerate((own_ref, far_ref)):
                outs[k][i] = ref[:, :, at]

    piece = ((2, heads, val, bins), BF16)
    pieces = call(split_body, [piece] * 4, (raw_own, raw_far), "split_grad")
    pieces = [pieces[0]] + [swap(pieces[k], "ctx", k) for k in (1, 2, 3)]

    def join_body(*refs):
        c = lax.axis_index("ctx")
        out = refs[4]
        for k in range(4):
            out[:, :, c ^ k] = refs[k][...]

    (g_pair,) = call(join_body, [((2, heads, 4, val, bins), BF16)], pieces, "join_grad")
    g_pair = g_pair.reshape(2, rows, bins)
    g_near = swap(g_pair, "mp", 1)

    def first_body(x0, x1, x2, x3, k_ref, p_ref, _, z_ref, v_ref, s_ref, keep_ref, send_ref):
        m = lax.axis_index("mp")
        u = jnp.zeros((hid, bins), F32)
        for j, ref in enumerate((x0, x1, x2, x3)):
            z = gelu(ref[...].astype(F32)).astype(BF16)
            z_ref[j] = z
            u = u + dot(k_ref[:, block(m, j)], z)
        v, slope = gelu_and_slope(u)
        v = v.astype(BF16)
        v_ref[...] = v
        s_ref[...] = slope
        for i, j in enumerate((1, 3)):
            send_ref[i] = dot(p_ref[:, block(m, j)], v, ((0,), (0,))).astype(BF16)
        for i, j in enumerate((0, 2)):
            keep_ref[i] = dot(p_ref[:, block(m, j)], v, ((0,), (0,)))

    z_a, v_a, slope_a, keep, send = call(
        first_body,
        [
            ((4, rows, bins), BF16),
            ((hid, bins), BF16),
            ((hid, bins), F32),
            ((2, rows, bins), F32),
            ((2, rows, bins), BF16),
        ],
        (x_own, x_near, x_far, x_cross, tap_a, cols_a, raw_far),
        "first_forward",
    )
    got = swap(send, "mp", 1)

    def near_body(keep_ref, got_ref, *rest):
        rest[-1][...] = (keep_ref[...] + got_ref[...].astype(F32)).astype(BF16)

    def near_sum(keep, got, name, after=()):
        return call(near_body, [((2, rows, bins), BF16)], (keep, got, *after), name)[0]

    chip = near_sum(keep, got, "mix_sum")
    other = swap(chip, "mp", 2)

    def middle_body(x0, x2, chip_ref, other_ref, out_ref):
        for i, ref in enumerate((x0, x2)):
            mixed = chip_ref[i].astype(F32) + other_ref[1 - i].astype(F32)
            out_ref[i] = (ref[...].astype(F32) + mixed).astype(BF16)

    (mid,) = call(
        middle_body, [((2, rows, bins), BF16)], (x_own, x_far, chip, other), "middle"
    )
    mid_near = swap(mid, "mp", 1)

    def second_body(
        a_ref, b_ref, ga_ref, gb_ref, k_ref, p_ref,
        z_ref, v_ref, gu_ref, keep_ref, send_ref, ykeep_ref, ysend_ref,
    ):
        m = lax.axis_index("mp")
        u = jnp.zeros((hid, bins), F32)
        for j in range(4):
            part = (a_ref, b_ref)[j & 1][j >> 1]
            z = gelu(part.astype(F32)).astype(BF16)
            z_ref[j] = z
            u = u + dot(k_ref[:, block(m, j)], z)
        v, slope = gelu_and_slope(u)
        v = v.astype(BF16)
        v_ref[...] = v
        gv = jnp.zeros((hid, bins), F32)
        for j in range(4):
            gv = gv + dot(p_ref[:, block(m, j)], (ga_ref, gb_ref)[j & 1][j >> 1])
        gu = (gv * slope).astype(BF16)
        gu_ref[...] = gu
        for i, j in enumerate((1, 3)):
            send_ref[i] = dot(k_ref[:, block(m, j)], gu, ((0,), (0,))).astype(BF16)
        for i, j in enumerate((0, 2)):
            keep_ref[i] = dot(k_ref[:, block(m, j)], gu, ((0,), (0,)))
        for i, j in enumerate((1, 3)):
            ysend_ref[i] = dot(p_ref[:, block(m, j)], v, ((0,), (0,))).astype(BF16)
        for i, j in enumerate((0, 2)):
            ykeep_ref[i] = dot(p_ref[:, block(m, j)], v, ((0,), (0,)))

    z_b, v_b, gu_b, keep, send, ykeep, ysend = call(
        second_body,
        [
            ((4, rows, bins), BF16),
            ((hid, bins), BF16),
            ((hid, bins), BF16),
            ((2, rows, bins), F32),
            ((2, rows, bins), BF16),
            ((2, rows, bins), F32),
            ((2, rows, bins), BF16),
        ],
        (mid, mid_near, g_pair, g_near, tap_b, cols_b),
        "second_block",
    )
    def weight_pieces(z_ref, gu_ref, v_ref, g_ref, keep_k, keep_p, send_k, send_p):
        j = lax.axis_index("mp") ^ lax.axis_index("ctx")

        def taps(k):
            return dot(gu_ref[...], z_ref[j ^ k], ((1,), (1,)))

        def proj(k):
            return dot(v_ref[...], g_ref[j ^ k], ((1,), (1,)))

        for i, k in enumerate((1, 3)):
            send_k[i] = taps(k).astype(BF16)
        for i, k in enumerate((2, 3)):
            send_p[i] = proj(k).astype(BF16)
        for i, k in enumerate((0, 2)):
            keep_k[i] = taps(k)
        for i, k in enumerate((0, 1)):
            keep_p[i] = proj(k)

    one, two, three = ((n, hid, rows) for n in (1, 2, 3))

    def second_weight_body(z_ref, gu_ref, v_ref, ga_ref, gb_ref, *rest):
        g_ref = rest[4]
        for i in range(4):
            g_ref[i] = (ga_ref, gb_ref)[i & 1][i >> 1]
        weight_pieces(z_ref, gu_ref, v_ref, g_ref, *rest[:4])

    def half_sum(keep, got, own):
        own[0] = keep[0] + got[0].astype(F32)
        return (keep[1] + got[1].astype(F32)).astype(BF16)

    def first_weight_body(z_ref, gu_ref, v_ref, g0, g1, g2, g3, *rest):
        keep_k, keep_p, got_k, got_p = rest[:4]
        own_k, own_p = rest[8:10]
        g_ref = rest[10]
        for i, ref in enumerate((g0, g1, g2, g3)):
            g_ref[i] = ref[...]
        send_k, send_p = rest[6:8]
        send_p[2] = half_sum(keep_k, got_k, own_k)
        send_k[2] = half_sum(keep_p, got_p, own_p)
        weight_pieces(z_ref, gu_ref, v_ref, g_ref, *rest[4:8])

    def half_body(keep_k, keep_p, got_k, got_p, own_k, own_p, send_k, send_p):
        send_k[...] = half_sum(keep_k, got_k, own_k)
        send_p[...] = half_sum(keep_p, got_p, own_p)

    def total_body(place_k, place_p, own_k, own_p, got_k, got_p, taps_ref, proj_ref):
        taps_ref[0] = jnp.zeros((hid, rows), F32)
        taps_ref[1] = own_k[0] + got_k[place_k].astype(F32)
        taps_ref[2] = jnp.zeros((hid, rows), F32)
        proj_ref[...] = own_p[0] + got_p[place_p].astype(F32)

    def total(place, own_k, own_p, got_k, got_p, name):
        taps, proj = call(
            functools.partial(total_body, place, place),
            [((3, hid, rows), F32), ((hid, rows), F32)],
            (own_k, own_p, got_k, got_p),
            name,
            final=True,
        )
        return taps, proj.T

    pack = [pltpu.VMEM((4, rows, bins), BF16)]
    *keep_b, send_k, send_p = call(
        second_weight_body,
        [(two, F32), (two, F32), (two, BF16), (two, BF16)],
        (z_b, gu_b, v_b, g_pair, g_near),
        "second_weights",
        pack,
    )
    got = swap(send, "mp", 1)
    chip = near_sum(keep, got, "squash_sum", keep_b[:1])
    other = swap(chip, "mp", 2)
    got_b = swap(send_k, "ctx", 1), swap(send_p, "ctx", 2)

    def back_body(g_ref, mid_ref, chip_ref, other_ref, *outs):
        for i in (0, 1):
            grad = chip_ref[i].astype(F32) + other_ref[1 - i].astype(F32)
            outs[i][...] = (
                g_ref[i].astype(F32) + grad * slope_of(mid_ref[i].astype(F32))
            ).astype(BF16)

    g_mid = call(
        back_body, [((rows, bins), BF16)] * 2, (g_pair, mid, chip, other), "middle_grad"
    )
    g_mid = [g_mid[0], swap(g_mid[0], "mp", 1), g_mid[1], swap(g_mid[1], "mp", 1)]

    ygot = swap(ysend, "mp", 1)

    def last_sum_body(keep_ref, got_ref, *rest):
        own_ref, send_ref = rest[-2:]
        own_ref[...] = keep_ref[0] + got_ref[0].astype(F32)
        send_ref[...] = (keep_ref[1] + got_ref[1].astype(F32)).astype(BF16)

    def last_sum(keep, got, name, after=()):
        outs = [((rows, bins), F32), ((rows, bins), BF16)]
        return call(last_sum_body, outs, (keep, got, *after), name)

    y_own, y_send = last_sum(ykeep, ygot, "out_sum")
    y_got = swap(y_send, "mp", 2)

    def out_body(mid_ref, own_ref, got_ref, out_ref):
        mixed = own_ref[...] + got_ref[...].astype(F32)
        out_ref[...] = (mid_ref[0].astype(F32) + mixed).astype(BF16)

    (second_out,) = call(out_body, [((rows, bins), BF16)], (mid, y_own, y_got), "out", final=True)

    def first_back_body(*refs):
        grads, (k_ref, p_ref, s_ref, gu_ref, keep_ref, send_ref) = refs[:4], refs[4:]
        m = lax.axis_index("mp")
        gv = jnp.zeros((hid, bins), F32)
        for j in range(4):
            gv = gv + dot(p_ref[:, block(m, j)], grads[j][...])
        gu = (gv * s_ref[...]).astype(BF16)
        gu_ref[...] = gu
        for i, j in enumerate((1, 3)):
            send_ref[i] = dot(k_ref[:, block(m, j)], gu, ((0,), (0,))).astype(BF16)
        for i, j in enumerate((0, 2)):
            keep_ref[i] = dot(k_ref[:, block(m, j)], gu, ((0,), (0,)))

    gu_a, keep, send = call(
        first_back_body,
        [((hid, bins), BF16), ((2, rows, bins), F32), ((2, rows, bins), BF16)],
        (*g_mid, tap_a, cols_a, slope_a),
        "first_backward",
    )
    *keep_a, send_k, send_p, own_bk, own_bp = call(
        first_weight_body,
        [(two, F32), (two, F32), (three, BF16), (three, BF16), (one, F32), (one, F32)],
        (z_a, gu_a, v_a, *g_mid, *keep_b, *got_b),
        "first_weights",
        pack,
    )
    got_k, got_p = swap(send_k, "ctx", 1), swap(send_p, "ctx", 2)
    got = swap(send, "mp", 1)
    e_own, e_send = last_sum(keep, got, "entry_sum")
    e_got = swap(e_send, "mp", 2)

    def entry_body(g_ref, x_ref, own_ref, got_ref, out_ref):
        grad = own_ref[...] + got_ref[...].astype(F32)
        out_ref[...] = (
            g_ref[...].astype(F32) + grad * slope_of(x_ref[...].astype(F32))
        ).astype(BF16)

    (entry,) = call(entry_body, [((rows, bins), BF16)], (g_mid[0], x_own, e_own, e_got), "entry", final=True)

    own_ak, own_ap, send_k, send_p = call(
        half_body,
        [(one, F32), (one, F32), (one[1:], BF16), (one[1:], BF16)],
        (*keep_a, got_k, got_p),
        "first_half",
    )
    last_k, last_p = swap(send_k, "ctx", 2), swap(send_p, "ctx", 1)
    taps_b_grad, point_b_grad = total(2, own_bk, own_bp, got_p, got_k, "second_total")
    taps_a_grad, point_a_grad = total(Ellipsis, own_ak, own_ap, last_k, last_p, "first_total")
    return second_out, entry, taps_a_grad, point_a_grad, taps_b_grad, point_b_grad


def solution(mesh):
    sizes = dict(mesh.shape)

    def shards(x, *rest):
        span = x.shape[1] * sizes["ctx"]
        fast = (
            min(FIRST_DILATION, SECOND_DILATION) >= span
            and sizes["mp"] == 4
            and sizes["ctx"] == 4
        )
        return (fast_shards if fast else general_shards)(x, *rest)

    return jax.shard_map(
        shards,
        mesh=mesh,
        in_specs=(
            P("mp", ("groups", "ctx")),
            P(None, "mp", None),
            P(None, "mp"),
            P(None, "mp", None),
            P(None, "mp"),
            P("mp", "ctx", "groups"),
        ),
        out_specs=(
            P("mp", ("groups", "ctx")),
            P("mp", ("groups", "ctx")),
            P("groups", "mp", "ctx"),
            P(("groups", "ctx"), "mp"),
            P("groups", "mp", "ctx"),
            P(("groups", "ctx"), "mp"),
        ),
        check_vma=False,
    )
```

```python
import functools

import jax
import jax.numpy as jnp
from jax import lax
from jax.experimental import pallas as pl
from jax.experimental.pallas import tpu as pltpu
from jax.sharding import PartitionSpec as P

FIRST_DILATION = 1024
SECOND_DILATION = 2048
F32 = jnp.float32
BF16 = jnp.bfloat16
ROOT = 0.7978845608028654
CUBIC = 0.044715


def shifted(value, axis, by):
    length = lax.axis_size(axis)
    pairs = [(i, i + by) for i in range(length) if 0 <= i + by < length]
    return lax.ppermute(value, axis, pairs)


def gelu_slope(values):
    return jax.jvp(jax.nn.gelu, (values,), (jnp.ones_like(values),))[1]


def contract_first(left, right):
    return lax.dot_general(
        left, right, (((0,), (0,)), ((), ())), preferred_element_type=jnp.float32
    )


def contract_last(left, right):
    return lax.dot_general(
        left, right, (((1,), (1,)), ((), ())), preferred_element_type=jnp.float32
    )


def hop_steps(activations, dilation):
    return dilation // activations.shape[1]


def residual_block_forward(activations, conv_weight, point_weight, dilation):
    hop_count = hop_steps(activations, dilation)
    squash_part = jax.nn.gelu(activations.astype(jnp.float32)).astype(jnp.bfloat16)
    squashed = lax.all_gather(squash_part, "mp", axis=0, tiled=True)
    earlier = shifted(squashed, "ctx", hop_count)
    later = shifted(squashed, "ctx", -hop_count)
    pre_act = jnp.dot(conv_weight[0], earlier, preferred_element_type=jnp.float32)
    pre_act = pre_act + jnp.dot(conv_weight[1], squashed, preferred_element_type=jnp.float32)
    pre_act = pre_act + jnp.dot(conv_weight[2], later, preferred_element_type=jnp.float32)
    hidden = jax.nn.gelu(pre_act).astype(jnp.bfloat16)
    mixed = lax.psum_scatter(
        jnp.dot(point_weight, hidden, preferred_element_type=jnp.float32).astype(jnp.bfloat16),
        "mp",
        scatter_dimension=0,
        tiled=True,
    ).astype(jnp.float32)
    result = (activations.astype(jnp.float32) + mixed).astype(jnp.bfloat16)
    return (result, squashed, pre_act, hidden)


def residual_block_backward(
    incoming_gradient, activations, squashed, pre_act, hidden, conv_weight, point_weight, dilation
):
    hop_count = hop_steps(activations, dilation)
    upstream_full = lax.all_gather(incoming_gradient, "mp", axis=0, tiled=True)
    grad_hidden = contract_first(point_weight, upstream_full)
    grad_pre = (grad_hidden * gelu_slope(pre_act)).astype(jnp.bfloat16)
    grad_later = shifted(grad_pre, "ctx", -hop_count)
    grad_earlier = shifted(grad_pre, "ctx", hop_count)
    moved = (grad_later, grad_pre, grad_earlier)
    grad_conv = jnp.stack([contract_last(part, squashed) for part in moved])
    grad_point = contract_last(upstream_full, hidden)
    total = contract_first(conv_weight[0], moved[0])
    total = total + contract_first(conv_weight[1], moved[1])
    grad_squash = lax.psum_scatter(
        (total + contract_first(conv_weight[2], moved[2])).astype(jnp.bfloat16),
        "mp",
        scatter_dimension=0,
        tiled=True,
    ).astype(jnp.float32)
    previous = (
        incoming_gradient.astype(jnp.float32)
        + grad_squash * gelu_slope(activations.astype(jnp.float32))
    ).astype(jnp.bfloat16)
    return (previous, grad_conv, grad_point)


def reduce_block(grad_conv, grad_point):
    return (
        lax.psum_scatter(
            grad_conv.astype(jnp.bfloat16), "ctx", scatter_dimension=2, tiled=True
        ).astype(jnp.float32),
        lax.psum_scatter(
            grad_point.astype(jnp.bfloat16), "ctx", scatter_dimension=0, tiled=True
        ).astype(jnp.float32),
    )


def general_shards(x, taps_a, point_a, taps_b, point_b, grad_heads):
    regrouped = lax.all_to_all(grad_heads, "ctx", split_axis=2, concat_axis=1, tiled=True)
    gradient = regrouped.reshape(regrouped.shape[0] * regrouped.shape[1], regrouped.shape[2])
    middle, z_a, u_a, v_a = residual_block_forward(x, taps_a, point_a, FIRST_DILATION)
    result, z_b, u_b, v_b = residual_block_forward(middle, taps_b, point_b, SECOND_DILATION)
    gradient, conv_b, proj_b = residual_block_backward(
        gradient, middle, z_b, u_b, v_b, taps_b, point_b, SECOND_DILATION
    )
    conv_b, proj_b = reduce_block(conv_b, proj_b)
    gradient, conv_a, proj_a = residual_block_backward(
        gradient, x, z_a, u_a, v_a, taps_a, point_a, FIRST_DILATION
    )
    conv_a, proj_a = reduce_block(conv_a, proj_a)
    return result, gradient, conv_a, proj_a, conv_b, proj_b


def swap(value, axis, bits):
    size = lax.axis_size(axis)
    return lax.ppermute(value, axis, [(i, i ^ bits) for i in range(size)])


def dot(left, right, dims=((1,), (0,))):
    return lax.dot_general(left, right, (dims, ((), ())), preferred_element_type=F32)


def gelu(s):
    return 0.5 * s * (1.0 + jnp.tanh(ROOT * (s + CUBIC * (s * s * s))))


def gelu_and_slope(s):
    sq = s * s
    t = jnp.tanh(ROOT * (s + CUBIC * (s * sq)))
    half = 0.5 * (1.0 + t)
    slope = half + 0.5 * s * (1.0 - t * t) * (ROOT * (1.0 + 3.0 * CUBIC * sq))
    return s * half, slope


def slope_of(s):
    return gelu_and_slope(s)[1]


VMEM = pl.BlockSpec(memory_space=pltpu.VMEM)


def call(body, outs, args, name, scratch=(), final=False):
    struct = jax.ShapeDtypeStruct if final else pltpu.VMEM
    return pl.pallas_call(
        body,
        out_shape=[struct(s, d) for s, d in outs],
        in_specs=[VMEM] * len(args),
        out_specs=[VMEM] * len(outs),
        scratch_shapes=scratch,
        compiler_params=pltpu.CompilerParams(vmem_limit_bytes=16 << 20),
        name=name,
    )(*[pltpu.with_memory_space_constraint(a, pltpu.VMEM) for a in args])


def fast_shards(x, taps_a, point_a, taps_b, point_b, grad_heads):
    rows, bins = x.shape
    hid, chans = taps_a.shape[1], taps_a.shape[2]
    heads, val, _ = grad_heads.shape
    def block(m, j):
        return pl.ds(pl.multiple_of((m ^ j) * rows, rows), rows)

    x_far = swap(x, "mp", 2)
    x_near = swap(x, "mp", 1)

    raw_far = swap(grad_heads, "mp", 2)

    def load_body(x_ref, ta, tb, ca, cb, g_ref, *rest):
        outs, sems = rest[:-1], rest[-1]
        sources = [x_ref, ta.at[1], tb.at[1], ca, cb, g_ref]
        copies = [
            pltpu.make_async_copy(source, out, sems.at[i])
            for i, (source, out) in enumerate(zip(sources, outs))
        ]
        for copy in copies:
            copy.start()
        for copy in copies:
            copy.wait()

    x_own, tap_a, tap_b, cols_a, cols_b, raw_own = pl.pallas_call(
        load_body,
        out_shape=[pltpu.VMEM((rows, bins), BF16)]
        + [pltpu.VMEM((hid, chans), BF16)] * 4
        + [pltpu.VMEM(grad_heads.shape, BF16)],
        in_specs=[pl.BlockSpec(memory_space=pltpu.HBM)] * 6,
        out_specs=[VMEM] * 6,
        scratch_shapes=[pltpu.SemaphoreType.DMA((6,))],
        compiler_params=pltpu.CompilerParams(vmem_limit_bytes=16 << 20),
        name="load",
    )(
        *[
            pltpu.with_memory_space_constraint(source, pltpu.HBM)
            for source in (x, taps_a, taps_b, point_a.T, point_b.T, grad_heads)
        ]
    )
    x_far, x_own = lax.optimization_barrier((x_far, x_own))
    x_cross = swap(x_far, "mp", 1)

    def split_body(own_ref, far_ref, *outs):
        c = lax.axis_index("ctx")
        for k in range(4):
            at = pl.ds(pl.multiple_of((c ^ k) * bins, bins), bins)
            for i, ref in enumerate((own_ref, far_ref)):
                outs[k][i] = ref[:, :, at]

    piece = ((2, heads, val, bins), BF16)
    pieces = call(split_body, [piece] * 4, (raw_own, raw_far), "split_grad")
    pieces = [pieces[0]] + [swap(pieces[k], "ctx", k) for k in (1, 2, 3)]

    def join_body(*refs):
        c = lax.axis_index("ctx")
        out = refs[4]
        for k in range(4):
            out[:, :, c ^ k] = refs[k][...]

    (g_pair,) = call(join_body, [((2, heads, 4, val, bins), BF16)], pieces, "join_grad")
    g_pair = g_pair.reshape(2, rows, bins)
    g_near = swap(g_pair, "mp", 1)

    def first_body(x0, x1, x2, x3, k_ref, p_ref, _, z_ref, v_ref, s_ref, keep_ref, send_ref):
        m = lax.axis_index("mp")
        u = jnp.zeros((hid, bins), F32)
        for j, ref in enumerate((x0, x1, x2, x3)):
            z = gelu(ref[...].astype(F32)).astype(BF16)
            z_ref[j] = z
            u = u + dot(k_ref[:, block(m, j)], z)
        v, slope = gelu_and_slope(u)
        v = v.astype(BF16)
        v_ref[...] = v
        s_ref[...] = slope
        for i, j in enumerate((1, 3)):
            send_ref[i] = dot(p_ref[:, block(m, j)], v, ((0,), (0,))).astype(BF16)
        for i, j in enumerate((0, 2)):
            keep_ref[i] = dot(p_ref[:, block(m, j)], v, ((0,), (0,)))

    z_a, v_a, slope_a, keep, send = call(
        first_body,
        [
            ((4, rows, bins), BF16),
            ((hid, bins), BF16),
            ((hid, bins), F32),
            ((2, rows, bins), F32),
            ((2, rows, bins), BF16),
        ],
        (x_own, x_near, x_far, x_cross, tap_a, cols_a, raw_far),
        "first_forward",
    )
    got = swap(send, "mp", 1)

    def mix_body(keep_ref, got_ref, out_ref):
        out_ref[...] = (keep_ref[...] + got_ref[...].astype(F32)).astype(BF16)

    (chip,) = call(mix_body, [((2, rows, bins), BF16)], (keep, got), "mix_sum")
    other = swap(chip, "mp", 2)

    def middle_body(x0, x2, chip_ref, other_ref, out_ref):
        for i, ref in enumerate((x0, x2)):
            mixed = chip_ref[i].astype(F32) + other_ref[1 - i].astype(F32)
            out_ref[i] = (ref[...].astype(F32) + mixed).astype(BF16)

    (mid,) = call(
        middle_body, [((2, rows, bins), BF16)], (x_own, x_far, chip, other), "middle"
    )
    mid_near = swap(mid, "mp", 1)

    def second_body(
        a_ref, b_ref, ga_ref, gb_ref, k_ref, p_ref,
        z_ref, v_ref, gu_ref, keep_ref, send_ref, ykeep_ref, ysend_ref,
    ):
        m = lax.axis_index("mp")
        u = jnp.zeros((hid, bins), F32)
        for j in range(4):
            part = (a_ref, b_ref)[j & 1][j >> 1]
            z = gelu(part.astype(F32)).astype(BF16)
            z_ref[j] = z
            u = u + dot(k_ref[:, block(m, j)], z)
        v, slope = gelu_and_slope(u)
        v = v.astype(BF16)
        v_ref[...] = v
        gv = jnp.zeros((hid, bins), F32)
        for j in range(4):
            gv = gv + dot(p_ref[:, block(m, j)], (ga_ref, gb_ref)[j & 1][j >> 1])
        gu = (gv * slope).astype(BF16)
        gu_ref[...] = gu
        for i, j in enumerate((1, 3)):
            send_ref[i] = dot(k_ref[:, block(m, j)], gu, ((0,), (0,))).astype(BF16)
        for i, j in enumerate((0, 2)):
            keep_ref[i] = dot(k_ref[:, block(m, j)], gu, ((0,), (0,)))
        for i, j in enumerate((1, 3)):
            ysend_ref[i] = dot(p_ref[:, block(m, j)], v, ((0,), (0,))).astype(BF16)
        for i, j in enumerate((0, 2)):
            ykeep_ref[i] = dot(p_ref[:, block(m, j)], v, ((0,), (0,)))

    z_b, v_b, gu_b, keep, send, ykeep, ysend = call(
        second_body,
        [
            ((4, rows, bins), BF16),
            ((hid, bins), BF16),
            ((hid, bins), BF16),
            ((2, rows, bins), F32),
            ((2, rows, bins), BF16),
            ((2, rows, bins), F32),
            ((2, rows, bins), BF16),
        ],
        (mid, mid_near, g_pair, g_near, tap_b, cols_b),
        "second_block",
    )
    def place(k):
        return lax.axis_index("mp") ^ lax.axis_index("ctx") ^ k

    def taps_pieces(z_ref, gu_ref, keep, send):
        for i in (0, 1):
            send[i] = dot(gu_ref[...], z_ref[place(1 + 2 * i)], ((1,), (1,))).astype(BF16)
        for i in (0, 1):
            keep[i] = dot(gu_ref[...], z_ref[place(2 * i)], ((1,), (1,)))

    def proj_pieces(v_ref, g_ref, keep, send):
        for i in (0, 1):
            send[i] = dot(v_ref[...], g_ref[place(2 + i)], ((1,), (1,))).astype(BF16)
        for i in (0, 1):
            keep[i] = dot(v_ref[...], g_ref[place(i)], ((1,), (1,)))

    one, two, three = ((n, hid, rows) for n in (1, 2, 3))

    def second_weight_body(z_ref, gu_ref, v_ref, ga_ref, gb_ref, *rest):
        keep_k, keep_p, send_k, send_p, g_ref = rest
        for i in range(4):
            g_ref[i] = (ga_ref, gb_ref)[i & 1][i >> 1]
        proj_pieces(v_ref, g_ref, keep_p, send_p)
        taps_pieces(z_ref, gu_ref, keep_k, send_k)

    def half_sum(keep, got, own):
        own[0] = keep[0] + got[0].astype(F32)
        return (keep[1] + got[1].astype(F32)).astype(BF16)

    def first_proj_body(v_ref, g0, g1, g2, g3, keep_b, got_b, keep, send, own, g_ref):
        for i, ref in enumerate((g0, g1, g2, g3)):
            g_ref[i] = ref[...]
        send[2] = half_sum(keep_b, got_b, own)
        proj_pieces(v_ref, g_ref, keep, send)

    def first_taps_body(z_ref, gu_ref, keep_b, got_b, _, keep, send, own):
        send[2] = half_sum(keep_b, got_b, own)
        taps_pieces(z_ref, gu_ref, keep, send)

    def half_body(keep, got, own, send):
        send[...] = half_sum(keep, got, own)

    plane = ((3, hid, rows), F32)
    hbm = pl.BlockSpec(memory_space=pltpu.HBM)

    def zero_body(*refs):
        outs, (zero, sems) = refs[:2], refs[2:]
        zero[...] = jnp.zeros((hid, rows), F32)
        copies = [
            pltpu.make_async_copy(zero, out.at[tap], sems.at[2 * i + tap // 2])
            for i, out in enumerate(outs)
            for tap in (0, 2)
        ]
        for copy in copies:
            copy.start()
        for copy in copies:
            copy.wait()

    def total_body(place, _, own_k, own_p, got_k, got_p, taps_ref, proj_ref, k, p, sems):
        k[...] = own_k[0] + got_k[place].astype(F32)
        first = pltpu.make_async_copy(k, taps_ref.at[1], sems.at[0])
        first.start()
        p[...] = own_p[0] + got_p[place].astype(F32)
        second = pltpu.make_async_copy(p, proj_ref, sems.at[1])
        second.start()
        first.wait()
        second.wait()

    def total(place, planes, own_k, own_p, got_k, got_p, name):
        taps, proj = pl.pallas_call(
            functools.partial(total_body, place),
            out_shape=[jax.ShapeDtypeStruct(*plane), jax.ShapeDtypeStruct((hid, rows), F32)],
            in_specs=[hbm] + [VMEM] * 4,
            out_specs=[hbm, hbm],
            scratch_shapes=[pltpu.VMEM((hid, rows), F32)] * 2 + [pltpu.SemaphoreType.DMA((2,))],
            input_output_aliases={0: 0},
            compiler_params=pltpu.CompilerParams(vmem_limit_bytes=16 << 20),
            name=name,
        )(
            pltpu.with_memory_space_constraint(planes, pltpu.HBM),
            *[
                pltpu.with_memory_space_constraint(a, pltpu.VMEM)
                for a in (own_k, own_p, got_k, got_p)
            ],
        )
        return taps, proj.T

    planes = pl.pallas_call(
        zero_body,
        out_shape=[pltpu.HBM(*plane)] * 2,
        in_specs=[],
        out_specs=[hbm, hbm],
        scratch_shapes=[pltpu.VMEM((hid, rows), F32), pltpu.SemaphoreType.DMA((4,))],
        compiler_params=pltpu.CompilerParams(vmem_limit_bytes=16 << 20),
        name="zero_planes",
    )()

    pack = [pltpu.VMEM((4, rows, bins), BF16)]
    *keep_b, send_k, send_p = call(
        second_weight_body,
        [(two, F32), (two, F32), (two, BF16), (two, BF16)],
        (z_b, gu_b, v_b, g_pair, g_near),
        "second_weights",
        pack,
    )
    got = swap(send, "mp", 1)

    def squash_body(keep_ref, got_ref, _, *outs):
        for i in (0, 1):
            outs[i][...] = (keep_ref[i] + got_ref[i].astype(F32)).astype(BF16)

    chip = call(squash_body, [((rows, bins), BF16)] * 2, (keep, got, keep_b[0]), "squash_sum")
    other = [swap(part, "mp", 2) for part in chip]
    got_b = swap(send_k, "ctx", 1), swap(send_p, "ctx", 2)

    def back_body(g_ref, mid_ref, chip0, chip1, other0, other1, *outs):
        for i, (chip_ref, other_ref) in enumerate(((chip0, other1), (chip1, other0))):
            grad = chip_ref[...].astype(F32) + other_ref[...].astype(F32)
            outs[i][...] = (
                g_ref[i].astype(F32) + grad * slope_of(mid_ref[i].astype(F32))
            ).astype(BF16)

    g_mid = call(
        back_body, [((rows, bins), BF16)] * 2, (g_pair, mid, *chip, *other), "middle_grad"
    )
    g_mid = [g_mid[0], swap(g_mid[0], "mp", 1), g_mid[1], swap(g_mid[1], "mp", 1)]

    ygot = swap(ysend, "mp", 1)

    def last_sum_body(keep_ref, got_ref, *rest):
        own_ref, send_ref = rest[-2:]
        own_ref[...] = keep_ref[0] + got_ref[0].astype(F32)
        send_ref[...] = (keep_ref[1] + got_ref[1].astype(F32)).astype(BF16)

    def last_sum(keep, got, name, after=()):
        outs = [((rows, bins), F32), ((rows, bins), BF16)]
        return call(last_sum_body, outs, (keep, got, *after), name)

    y_own, y_send = last_sum(ykeep, ygot, "out_sum")
    y_got = swap(y_send, "mp", 2)

    def out_body(mid_ref, own_ref, got_ref, out_ref):
        mixed = own_ref[...] + got_ref[...].astype(F32)
        out_ref[...] = (mid_ref[0].astype(F32) + mixed).astype(BF16)

    (second_out,) = call(out_body, [((rows, bins), BF16)], (mid, y_own, y_got), "out", final=True)

    def first_back_body(*refs):
        grads, (k_ref, p_ref, s_ref, gu_ref, keep_ref, send_ref) = refs[:4], refs[4:]
        m = lax.axis_index("mp")
        gv = jnp.zeros((hid, bins), F32)
        for j in range(4):
            gv = gv + dot(p_ref[:, block(m, j)], grads[j][...])
        gu = (gv * s_ref[...]).astype(BF16)
        gu_ref[...] = gu
        for i, j in enumerate((1, 3)):
            send_ref[i] = dot(k_ref[:, block(m, j)], gu, ((0,), (0,))).astype(BF16)
        for i, j in enumerate((0, 2)):
            keep_ref[i] = dot(k_ref[:, block(m, j)], gu, ((0,), (0,)))

    gu_a, keep, send = call(
        first_back_body,
        [((hid, bins), BF16), ((2, rows, bins), F32), ((2, rows, bins), BF16)],
        (*g_mid, tap_a, cols_a, slope_a),
        "first_backward",
    )
    keep_ap, send_p, own_bk = call(
        first_proj_body,
        [(two, F32), (three, BF16), (one, F32)],
        (v_a, *g_mid, keep_b[0], got_b[0]),
        "first_proj",
        pack,
    )
    got_p = swap(send_p, "ctx", 2)
    keep_ak, send_k, own_bp = call(
        first_taps_body,
        [(two, F32), (three, BF16), (one, F32)],
        (z_a, gu_a, keep_b[1], got_b[1], own_bk),
        "first_taps",
    )
    got_k = swap(send_k, "ctx", 1)
    got = swap(send, "mp", 1)
    e_own, e_send = last_sum(keep, got, "entry_sum")
    e_got = swap(e_send, "mp", 2)

    def entry_body(g_ref, x_ref, own_ref, got_ref, out_ref):
        grad = own_ref[...] + got_ref[...].astype(F32)
        out_ref[...] = (
            g_ref[...].astype(F32) + grad * slope_of(x_ref[...].astype(F32))
        ).astype(BF16)

    (entry,) = call(entry_body, [((rows, bins), BF16)], (g_mid[0], x_own, e_own, e_got), "entry", final=True)

    half = [(one, F32), (one[1:], BF16)]
    own_ak, send_k = call(half_body, half, (keep_ak, got_k), "taps_half")
    last_k = swap(send_k, "ctx", 2)
    own_ap, send_p = call(half_body, half, (keep_ap, got_p), "proj_half")
    last_p = swap(send_p, "ctx", 1)
    taps_b_grad, point_b_grad = total(2, planes[0], own_bk, own_bp, got_p, got_k, "second_total")
    taps_a_grad, point_a_grad = total(Ellipsis, planes[1], own_ak, own_ap, last_k, last_p, "first_total")
    return second_out, entry, taps_a_grad, point_a_grad, taps_b_grad, point_b_grad


def solution(mesh):
    sizes = dict(mesh.shape)

    def shards(x, *rest):
        span = x.shape[1] * sizes["ctx"]
        fast = (
            min(FIRST_DILATION, SECOND_DILATION) >= span
            and sizes["mp"] == 4
            and sizes["ctx"] == 4
        )
        return (fast_shards if fast else general_shards)(x, *rest)

    return jax.shard_map(
        shards,
        mesh=mesh,
        in_specs=(
            P("mp", ("groups", "ctx")),
            P(None, "mp", None),
            P(None, "mp"),
            P(None, "mp", None),
            P(None, "mp"),
            P("mp", "ctx", "groups"),
        ),
        out_specs=(
            P("mp", ("groups", "ctx")),
            P("mp", ("groups", "ctx")),
            P("groups", "mp", "ctx"),
            P(("groups", "ctx"), "mp"),
            P("groups", "mp", "ctx"),
            P(("groups", "ctx"), "mp"),
        ),
        check_vma=False,
    )
```

```python
import functools

import jax
import jax.numpy as jnp
from jax import lax
from jax.experimental import pallas as pl
from jax.experimental.pallas import tpu as pltpu
from jax.sharding import PartitionSpec as P

FIRST_DILATION = 1024
SECOND_DILATION = 2048
F32 = jnp.float32
BF16 = jnp.bfloat16
ROOT = 0.7978845608028654
CUBIC = 0.044715


def shifted(value, axis, by):
    length = lax.axis_size(axis)
    pairs = [(i, i + by) for i in range(length) if 0 <= i + by < length]
    return lax.ppermute(value, axis, pairs)


def gelu_slope(values):
    return jax.jvp(jax.nn.gelu, (values,), (jnp.ones_like(values),))[1]


def contract_first(left, right):
    return lax.dot_general(
        left, right, (((0,), (0,)), ((), ())), preferred_element_type=jnp.float32
    )


def contract_last(left, right):
    return lax.dot_general(
        left, right, (((1,), (1,)), ((), ())), preferred_element_type=jnp.float32
    )


def hop_steps(activations, dilation):
    return dilation // activations.shape[1]


def residual_block_forward(activations, conv_weight, point_weight, dilation):
    hop_count = hop_steps(activations, dilation)
    squash_part = jax.nn.gelu(activations.astype(jnp.float32)).astype(jnp.bfloat16)
    squashed = lax.all_gather(squash_part, "mp", axis=0, tiled=True)
    earlier = shifted(squashed, "ctx", hop_count)
    later = shifted(squashed, "ctx", -hop_count)
    pre_act = jnp.dot(conv_weight[0], earlier, preferred_element_type=jnp.float32)
    pre_act = pre_act + jnp.dot(conv_weight[1], squashed, preferred_element_type=jnp.float32)
    pre_act = pre_act + jnp.dot(conv_weight[2], later, preferred_element_type=jnp.float32)
    hidden = jax.nn.gelu(pre_act).astype(jnp.bfloat16)
    mixed = lax.psum_scatter(
        jnp.dot(point_weight, hidden, preferred_element_type=jnp.float32).astype(jnp.bfloat16),
        "mp",
        scatter_dimension=0,
        tiled=True,
    ).astype(jnp.float32)
    result = (activations.astype(jnp.float32) + mixed).astype(jnp.bfloat16)
    return (result, squashed, pre_act, hidden)


def residual_block_backward(
    incoming_gradient, activations, squashed, pre_act, hidden, conv_weight, point_weight, dilation
):
    hop_count = hop_steps(activations, dilation)
    upstream_full = lax.all_gather(incoming_gradient, "mp", axis=0, tiled=True)
    grad_hidden = contract_first(point_weight, upstream_full)
    grad_pre = (grad_hidden * gelu_slope(pre_act)).astype(jnp.bfloat16)
    grad_later = shifted(grad_pre, "ctx", -hop_count)
    grad_earlier = shifted(grad_pre, "ctx", hop_count)
    moved = (grad_later, grad_pre, grad_earlier)
    grad_conv = jnp.stack([contract_last(part, squashed) for part in moved])
    grad_point = contract_last(upstream_full, hidden)
    total = contract_first(conv_weight[0], moved[0])
    total = total + contract_first(conv_weight[1], moved[1])
    grad_squash = lax.psum_scatter(
        (total + contract_first(conv_weight[2], moved[2])).astype(jnp.bfloat16),
        "mp",
        scatter_dimension=0,
        tiled=True,
    ).astype(jnp.float32)
    previous = (
        incoming_gradient.astype(jnp.float32)
        + grad_squash * gelu_slope(activations.astype(jnp.float32))
    ).astype(jnp.bfloat16)
    return (previous, grad_conv, grad_point)


def reduce_block(grad_conv, grad_point):
    return (
        lax.psum_scatter(
            grad_conv.astype(jnp.bfloat16), "ctx", scatter_dimension=2, tiled=True
        ).astype(jnp.float32),
        lax.psum_scatter(
            grad_point.astype(jnp.bfloat16), "ctx", scatter_dimension=0, tiled=True
        ).astype(jnp.float32),
    )


def general_shards(x, taps_a, point_a, taps_b, point_b, grad_heads):
    regrouped = lax.all_to_all(grad_heads, "ctx", split_axis=2, concat_axis=1, tiled=True)
    gradient = regrouped.reshape(regrouped.shape[0] * regrouped.shape[1], regrouped.shape[2])
    middle, z_a, u_a, v_a = residual_block_forward(x, taps_a, point_a, FIRST_DILATION)
    result, z_b, u_b, v_b = residual_block_forward(middle, taps_b, point_b, SECOND_DILATION)
    gradient, conv_b, proj_b = residual_block_backward(
        gradient, middle, z_b, u_b, v_b, taps_b, point_b, SECOND_DILATION
    )
    conv_b, proj_b = reduce_block(conv_b, proj_b)
    gradient, conv_a, proj_a = residual_block_backward(
        gradient, x, z_a, u_a, v_a, taps_a, point_a, FIRST_DILATION
    )
    conv_a, proj_a = reduce_block(conv_a, proj_a)
    return result, gradient, conv_a, proj_a, conv_b, proj_b


def swap(value, axis, bits):
    size = lax.axis_size(axis)
    return lax.ppermute(value, axis, [(i, i ^ bits) for i in range(size)])


def dot(left, right, dims=((1,), (0,))):
    return lax.dot_general(left, right, (dims, ((), ())), preferred_element_type=F32)


def gelu(s):
    return 0.5 * s * (1.0 + jnp.tanh(ROOT * (s + CUBIC * (s * s * s))))


def gelu_and_slope(s):
    sq = s * s
    t = jnp.tanh(ROOT * (s + CUBIC * (s * sq)))
    half = 0.5 * (1.0 + t)
    slope = half + 0.5 * s * (1.0 - t * t) * (ROOT * (1.0 + 3.0 * CUBIC * sq))
    return s * half, slope


def slope_of(s):
    return gelu_and_slope(s)[1]


VMEM = pl.BlockSpec(memory_space=pltpu.VMEM)


def call(body, outs, args, name, scratch=(), final=False):
    struct = jax.ShapeDtypeStruct if final else pltpu.VMEM
    return pl.pallas_call(
        body,
        out_shape=[struct(s, d) for s, d in outs],
        in_specs=[VMEM] * len(args),
        out_specs=[VMEM] * len(outs),
        scratch_shapes=scratch,
        compiler_params=pltpu.CompilerParams(vmem_limit_bytes=16 << 20),
        name=name,
    )(*[pltpu.with_memory_space_constraint(a, pltpu.VMEM) for a in args])


def fast_shards(x, taps_a, point_a, taps_b, point_b, grad_heads):
    rows, bins = x.shape
    hid, chans = taps_a.shape[1], taps_a.shape[2]
    heads, val, _ = grad_heads.shape
    def block(m, j):
        return pl.ds(pl.multiple_of((m ^ j) * rows, rows), rows)

    x_far = swap(x, "mp", 2)
    x_near = swap(x, "mp", 1)

    raw_far = swap(grad_heads, "mp", 2)

    def load_body(x_ref, ta, tb, ca, cb, g_ref, *rest):
        outs, sems = rest[:-1], rest[-1]
        sources = [x_ref, ta.at[1], tb.at[1], ca, cb, g_ref]
        copies = [
            pltpu.make_async_copy(source, out, sems.at[i])
            for i, (source, out) in enumerate(zip(sources, outs))
        ]
        for copy in copies:
            copy.start()
        for copy in copies:
            copy.wait()

    x_own, tap_a, tap_b, cols_a, cols_b, raw_own = pl.pallas_call(
        load_body,
        out_shape=[pltpu.VMEM((rows, bins), BF16)]
        + [pltpu.VMEM((hid, chans), BF16)] * 4
        + [pltpu.VMEM(grad_heads.shape, BF16)],
        in_specs=[pl.BlockSpec(memory_space=pltpu.HBM)] * 6,
        out_specs=[VMEM] * 6,
        scratch_shapes=[pltpu.SemaphoreType.DMA((6,))],
        compiler_params=pltpu.CompilerParams(vmem_limit_bytes=16 << 20),
        name="load",
    )(
        *[
            pltpu.with_memory_space_constraint(source, pltpu.HBM)
            for source in (x, taps_a, taps_b, point_a.T, point_b.T, grad_heads)
        ]
    )
    x_far, x_own = lax.optimization_barrier((x_far, x_own))
    x_cross = swap(x_far, "mp", 1)

    def split_body(own_ref, far_ref, *outs):
        c = lax.axis_index("ctx")
        for k in range(4):
            at = pl.ds(pl.multiple_of((c ^ k) * bins, bins), bins)
            for i, ref in enumerate((own_ref, far_ref)):
                outs[k][i] = ref[:, :, at]

    piece = ((2, heads, val, bins), BF16)
    pieces = call(split_body, [piece] * 4, (raw_own, raw_far), "split_grad")
    pieces = [pieces[0]] + [swap(pieces[k], "ctx", k) for k in (1, 2, 3)]

    def join_body(*refs):
        c = lax.axis_index("ctx")
        out = refs[4]
        for k in range(4):
            out[:, :, c ^ k] = refs[k][...]

    (g_pair,) = call(join_body, [((2, heads, 4, val, bins), BF16)], pieces, "join_grad")
    g_pair = g_pair.reshape(2, rows, bins)
    g_near = swap(g_pair, "mp", 1)

    def first_body(x0, x1, x2, x3, k_ref, p_ref, _, z_ref, v_ref, s_ref, keep_ref, send_ref):
        m = lax.axis_index("mp")
        u = jnp.zeros((hid, bins), F32)
        for j, ref in enumerate((x0, x1, x2, x3)):
            z = gelu(ref[...].astype(F32)).astype(BF16)
            z_ref[j] = z
            u = u + dot(k_ref[:, block(m, j)], z)
        v, slope = gelu_and_slope(u)
        v = v.astype(BF16)
        v_ref[...] = v
        s_ref[...] = slope
        for i, j in enumerate((1, 3)):
            send_ref[i] = dot(p_ref[:, block(m, j)], v, ((0,), (0,))).astype(BF16)
        for i, j in enumerate((0, 2)):
            keep_ref[i] = dot(p_ref[:, block(m, j)], v, ((0,), (0,)))

    z_a, v_a, slope_a, keep, send = call(
        first_body,
        [
            ((4, rows, bins), BF16),
            ((hid, bins), BF16),
            ((hid, bins), F32),
            ((2, rows, bins), F32),
            ((2, rows, bins), BF16),
        ],
        (x_own, x_near, x_far, x_cross, tap_a, cols_a, raw_far),
        "first_forward",
    )
    got = swap(send, "mp", 1)

    def mix_body(keep_ref, got_ref, out_ref):
        out_ref[...] = (keep_ref[...] + got_ref[...].astype(F32)).astype(BF16)

    (chip,) = call(mix_body, [((2, rows, bins), BF16)], (keep, got), "mix_sum")
    other = swap(chip, "mp", 2)

    def middle_body(x0, x2, chip_ref, other_ref, out_ref):
        for i, ref in enumerate((x0, x2)):
            mixed = chip_ref[i].astype(F32) + other_ref[1 - i].astype(F32)
            out_ref[i] = (ref[...].astype(F32) + mixed).astype(BF16)

    (mid,) = call(
        middle_body, [((2, rows, bins), BF16)], (x_own, x_far, chip, other), "middle"
    )
    mid_near = swap(mid, "mp", 1)

    def second_body(
        a_ref, b_ref, ga_ref, gb_ref, k_ref, p_ref,
        z_ref, v_ref, gu_ref, keep_ref, send_ref, ykeep_ref, ysend_ref,
    ):
        m = lax.axis_index("mp")
        u = jnp.zeros((hid, bins), F32)
        for j in range(4):
            part = (a_ref, b_ref)[j & 1][j >> 1]
            z = gelu(part.astype(F32)).astype(BF16)
            z_ref[j] = z
            u = u + dot(k_ref[:, block(m, j)], z)
        v, slope = gelu_and_slope(u)
        v = v.astype(BF16)
        v_ref[...] = v
        gv = jnp.zeros((hid, bins), F32)
        for j in range(4):
            gv = gv + dot(p_ref[:, block(m, j)], (ga_ref, gb_ref)[j & 1][j >> 1])
        gu = (gv * slope).astype(BF16)
        gu_ref[...] = gu
        for i, j in enumerate((1, 3)):
            send_ref[i] = dot(k_ref[:, block(m, j)], gu, ((0,), (0,))).astype(BF16)
        for i, j in enumerate((0, 2)):
            keep_ref[i] = dot(k_ref[:, block(m, j)], gu, ((0,), (0,)))
        for i, j in enumerate((1, 3)):
            ysend_ref[i] = dot(p_ref[:, block(m, j)], v, ((0,), (0,))).astype(BF16)
        for i, j in enumerate((0, 2)):
            ykeep_ref[i] = dot(p_ref[:, block(m, j)], v, ((0,), (0,)))

    z_b, v_b, gu_b, keep, send, ykeep, ysend = call(
        second_body,
        [
            ((4, rows, bins), BF16),
            ((hid, bins), BF16),
            ((hid, bins), BF16),
            ((2, rows, bins), F32),
            ((2, rows, bins), BF16),
            ((2, rows, bins), F32),
            ((2, rows, bins), BF16),
        ],
        (mid, mid_near, g_pair, g_near, tap_b, cols_b),
        "second_block",
    )
    def place(k):
        return lax.axis_index("mp") ^ lax.axis_index("ctx") ^ k

    def taps_pieces(z_ref, gu_ref, keep, send):
        for i in (0, 1):
            send[i] = dot(gu_ref[...], z_ref[place(1 + 2 * i)], ((1,), (1,))).astype(BF16)
        for i in (0, 1):
            keep[i] = dot(gu_ref[...], z_ref[place(2 * i)], ((1,), (1,)))

    def proj_pieces(v_ref, g_ref, keep, send):
        for i in (0, 1):
            send[i] = dot(v_ref[...], g_ref[place(2 + i)], ((1,), (1,))).astype(BF16)
        for i in (0, 1):
            keep[i] = dot(v_ref[...], g_ref[place(i)], ((1,), (1,)))

    one, two, three = ((n, hid, rows) for n in (1, 2, 3))

    def second_weight_body(z_ref, gu_ref, v_ref, ga_ref, gb_ref, *rest):
        keep_k, keep_p, send_k, send_p, g_ref = rest
        for i in range(4):
            g_ref[i] = (ga_ref, gb_ref)[i & 1][i >> 1]
        proj_pieces(v_ref, g_ref, keep_p, send_p)
        taps_pieces(z_ref, gu_ref, keep_k, send_k)

    def half_sum(keep, got, own):
        own[0] = keep[0] + got[0].astype(F32)
        return (keep[1] + got[1].astype(F32)).astype(BF16)

    def first_proj_body(v_ref, g0, g1, g2, g3, keep_b, got_b, keep, send, own, g_ref):
        for i, ref in enumerate((g0, g1, g2, g3)):
            g_ref[i] = ref[...]
        send[2] = half_sum(keep_b, got_b, own)
        proj_pieces(v_ref, g_ref, keep, send)

    def first_taps_body(z_ref, gu_ref, keep_b, got_b, keep, send, own):
        send[2] = half_sum(keep_b, got_b, own)
        taps_pieces(z_ref, gu_ref, keep, send)

    def half_body(keep, got, *rest):
        own, send = rest[-2:]
        send[...] = half_sum(keep, got, own)

    plane = ((3, hid, rows), F32)
    hbm = pl.BlockSpec(memory_space=pltpu.HBM)

    def zero_body(*refs):
        outs, (zero, sems) = refs[:2], refs[2:]
        zero[...] = jnp.zeros((hid, rows), F32)
        copies = [
            pltpu.make_async_copy(zero, out.at[tap], sems.at[2 * i + tap // 2])
            for i, out in enumerate(outs)
            for tap in (0, 2)
        ]
        for copy in copies:
            copy.start()
        for copy in copies:
            copy.wait()

    def total_body(place, _, own_k, own_p, got_k, got_p, taps_ref, proj_ref, k, p, sems):
        k[...] = own_k[0] + got_k[place].astype(F32)
        first = pltpu.make_async_copy(k, taps_ref.at[1], sems.at[0])
        first.start()
        p[...] = own_p[0] + got_p[place].astype(F32)
        second = pltpu.make_async_copy(p, proj_ref, sems.at[1])
        second.start()
        first.wait()
        second.wait()

    def total(place, planes, own_k, own_p, got_k, got_p, name):
        taps, proj = pl.pallas_call(
            functools.partial(total_body, place),
            out_shape=[jax.ShapeDtypeStruct(*plane), jax.ShapeDtypeStruct((hid, rows), F32)],
            in_specs=[hbm] + [VMEM] * 4,
            out_specs=[hbm, hbm],
            scratch_shapes=[pltpu.VMEM((hid, rows), F32)] * 2 + [pltpu.SemaphoreType.DMA((2,))],
            input_output_aliases={0: 0},
            compiler_params=pltpu.CompilerParams(vmem_limit_bytes=16 << 20),
            name=name,
        )(
            pltpu.with_memory_space_constraint(planes, pltpu.HBM),
            *[
                pltpu.with_memory_space_constraint(a, pltpu.VMEM)
                for a in (own_k, own_p, got_k, got_p)
            ],
        )
        return taps, proj.T

    planes = pl.pallas_call(
        zero_body,
        out_shape=[pltpu.HBM(*plane)] * 2,
        in_specs=[],
        out_specs=[hbm, hbm],
        scratch_shapes=[pltpu.VMEM((hid, rows), F32), pltpu.SemaphoreType.DMA((4,))],
        compiler_params=pltpu.CompilerParams(vmem_limit_bytes=16 << 20),
        name="zero_planes",
    )()

    pack = [pltpu.VMEM((4, rows, bins), BF16)]
    *keep_b, send_k, send_p = call(
        second_weight_body,
        [(two, F32), (two, F32), (two, BF16), (two, BF16)],
        (z_b, gu_b, v_b, g_pair, g_near),
        "second_weights",
        pack,
    )
    got = swap(send, "mp", 1)

    def squash_body(keep_ref, got_ref, _, out_ref):
        mix_body(keep_ref, got_ref, out_ref)

    (chip,) = call(squash_body, [((2, rows, bins), BF16)], (keep, got, keep_b[0]), "squash_sum")
    other = swap(chip, "mp", 2)
    got_b = swap(send_k, "ctx", 1), swap(send_p, "ctx", 2)

    def back_body(g_ref, mid_ref, chip_ref, other_ref, *outs):
        for i in (0, 1):
            grad = chip_ref[i].astype(F32) + other_ref[1 - i].astype(F32)
            outs[i][...] = (
                g_ref[i].astype(F32) + grad * slope_of(mid_ref[i].astype(F32))
            ).astype(BF16)

    g_mid = call(
        back_body, [((rows, bins), BF16)] * 2, (g_pair, mid, chip, other), "middle_grad"
    )
    g_mid = [g_mid[0], swap(g_mid[0], "mp", 1), g_mid[1], swap(g_mid[1], "mp", 1)]

    ygot = swap(ysend, "mp", 1)

    def last_sum_body(keep_ref, got_ref, *rest):
        own_ref, send_ref = rest[-2:]
        own_ref[...] = keep_ref[0] + got_ref[0].astype(F32)
        send_ref[...] = (keep_ref[1] + got_ref[1].astype(F32)).astype(BF16)

    def last_sum(keep, got, name, after=()):
        outs = [((rows, bins), F32), ((rows, bins), BF16)]
        return call(last_sum_body, outs, (keep, got, *after), name)

    y_own, y_send = last_sum(ykeep, ygot, "out_sum")
    y_got = swap(y_send, "mp", 2)

    def out_body(mid_ref, own_ref, got_ref, out_ref):
        mixed = own_ref[...] + got_ref[...].astype(F32)
        out_ref[...] = (mid_ref[0].astype(F32) + mixed).astype(BF16)

    (second_out,) = call(out_body, [((rows, bins), BF16)], (mid, y_own, y_got), "out", final=True)

    def first_back_body(*refs):
        grads, (k_ref, p_ref, s_ref, gu_ref, keep_ref, send_ref) = refs[:4], refs[4:]
        m = lax.axis_index("mp")
        gv = jnp.zeros((hid, bins), F32)
        for j in range(4):
            gv = gv + dot(p_ref[:, block(m, j)], grads[j][...])
        gu = (gv * s_ref[...]).astype(BF16)
        gu_ref[...] = gu
        for i, j in enumerate((1, 3)):
            send_ref[i] = dot(k_ref[:, block(m, j)], gu, ((0,), (0,))).astype(BF16)
        for i, j in enumerate((0, 2)):
            keep_ref[i] = dot(k_ref[:, block(m, j)], gu, ((0,), (0,)))

    gu_a, keep, send = call(
        first_back_body,
        [((hid, bins), BF16), ((2, rows, bins), F32), ((2, rows, bins), BF16)],
        (*g_mid, tap_a, cols_a, slope_a),
        "first_backward",
    )
    keep_ap, send_p, own_bk = call(
        first_proj_body,
        [(two, F32), (three, BF16), (one, F32)],
        (v_a, *g_mid, keep_b[0], got_b[0]),
        "first_proj",
        pack,
    )
    got_p = swap(send_p, "ctx", 2)
    keep_ak, send_k, own_bp = call(
        first_taps_body,
        [(two, F32), (three, BF16), (one, F32)],
        (z_a, gu_a, keep_b[1], got_b[1]),
        "first_taps",
    )
    got_k = swap(send_k, "ctx", 1)
    got = swap(send, "mp", 1)
    e_own, e_send = last_sum(keep, got, "entry_sum")
    e_got = swap(e_send, "mp", 2)

    def entry_body(g_ref, x_ref, own_ref, got_ref, out_ref):
        grad = own_ref[...] + got_ref[...].astype(F32)
        out_ref[...] = (
            g_ref[...].astype(F32) + grad * slope_of(x_ref[...].astype(F32))
        ).astype(BF16)

    (entry,) = call(entry_body, [((rows, bins), BF16)], (g_mid[0], x_own, e_own, e_got), "entry", final=True)

    half = [(one, F32), (one[1:], BF16)]
    own_ap, send_p = call(half_body, half, (keep_ap, got_p), "proj_half")
    last_p = swap(send_p, "ctx", 1)
    own_ak, send_k = call(half_body, half, (keep_ak, got_k, own_ap), "taps_half")
    last_k = swap(send_k, "ctx", 2)
    taps_b_grad, point_b_grad = total(2, planes[0], own_bk, own_bp, got_p, got_k, "second_total")
    taps_a_grad, point_a_grad = total(Ellipsis, planes[1], own_ak, own_ap, last_k, last_p, "first_total")
    return second_out, entry, taps_a_grad, point_a_grad, taps_b_grad, point_b_grad


def solution(mesh):
    sizes = dict(mesh.shape)

    def shards(x, *rest):
        span = x.shape[1] * sizes["ctx"]
        fast = (
            min(FIRST_DILATION, SECOND_DILATION) >= span
            and sizes["mp"] == 4
            and sizes["ctx"] == 4
        )
        return (fast_shards if fast else general_shards)(x, *rest)

    return jax.shard_map(
        shards,
        mesh=mesh,
        in_specs=(
            P("mp", ("groups", "ctx")),
            P(None, "mp", None),
            P(None, "mp"),
            P(None, "mp", None),
            P(None, "mp"),
            P("mp", "ctx", "groups"),
        ),
        out_specs=(
            P("mp", ("groups", "ctx")),
            P("mp", ("groups", "ctx")),
            P("groups", "mp", "ctx"),
            P(("groups", "ctx"), "mp"),
            P("groups", "mp", "ctx"),
            P(("groups", "ctx"), "mp"),
        ),
        check_vma=False,
    )
```

```python
import jax
import jax.numpy as jnp
from jax import lax
from jax.experimental import pallas as pl
from jax.experimental.pallas import tpu as pltpu
from jax.sharding import PartitionSpec as P

FIRST_DILATION = 1024
SECOND_DILATION = 2048
F32 = jnp.float32
BF16 = jnp.bfloat16
ROOT = 0.7978845608028654
CUBIC = 0.044715


def shifted(value, axis, by):
    length = lax.axis_size(axis)
    pairs = [(i, i + by) for i in range(length) if 0 <= i + by < length]
    return lax.ppermute(value, axis, pairs)


def gelu_slope(values):
    return jax.jvp(jax.nn.gelu, (values,), (jnp.ones_like(values),))[1]


def contract_first(left, right):
    return lax.dot_general(
        left, right, (((0,), (0,)), ((), ())), preferred_element_type=jnp.float32
    )


def contract_last(left, right):
    return lax.dot_general(
        left, right, (((1,), (1,)), ((), ())), preferred_element_type=jnp.float32
    )


def hop_steps(activations, dilation):
    return dilation // activations.shape[1]


def residual_block_forward(activations, conv_weight, point_weight, dilation):
    hop_count = hop_steps(activations, dilation)
    squash_part = jax.nn.gelu(activations.astype(jnp.float32)).astype(jnp.bfloat16)
    squashed = lax.all_gather(squash_part, "mp", axis=0, tiled=True)
    earlier = shifted(squashed, "ctx", hop_count)
    later = shifted(squashed, "ctx", -hop_count)
    pre_act = jnp.dot(conv_weight[0], earlier, preferred_element_type=jnp.float32)
    pre_act = pre_act + jnp.dot(conv_weight[1], squashed, preferred_element_type=jnp.float32)
    pre_act = pre_act + jnp.dot(conv_weight[2], later, preferred_element_type=jnp.float32)
    hidden = jax.nn.gelu(pre_act).astype(jnp.bfloat16)
    mixed = lax.psum_scatter(
        jnp.dot(point_weight, hidden, preferred_element_type=jnp.float32).astype(jnp.bfloat16),
        "mp",
        scatter_dimension=0,
        tiled=True,
    ).astype(jnp.float32)
    result = (activations.astype(jnp.float32) + mixed).astype(jnp.bfloat16)
    return (result, squashed, pre_act, hidden)


def residual_block_backward(
    incoming_gradient, activations, squashed, pre_act, hidden, conv_weight, point_weight, dilation
):
    hop_count = hop_steps(activations, dilation)
    upstream_full = lax.all_gather(incoming_gradient, "mp", axis=0, tiled=True)
    grad_hidden = contract_first(point_weight, upstream_full)
    grad_pre = (grad_hidden * gelu_slope(pre_act)).astype(jnp.bfloat16)
    grad_later = shifted(grad_pre, "ctx", -hop_count)
    grad_earlier = shifted(grad_pre, "ctx", hop_count)
    moved = (grad_later, grad_pre, grad_earlier)
    grad_conv = jnp.stack([contract_last(part, squashed) for part in moved])
    grad_point = contract_last(upstream_full, hidden)
    total = contract_first(conv_weight[0], moved[0])
    total = total + contract_first(conv_weight[1], moved[1])
    grad_squash = lax.psum_scatter(
        (total + contract_first(conv_weight[2], moved[2])).astype(jnp.bfloat16),
        "mp",
        scatter_dimension=0,
        tiled=True,
    ).astype(jnp.float32)
    previous = (
        incoming_gradient.astype(jnp.float32)
        + grad_squash * gelu_slope(activations.astype(jnp.float32))
    ).astype(jnp.bfloat16)
    return (previous, grad_conv, grad_point)


def reduce_block(grad_conv, grad_point):
    return (
        lax.psum_scatter(
            grad_conv.astype(jnp.bfloat16), "ctx", scatter_dimension=2, tiled=True
        ).astype(jnp.float32),
        lax.psum_scatter(
            grad_point.astype(jnp.bfloat16), "ctx", scatter_dimension=0, tiled=True
        ).astype(jnp.float32),
    )


def general_shards(x, taps_a, point_a, taps_b, point_b, grad_heads):
    regrouped = lax.all_to_all(grad_heads, "ctx", split_axis=2, concat_axis=1, tiled=True)
    gradient = regrouped.reshape(regrouped.shape[0] * regrouped.shape[1], regrouped.shape[2])
    middle, z_a, u_a, v_a = residual_block_forward(x, taps_a, point_a, FIRST_DILATION)
    result, z_b, u_b, v_b = residual_block_forward(middle, taps_b, point_b, SECOND_DILATION)
    gradient, conv_b, proj_b = residual_block_backward(
        gradient, middle, z_b, u_b, v_b, taps_b, point_b, SECOND_DILATION
    )
    conv_b, proj_b = reduce_block(conv_b, proj_b)
    gradient, conv_a, proj_a = residual_block_backward(
        gradient, x, z_a, u_a, v_a, taps_a, point_a, FIRST_DILATION
    )
    conv_a, proj_a = reduce_block(conv_a, proj_a)
    return result, gradient, conv_a, proj_a, conv_b, proj_b


def swap(value, axis, bits):
    size = lax.axis_size(axis)
    return lax.ppermute(value, axis, [(i, i ^ bits) for i in range(size)])


def dot(left, right, dims=((1,), (0,))):
    return lax.dot_general(left, right, (dims, ((), ())), preferred_element_type=F32)


def gelu(s):
    return 0.5 * s * (1.0 + jnp.tanh(ROOT * (s + CUBIC * (s * s * s))))


def gelu_and_slope(s):
    sq = s * s
    t = jnp.tanh(ROOT * (s + CUBIC * (s * sq)))
    half = 0.5 * (1.0 + t)
    slope = half + 0.5 * s * (1.0 - t * t) * (ROOT * (1.0 + 3.0 * CUBIC * sq))
    return s * half, slope


def slope_of(s):
    return gelu_and_slope(s)[1]


VMEM = pl.BlockSpec(memory_space=pltpu.VMEM)


def call(body, outs, args, name, scratch=(), final=False):
    struct = jax.ShapeDtypeStruct if final else pltpu.VMEM
    return pl.pallas_call(
        body,
        out_shape=[struct(s, d) for s, d in outs],
        in_specs=[VMEM] * len(args),
        out_specs=[VMEM] * len(outs),
        scratch_shapes=scratch,
        compiler_params=pltpu.CompilerParams(vmem_limit_bytes=16 << 20),
        name=name,
    )(*[pltpu.with_memory_space_constraint(a, pltpu.VMEM) for a in args])


def fast_shards(x, taps_a, point_a, taps_b, point_b, grad_heads):
    rows, bins = x.shape
    hid, chans = taps_a.shape[1], taps_a.shape[2]
    heads, val, _ = grad_heads.shape
    def block(m, j):
        return pl.ds(pl.multiple_of((m ^ j) * rows, rows), rows)

    x_far = swap(x, "mp", 2)
    x_near = swap(x, "mp", 1)

    raw_far = swap(grad_heads, "mp", 2)

    def load_body(x_ref, ta, tb, ca, cb, g_ref, *rest):
        outs, sems = rest[:-1], rest[-1]
        sources = [x_ref, ta.at[1], tb.at[1], ca, cb, g_ref]
        copies = [
            pltpu.make_async_copy(source, out, sems.at[i])
            for i, (source, out) in enumerate(zip(sources, outs))
        ]
        for copy in copies:
            copy.start()
        for copy in copies:
            copy.wait()

    x_own, tap_a, tap_b, cols_a, cols_b, raw_own = pl.pallas_call(
        load_body,
        out_shape=[pltpu.VMEM((rows, bins), BF16)]
        + [pltpu.VMEM((hid, chans), BF16)] * 4
        + [pltpu.VMEM(grad_heads.shape, BF16)],
        in_specs=[pl.BlockSpec(memory_space=pltpu.HBM)] * 6,
        out_specs=[VMEM] * 6,
        scratch_shapes=[pltpu.SemaphoreType.DMA((6,))],
        compiler_params=pltpu.CompilerParams(vmem_limit_bytes=16 << 20),
        name="load",
    )(
        *[
            pltpu.with_memory_space_constraint(source, pltpu.HBM)
            for source in (x, taps_a, taps_b, point_a.T, point_b.T, grad_heads)
        ]
    )
    x_far, x_own = lax.optimization_barrier((x_far, x_own))
    x_cross = swap(x_far, "mp", 1)

    def split_body(own_ref, far_ref, *outs):
        c = lax.axis_index("ctx")
        for k in range(4):
            at = pl.ds(pl.multiple_of((c ^ k) * bins, bins), bins)
            for i, ref in enumerate((own_ref, far_ref)):
                outs[k][i] = ref[:, :, at]

    piece = ((2, heads, val, bins), BF16)
    pieces = call(split_body, [piece] * 4, (raw_own, raw_far), "split_grad")
    pieces = [pieces[0]] + [swap(pieces[k], "ctx", k) for k in (1, 2, 3)]

    def join_body(*refs):
        c = lax.axis_index("ctx")
        out = refs[4]
        for k in range(4):
            out[:, :, c ^ k] = refs[k][...]

    (g_pair,) = call(join_body, [((2, heads, 4, val, bins), BF16)], pieces, "join_grad")
    g_pair = g_pair.reshape(2, rows, bins)
    g_near = swap(g_pair, "mp", 1)

    def first_body(x0, x1, x2, x3, k_ref, p_ref, _, z_ref, v_ref, s_ref, keep_ref, send_ref):
        m = lax.axis_index("mp")
        u = jnp.zeros((hid, bins), F32)
        for j, ref in enumerate((x0, x1, x2, x3)):
            z = gelu(ref[...].astype(F32)).astype(BF16)
            z_ref[j] = z
            u = u + dot(k_ref[:, block(m, j)], z)
        v, slope = gelu_and_slope(u)
        v = v.astype(BF16)
        v_ref[...] = v
        s_ref[...] = slope
        for i, j in enumerate((1, 3)):
            send_ref[i] = dot(p_ref[:, block(m, j)], v, ((0,), (0,))).astype(BF16)
        for i, j in enumerate((0, 2)):
            keep_ref[i] = dot(p_ref[:, block(m, j)], v, ((0,), (0,)))

    z_a, v_a, slope_a, keep, send = call(
        first_body,
        [
            ((4, rows, bins), BF16),
            ((hid, bins), BF16),
            ((hid, bins), F32),
            ((2, rows, bins), F32),
            ((2, rows, bins), BF16),
        ],
        (x_own, x_near, x_far, x_cross, tap_a, cols_a, raw_far),
        "first_forward",
    )
    got = swap(send, "mp", 1)

    def mix_body(keep_ref, got_ref, out_ref):
        out_ref[...] = (keep_ref[...] + got_ref[...].astype(F32)).astype(BF16)

    (chip,) = call(mix_body, [((2, rows, bins), BF16)], (keep, got), "mix_sum")
    other = swap(chip, "mp", 2)

    def middle_body(x0, x2, chip_ref, other_ref, out_ref):
        for i, ref in enumerate((x0, x2)):
            mixed = chip_ref[i].astype(F32) + other_ref[1 - i].astype(F32)
            out_ref[i] = (ref[...].astype(F32) + mixed).astype(BF16)

    (mid,) = call(
        middle_body, [((2, rows, bins), BF16)], (x_own, x_far, chip, other), "middle"
    )
    mid_near = swap(mid, "mp", 1)

    def second_body(
        a_ref, b_ref, ga_ref, gb_ref, k_ref, p_ref,
        z_ref, v_ref, gu_ref, keep_ref, send_ref, ykeep_ref, ysend_ref,
    ):
        m = lax.axis_index("mp")
        u = jnp.zeros((hid, bins), F32)
        for j in range(4):
            part = (a_ref, b_ref)[j & 1][j >> 1]
            z = gelu(part.astype(F32)).astype(BF16)
            z_ref[j] = z
            u = u + dot(k_ref[:, block(m, j)], z)
        v, slope = gelu_and_slope(u)
        v = v.astype(BF16)
        v_ref[...] = v
        gv = jnp.zeros((hid, bins), F32)
        for j in range(4):
            gv = gv + dot(p_ref[:, block(m, j)], (ga_ref, gb_ref)[j & 1][j >> 1])
        gu = (gv * slope).astype(BF16)
        gu_ref[...] = gu
        for i, j in enumerate((1, 3)):
            send_ref[i] = dot(k_ref[:, block(m, j)], gu, ((0,), (0,))).astype(BF16)
        for i, j in enumerate((0, 2)):
            keep_ref[i] = dot(k_ref[:, block(m, j)], gu, ((0,), (0,)))
        for i, j in enumerate((1, 3)):
            ysend_ref[i] = dot(p_ref[:, block(m, j)], v, ((0,), (0,))).astype(BF16)
        for i, j in enumerate((0, 2)):
            ykeep_ref[i] = dot(p_ref[:, block(m, j)], v, ((0,), (0,)))

    z_b, v_b, gu_b, keep, send, ykeep, ysend = call(
        second_body,
        [
            ((4, rows, bins), BF16),
            ((hid, bins), BF16),
            ((hid, bins), BF16),
            ((2, rows, bins), F32),
            ((2, rows, bins), BF16),
            ((2, rows, bins), F32),
            ((2, rows, bins), BF16),
        ],
        (mid, mid_near, g_pair, g_near, tap_b, cols_b),
        "second_block",
    )
    def place(k):
        return lax.axis_index("mp") ^ lax.axis_index("ctx") ^ k

    def taps_pieces(z_ref, gu_ref, keep, send):
        for i in (0, 1):
            send[i] = dot(gu_ref[...], z_ref[place(1 + 2 * i)], ((1,), (1,))).astype(BF16)
        for i in (0, 1):
            keep[i] = dot(gu_ref[...], z_ref[place(2 * i)], ((1,), (1,)))

    def proj_pieces(v_ref, g_ref, keep, send):
        for i in (0, 1):
            send[i] = dot(v_ref[...], g_ref[place(2 + i)], ((1,), (1,))).astype(BF16)
        for i in (0, 1):
            keep[i] = dot(v_ref[...], g_ref[place(i)], ((1,), (1,)))

    one, two = ((n, hid, rows) for n in (1, 2))

    def second_weight_body(z_ref, gu_ref, v_ref, ga_ref, gb_ref, *rest):
        keep_k, keep_p, send_k, send_p, g_ref = rest
        for i in range(4):
            g_ref[i] = (ga_ref, gb_ref)[i & 1][i >> 1]
        proj_pieces(v_ref, g_ref, keep_p, send_p)
        taps_pieces(z_ref, gu_ref, keep_k, send_k)

    def half_sum(keep, got, own):
        own[0] = keep[0] + got[0].astype(F32)
        return (keep[1] + got[1].astype(F32)).astype(BF16)

    def first_proj_body(v_ref, g0, g1, g2, g3, _, keep, send, g_ref):
        for i, ref in enumerate((g0, g1, g2, g3)):
            g_ref[i] = ref[...]
        proj_pieces(v_ref, g_ref, keep, send)

    def first_taps_body(z_ref, gu_ref, _, keep, send):
        taps_pieces(z_ref, gu_ref, keep, send)

    def half_body(keep, got, *rest):
        own, send = rest[-2:]
        send[...] = half_sum(keep, got, own)

    plane = ((3, hid, rows), F32)
    hbm = pl.BlockSpec(memory_space=pltpu.HBM)

    def zero_body(*refs):
        outs, (zero, sems) = refs[:2], refs[2:]
        zero[...] = jnp.zeros((hid, rows), F32)
        copies = [
            pltpu.make_async_copy(zero, out.at[tap], sems.at[2 * i + tap // 2])
            for i, out in enumerate(outs)
            for tap in (0, 2)
        ]
        for copy in copies:
            copy.start()
        for copy in copies:
            copy.wait()

    def total_body(_, own_k, own_p, got_k, got_p, taps_ref, proj_ref, k, p, sems):
        k[...] = own_k[0] + got_k[...].astype(F32)
        first = pltpu.make_async_copy(k, taps_ref.at[1], sems.at[0])
        first.start()
        p[...] = own_p[0] + got_p[...].astype(F32)
        second = pltpu.make_async_copy(p, proj_ref, sems.at[1])
        second.start()
        first.wait()
        second.wait()

    def total(planes, own_k, own_p, got_k, got_p, name):
        taps, proj = pl.pallas_call(
            total_body,
            out_shape=[jax.ShapeDtypeStruct(*plane), jax.ShapeDtypeStruct((hid, rows), F32)],
            in_specs=[hbm] + [VMEM] * 4,
            out_specs=[hbm, hbm],
            scratch_shapes=[pltpu.VMEM((hid, rows), F32)] * 2 + [pltpu.SemaphoreType.DMA((2,))],
            input_output_aliases={0: 0},
            compiler_params=pltpu.CompilerParams(vmem_limit_bytes=16 << 20),
            name=name,
        )(
            pltpu.with_memory_space_constraint(planes, pltpu.HBM),
            *[
                pltpu.with_memory_space_constraint(a, pltpu.VMEM)
                for a in (own_k, own_p, got_k, got_p)
            ],
        )
        return taps, proj.T

    planes = pl.pallas_call(
        zero_body,
        out_shape=[pltpu.HBM(*plane)] * 2,
        in_specs=[],
        out_specs=[hbm, hbm],
        scratch_shapes=[pltpu.VMEM((hid, rows), F32), pltpu.SemaphoreType.DMA((4,))],
        compiler_params=pltpu.CompilerParams(vmem_limit_bytes=16 << 20),
        name="zero_planes",
    )()

    pack = [pltpu.VMEM((4, rows, bins), BF16)]
    *keep_b, send_k, send_p = call(
        second_weight_body,
        [(two, F32), (two, F32), (two, BF16), (two, BF16)],
        (z_b, gu_b, v_b, g_pair, g_near),
        "second_weights",
        pack,
    )
    got = swap(send, "mp", 1)

    def squash_body(keep_ref, got_ref, _, out_ref):
        mix_body(keep_ref, got_ref, out_ref)

    (chip,) = call(squash_body, [((2, rows, bins), BF16)], (keep, got, keep_b[0]), "squash_sum")
    other = swap(chip, "mp", 2)
    got_b = swap(send_k, "ctx", 1), swap(send_p, "ctx", 2)

    def back_body(g_ref, mid_ref, chip_ref, other_ref, *outs):
        for i in (0, 1):
            grad = chip_ref[i].astype(F32) + other_ref[1 - i].astype(F32)
            outs[i][...] = (
                g_ref[i].astype(F32) + grad * slope_of(mid_ref[i].astype(F32))
            ).astype(BF16)

    g_mid = call(
        back_body, [((rows, bins), BF16)] * 2, (g_pair, mid, chip, other), "middle_grad"
    )
    g_mid = [g_mid[0], swap(g_mid[0], "mp", 1), g_mid[1], swap(g_mid[1], "mp", 1)]

    ygot = swap(ysend, "mp", 1)

    def last_sum_body(keep_ref, got_ref, *rest):
        own_ref, send_ref = rest[-2:]
        own_ref[...] = keep_ref[0] + got_ref[0].astype(F32)
        send_ref[...] = (keep_ref[1] + got_ref[1].astype(F32)).astype(BF16)

    def last_sum(keep, got, name, after=()):
        outs = [((rows, bins), F32), ((rows, bins), BF16)]
        return call(last_sum_body, outs, (keep, got, *after), name)

    y_own, y_send = last_sum(ykeep, ygot, "out_sum")
    y_got = swap(y_send, "mp", 2)

    def out_body(mid_ref, own_ref, got_ref, out_ref):
        mixed = own_ref[...] + got_ref[...].astype(F32)
        out_ref[...] = (mid_ref[0].astype(F32) + mixed).astype(BF16)

    (second_out,) = call(out_body, [((rows, bins), BF16)], (mid, y_own, y_got), "out", final=True)

    def entry_sum_body(keep_ref, got0, got1, own_ref, send_ref):
        own_ref[...] = keep_ref[0] + got0[...].astype(F32)
        send_ref[...] = (keep_ref[1] + got1[...].astype(F32)).astype(BF16)

    def first_back_body(*refs):
        grads, (k_ref, p_ref, s_ref, gu_ref, keep_ref, *sends) = refs[:4], refs[4:]
        m = lax.axis_index("mp")
        gv = jnp.zeros((hid, bins), F32)
        for j in range(4):
            gv = gv + dot(p_ref[:, block(m, j)], grads[j][...])
        gu = (gv * s_ref[...]).astype(BF16)
        gu_ref[...] = gu
        for i, j in enumerate((1, 3)):
            sends[i][...] = dot(k_ref[:, block(m, j)], gu, ((0,), (0,))).astype(BF16)
        for i, j in enumerate((0, 2)):
            keep_ref[i] = dot(k_ref[:, block(m, j)], gu, ((0,), (0,)))

    gu_a, keep, *sends = call(
        first_back_body,
        [((hid, bins), BF16), ((2, rows, bins), F32)] + [((rows, bins), BF16)] * 2,
        (*g_mid, tap_a, cols_a, slope_a),
        "first_backward",
    )
    keep_ap, send_p = call(
        first_proj_body, [(two, F32), (two, BF16)], (v_a, *g_mid, got_b[1]), "first_proj", pack
    )
    got_p = swap(send_p, "ctx", 2)
    keep_ak, send_k = call(
        first_taps_body, [(two, F32), (two, BF16)], (z_a, gu_a, got_b[0]), "first_taps"
    )
    got_k = swap(send_k, "ctx", 1)
    half = [(one, F32), (one[1:], BF16)]
    own_bk, send_k = call(half_body, half, (keep_b[0], got_b[0]), "second_taps_half")
    own_bp, send_p = call(half_body, half, (keep_b[1], got_b[1]), "second_proj_half")
    last_b = swap(send_k, "ctx", 2), swap(send_p, "ctx", 1)
    e_own, e_send = call(
        entry_sum_body,
        [((rows, bins), F32), ((rows, bins), BF16)],
        (keep, *[swap(part, "mp", 1) for part in sends]),
        "entry_sum",
    )
    e_got = swap(e_send, "mp", 2)

    def entry_body(g_ref, x_ref, own_ref, got_ref, out_ref):
        grad = own_ref[...] + got_ref[...].astype(F32)
        out_ref[...] = (
            g_ref[...].astype(F32) + grad * slope_of(x_ref[...].astype(F32))
        ).astype(BF16)

    (entry,) = call(entry_body, [((rows, bins), BF16)], (g_mid[0], x_own, e_own, e_got), "entry", final=True)

    own_ak, send_k = call(half_body, half, (keep_ak, got_k), "taps_half")
    last_k = swap(send_k, "ctx", 2)
    own_ap, send_p = call(half_body, half, (keep_ap, got_p, *last_b), "proj_half")
    last_p = swap(send_p, "ctx", 1)
    taps_b_grad, point_b_grad = total(planes[0], own_bk, own_bp, *last_b, "second_total")
    taps_a_grad, point_a_grad = total(planes[1], own_ak, own_ap, last_k, last_p, "first_total")
    return second_out, entry, taps_a_grad, point_a_grad, taps_b_grad, point_b_grad


def solution(mesh):
    sizes = dict(mesh.shape)

    def shards(x, *rest):
        span = x.shape[1] * sizes["ctx"]
        fast = (
            min(FIRST_DILATION, SECOND_DILATION) >= span
            and sizes["mp"] == 4
            and sizes["ctx"] == 4
        )
        return (fast_shards if fast else general_shards)(x, *rest)

    return jax.shard_map(
        shards,
        mesh=mesh,
        in_specs=(
            P("mp", ("groups", "ctx")),
            P(None, "mp", None),
            P(None, "mp"),
            P(None, "mp", None),
            P(None, "mp"),
            P("mp", "ctx", "groups"),
        ),
        out_specs=(
            P("mp", ("groups", "ctx")),
            P("mp", ("groups", "ctx")),
            P("groups", "mp", "ctx"),
            P(("groups", "ctx"), "mp"),
            P("groups", "mp", "ctx"),
            P(("groups", "ctx"), "mp"),
        ),
        check_vma=False,
    )
```

```python
import functools

import jax
import jax.numpy as jnp
from jax import lax
from jax.experimental import pallas as pl
from jax.experimental.pallas import tpu as pltpu
from jax.sharding import PartitionSpec as P

FIRST_DILATION = 1024
SECOND_DILATION = 2048
F32 = jnp.float32
BF16 = jnp.bfloat16
ROOT = 0.7978845608028654
CUBIC = 0.044715


def shifted(value, axis, by):
    length = lax.axis_size(axis)
    pairs = [(i, i + by) for i in range(length) if 0 <= i + by < length]
    return lax.ppermute(value, axis, pairs)


def gelu_slope(values):
    return jax.jvp(jax.nn.gelu, (values,), (jnp.ones_like(values),))[1]


def contract_first(left, right):
    return lax.dot_general(
        left, right, (((0,), (0,)), ((), ())), preferred_element_type=jnp.float32
    )


def contract_last(left, right):
    return lax.dot_general(
        left, right, (((1,), (1,)), ((), ())), preferred_element_type=jnp.float32
    )


def hop_steps(activations, dilation):
    return dilation // activations.shape[1]


def residual_block_forward(activations, conv_weight, point_weight, dilation):
    hop_count = hop_steps(activations, dilation)
    squash_part = jax.nn.gelu(activations.astype(jnp.float32)).astype(jnp.bfloat16)
    squashed = lax.all_gather(squash_part, "mp", axis=0, tiled=True)
    earlier = shifted(squashed, "ctx", hop_count)
    later = shifted(squashed, "ctx", -hop_count)
    pre_act = jnp.dot(conv_weight[0], earlier, preferred_element_type=jnp.float32)
    pre_act = pre_act + jnp.dot(conv_weight[1], squashed, preferred_element_type=jnp.float32)
    pre_act = pre_act + jnp.dot(conv_weight[2], later, preferred_element_type=jnp.float32)
    hidden = jax.nn.gelu(pre_act).astype(jnp.bfloat16)
    mixed = lax.psum_scatter(
        jnp.dot(point_weight, hidden, preferred_element_type=jnp.float32).astype(jnp.bfloat16),
        "mp",
        scatter_dimension=0,
        tiled=True,
    ).astype(jnp.float32)
    result = (activations.astype(jnp.float32) + mixed).astype(jnp.bfloat16)
    return (result, squashed, pre_act, hidden)


def residual_block_backward(
    incoming_gradient, activations, squashed, pre_act, hidden, conv_weight, point_weight, dilation
):
    hop_count = hop_steps(activations, dilation)
    upstream_full = lax.all_gather(incoming_gradient, "mp", axis=0, tiled=True)
    grad_hidden = contract_first(point_weight, upstream_full)
    grad_pre = (grad_hidden * gelu_slope(pre_act)).astype(jnp.bfloat16)
    grad_later = shifted(grad_pre, "ctx", -hop_count)
    grad_earlier = shifted(grad_pre, "ctx", hop_count)
    moved = (grad_later, grad_pre, grad_earlier)
    grad_conv = jnp.stack([contract_last(part, squashed) for part in moved])
    grad_point = contract_last(upstream_full, hidden)
    total = contract_first(conv_weight[0], moved[0])
    total = total + contract_first(conv_weight[1], moved[1])
    grad_squash = lax.psum_scatter(
        (total + contract_first(conv_weight[2], moved[2])).astype(jnp.bfloat16),
        "mp",
        scatter_dimension=0,
        tiled=True,
    ).astype(jnp.float32)
    previous = (
        incoming_gradient.astype(jnp.float32)
        + grad_squash * gelu_slope(activations.astype(jnp.float32))
    ).astype(jnp.bfloat16)
    return (previous, grad_conv, grad_point)


def reduce_block(grad_conv, grad_point):
    return (
        lax.psum_scatter(
            grad_conv.astype(jnp.bfloat16), "ctx", scatter_dimension=2, tiled=True
        ).astype(jnp.float32),
        lax.psum_scatter(
            grad_point.astype(jnp.bfloat16), "ctx", scatter_dimension=0, tiled=True
        ).astype(jnp.float32),
    )


def general_shards(x, taps_a, point_a, taps_b, point_b, grad_heads):
    regrouped = lax.all_to_all(grad_heads, "ctx", split_axis=2, concat_axis=1, tiled=True)
    gradient = regrouped.reshape(regrouped.shape[0] * regrouped.shape[1], regrouped.shape[2])
    middle, z_a, u_a, v_a = residual_block_forward(x, taps_a, point_a, FIRST_DILATION)
    result, z_b, u_b, v_b = residual_block_forward(middle, taps_b, point_b, SECOND_DILATION)
    gradient, conv_b, proj_b = residual_block_backward(
        gradient, middle, z_b, u_b, v_b, taps_b, point_b, SECOND_DILATION
    )
    conv_b, proj_b = reduce_block(conv_b, proj_b)
    gradient, conv_a, proj_a = residual_block_backward(
        gradient, x, z_a, u_a, v_a, taps_a, point_a, FIRST_DILATION
    )
    conv_a, proj_a = reduce_block(conv_a, proj_a)
    return result, gradient, conv_a, proj_a, conv_b, proj_b


def swap(value, axis, bits):
    size = lax.axis_size(axis)
    return lax.ppermute(value, axis, [(i, i ^ bits) for i in range(size)])


def dot(left, right, dims=((1,), (0,))):
    return lax.dot_general(left, right, (dims, ((), ())), preferred_element_type=F32)


def gelu(s):
    return 0.5 * s * (1.0 + jnp.tanh(ROOT * (s + CUBIC * (s * s * s))))


def gelu_and_slope(s):
    sq = s * s
    t = jnp.tanh(ROOT * (s + CUBIC * (s * sq)))
    half = 0.5 * (1.0 + t)
    slope = half + 0.5 * s * (1.0 - t * t) * (ROOT * (1.0 + 3.0 * CUBIC * sq))
    return s * half, slope


def slope_of(s):
    return gelu_and_slope(s)[1]


VMEM = pl.BlockSpec(memory_space=pltpu.VMEM)


def call(body, outs, args, name, scratch=(), final=False, alias=None):
    struct = jax.ShapeDtypeStruct if final else pltpu.VMEM
    return pl.pallas_call(
        body,
        out_shape=[struct(s, d) for s, d in outs],
        in_specs=[VMEM] * len(args),
        out_specs=[VMEM] * len(outs),
        scratch_shapes=scratch,
        input_output_aliases=alias or {},
        compiler_params=pltpu.CompilerParams(vmem_limit_bytes=16 << 20),
        name=name,
    )(*[pltpu.with_memory_space_constraint(a, pltpu.VMEM) for a in args])


def fast_shards(x, taps_a, point_a, taps_b, point_b, grad_heads):
    rows, bins = x.shape
    hid, chans = taps_a.shape[1], taps_a.shape[2]
    heads, val, _ = grad_heads.shape
    def block(m, j):
        return pl.ds(pl.multiple_of((m ^ j) * rows, rows), rows)

    x_far = swap(x, "mp", 2)
    x_near = swap(x, "mp", 1)

    raw_far = swap(grad_heads, "mp", 2)

    def load_body(x_ref, ta, tb, ca, cb, g_ref, *rest):
        outs, sems = rest[:-1], rest[-1]
        sources = [x_ref, ta.at[1], tb.at[1], ca, cb, g_ref]
        copies = [
            pltpu.make_async_copy(source, out, sems.at[i])
            for i, (source, out) in enumerate(zip(sources, outs))
        ]
        for copy in copies:
            copy.start()
        for copy in copies:
            copy.wait()

    x_own, tap_a, tap_b, cols_a, cols_b, raw_own = pl.pallas_call(
        load_body,
        out_shape=[pltpu.VMEM((rows, bins), BF16)]
        + [pltpu.VMEM((hid, chans), BF16)] * 4
        + [pltpu.VMEM(grad_heads.shape, BF16)],
        in_specs=[pl.BlockSpec(memory_space=pltpu.HBM)] * 6,
        out_specs=[VMEM] * 6,
        scratch_shapes=[pltpu.SemaphoreType.DMA((6,))],
        compiler_params=pltpu.CompilerParams(vmem_limit_bytes=16 << 20),
        name="load",
    )(
        *[
            pltpu.with_memory_space_constraint(source, pltpu.HBM)
            for source in (x, taps_a, taps_b, point_a.T, point_b.T, grad_heads)
        ]
    )

    def conv(refs, js, m, k_ref, z_ref, u):
        for ref, j in zip(refs, js):
            z = gelu(ref[...].astype(F32)).astype(BF16)
            z_ref[j] = z
            part = dot(k_ref[:, block(m, j)], z)
            u = part if u is None else u + part
        return u

    stack = ((4, rows, bins), BF16)
    inner = (hid, bins)

    def near_forward_body(x0, x1, k_ref, z_ref, u_ref):
        u_ref[...] = conv((x0, x1), (0, 1), lax.axis_index("mp"), k_ref, z_ref, None)

    z_a, u_a = call(
        near_forward_body, [stack, (inner, F32)], (x_own, x_near, tap_a), "near_forward"
    )
    x_far, u_a = lax.optimization_barrier((x_far, u_a))
    x_cross = swap(x_far, "mp", 1)

    def split_body(own_ref, far_ref, *outs):
        c = lax.axis_index("ctx")
        for k in range(4):
            at = pl.ds(pl.multiple_of((c ^ k) * bins, bins), bins)
            for i, ref in enumerate((own_ref, far_ref)):
                outs[k][i] = ref[:, :, at]

    piece = ((2, heads, val, bins), BF16)
    pieces = call(split_body, [piece] * 4, (raw_own, raw_far), "split_grad")
    pieces = [pieces[0]] + [swap(pieces[k], "ctx", k) for k in (1, 2, 3)]

    def join_body(*refs):
        c = lax.axis_index("ctx")
        out = refs[4]
        for k in range(4):
            out[:, :, c ^ k] = refs[k][...]

    (g_pair,) = call(join_body, [((2, heads, 4, val, bins), BF16)], pieces, "join_grad")
    g_pair = g_pair.reshape(2, rows, bins)
    g_near = swap(g_pair, "mp", 1)

    def near_half(w_ref, v, m, send_ref):
        for i, j in enumerate((1, 3)):
            send_ref[i] = dot(w_ref[:, block(m, j)], v, ((0,), (0,))).astype(BF16)

    def own_half(w_ref, v, m, keep_ref):
        for i, j in enumerate((0, 2)):
            keep_ref[i] = dot(w_ref[:, block(m, j)], v, ((0,), (0,)))

    def keep_body(w_ref, v_ref, keep_ref):
        own_half(w_ref, v_ref[...], lax.axis_index("mp"), keep_ref)

    def kept(w, v, name):
        return call(keep_body, [((2, rows, bins), F32)], (w, v), name)[0]

    def first_body(x2, x3, k_ref, p_ref, _, u_ref, zin_ref, z_ref, v_ref, s_ref, send_ref):
        m = lax.axis_index("mp")
        u = conv((x2, x3), (2, 3), m, k_ref, z_ref, u_ref[...])
        v, slope = gelu_and_slope(u)
        v = v.astype(BF16)
        v_ref[...] = v
        s_ref[...] = slope
        near_half(p_ref, v, m, send_ref)

    z_a, v_a, slope_a, send = call(
        first_body,
        [stack, (inner, BF16), (inner, F32), ((2, rows, bins), BF16)],
        (x_far, x_cross, tap_a, cols_a, raw_far, u_a, z_a),
        "first_forward",
        alias={6: 0},
    )
    keep = kept(cols_a, v_a, "mix_keep")
    got = swap(send, "mp", 1)

    def mix_body(keep_ref, got_ref, out_ref):
        out_ref[...] = (keep_ref[...] + got_ref[...].astype(F32)).astype(BF16)

    (chip,) = call(mix_body, [((2, rows, bins), BF16)], (keep, got), "mix_sum")
    other = swap(chip, "mp", 2)

    def middle_body(x0, x2, chip_ref, other_ref, out_ref):
        for i, ref in enumerate((x0, x2)):
            mixed = chip_ref[i].astype(F32) + other_ref[1 - i].astype(F32)
            out_ref[i] = (ref[...].astype(F32) + mixed).astype(BF16)

    (mid,) = call(
        middle_body, [((2, rows, bins), BF16)], (x_own, x_far, chip, other), "middle"
    )
    mid_near = swap(mid, "mp", 1)

    def own_block_body(a_ref, g_ref, k_ref, p_ref, z_ref, u_ref, gv_ref):
        m = lax.axis_index("mp")
        parts = (a_ref.at[0], a_ref.at[1])
        u_ref[...] = conv(parts, (0, 2), m, k_ref, z_ref, None)
        gv = dot(p_ref[:, block(m, 0)], g_ref[0])
        gv_ref[...] = gv + dot(p_ref[:, block(m, 2)], g_ref[1])

    z_b, u_b, gv_b = call(
        own_block_body,
        [stack, (inner, F32), (inner, F32)],
        (mid, g_pair, tap_b, cols_b),
        "own_block",
    )

    def second_body(
        b_ref, g_ref, k_ref, p_ref, u_ref, gv_ref, zin_ref, z_ref, v_ref, gu_ref, send_ref
    ):
        m = lax.axis_index("mp")
        u = conv((b_ref.at[0], b_ref.at[1]), (1, 3), m, k_ref, z_ref, u_ref[...])
        v, slope = gelu_and_slope(u)
        v_ref[...] = v.astype(BF16)
        gv = gv_ref[...] + dot(p_ref[:, block(m, 1)], g_ref[0])
        gv = gv + dot(p_ref[:, block(m, 3)], g_ref[1])
        gu = (gv * slope).astype(BF16)
        gu_ref[...] = gu
        near_half(k_ref, gu, m, send_ref)

    z_b, v_b, gu_b, send = call(
        second_body,
        [stack, (inner, BF16), (inner, BF16), ((2, rows, bins), BF16)],
        (mid_near, g_near, tap_b, cols_b, u_b, gv_b, z_b),
        "second_block",
        alias={6: 0},
    )
    keep = kept(tap_b, gu_b, "squash_keep")

    def output_body(p_ref, v_ref, keep_ref, send_ref):
        m = lax.axis_index("mp")
        near_half(p_ref, v_ref[...], m, send_ref)
        own_half(p_ref, v_ref[...], m, keep_ref)

    def place(k):
        return lax.axis_index("mp") ^ lax.axis_index("ctx") ^ k

    def taps_pieces(z_ref, gu_ref, keep, send):
        for i in (0, 1):
            send[i] = dot(gu_ref[...], z_ref[place(1 + 2 * i)], ((1,), (1,))).astype(BF16)
        for i in (0, 1):
            keep[i] = dot(gu_ref[...], z_ref[place(2 * i)], ((1,), (1,)))

    def proj_pieces(v_ref, g_ref, keep, send):
        for i in (0, 1):
            send[i] = dot(v_ref[...], g_ref[place(2 + i)], ((1,), (1,))).astype(BF16)
        for i in (0, 1):
            keep[i] = dot(v_ref[...], g_ref[place(i)], ((1,), (1,)))

    one, two, three = ((n, hid, rows) for n in (1, 2, 3))

    def second_weight_body(z_ref, gu_ref, v_ref, ga_ref, gb_ref, *rest):
        keep_k, keep_p, send_k, send_p, g_ref = rest
        for i in range(4):
            g_ref[i] = (ga_ref, gb_ref)[i & 1][i >> 1]
        proj_pieces(v_ref, g_ref, keep_p, send_p)
        taps_pieces(z_ref, gu_ref, keep_k, send_k)

    def half_sum(keep, got, own):
        own[0] = keep[0] + got[0].astype(F32)
        return (keep[1] + got[1].astype(F32)).astype(BF16)

    def first_proj_body(v_ref, g0, g1, g2, g3, keep_b, got_b, keep, send, own, g_ref):
        for i, ref in enumerate((g0, g1, g2, g3)):
            g_ref[i] = ref[...]
        send[2] = half_sum(keep_b, got_b, own)
        proj_pieces(v_ref, g_ref, keep, send)

    def first_taps_body(z_ref, gu_ref, keep_b, got_b, keep, send, own):
        send[2] = half_sum(keep_b, got_b, own)
        taps_pieces(z_ref, gu_ref, keep, send)

    def half_body(keep, got, *rest):
        own, send = rest[-2:]
        send[...] = half_sum(keep, got, own)

    plane = ((3, hid, rows), F32)
    hbm = pl.BlockSpec(memory_space=pltpu.HBM)

    def zero_body(*refs):
        outs, (zero, sems) = refs[:2], refs[2:]
        zero[...] = jnp.zeros((hid, rows), F32)
        copies = [
            pltpu.make_async_copy(zero, out.at[tap], sems.at[2 * i + tap // 2])
            for i, out in enumerate(outs)
            for tap in (0, 2)
        ]
        for copy in copies:
            copy.start()
        for copy in copies:
            copy.wait()

    def total_body(place, _, own_k, own_p, got_k, got_p, taps_ref, proj_ref, k, p, sems):
        k[...] = own_k[0] + got_k[place].astype(F32)
        first = pltpu.make_async_copy(k, taps_ref.at[1], sems.at[0])
        first.start()
        p[...] = own_p[0] + got_p[place].astype(F32)
        second = pltpu.make_async_copy(p, proj_ref, sems.at[1])
        second.start()
        first.wait()
        second.wait()

    def total(place, planes, own_k, own_p, got_k, got_p, name):
        taps, proj = pl.pallas_call(
            functools.partial(total_body, place),
            out_shape=[jax.ShapeDtypeStruct(*plane), jax.ShapeDtypeStruct((hid, rows), F32)],
            in_specs=[hbm] + [VMEM] * 4,
            out_specs=[hbm, hbm],
            scratch_shapes=[pltpu.VMEM((hid, rows), F32)] * 2 + [pltpu.SemaphoreType.DMA((2,))],
            input_output_aliases={0: 0},
            compiler_params=pltpu.CompilerParams(vmem_limit_bytes=16 << 20),
            name=name,
        )(
            pltpu.with_memory_space_constraint(planes, pltpu.HBM),
            *[
                pltpu.with_memory_space_constraint(a, pltpu.VMEM)
                for a in (own_k, own_p, got_k, got_p)
            ],
        )
        return taps, proj.T

    planes = pl.pallas_call(
        zero_body,
        out_shape=[pltpu.HBM(*plane)] * 2,
        in_specs=[],
        out_specs=[hbm, hbm],
        scratch_shapes=[pltpu.VMEM((hid, rows), F32), pltpu.SemaphoreType.DMA((4,))],
        compiler_params=pltpu.CompilerParams(vmem_limit_bytes=16 << 20),
        name="zero_planes",
    )()

    pack = [pltpu.VMEM((4, rows, bins), BF16)]
    *keep_b, send_k, send_p = call(
        second_weight_body,
        [(two, F32), (two, F32), (two, BF16), (two, BF16)],
        (z_b, gu_b, v_b, g_pair, g_near),
        "second_weights",
        pack,
    )
    got = swap(send, "mp", 1)

    def squash_body(keep_ref, got_ref, _, out_ref):
        mix_body(keep_ref, got_ref, out_ref)

    (chip,) = call(squash_body, [((2, rows, bins), BF16)], (keep, got, keep_b[0]), "squash_sum")
    other = swap(chip, "mp", 2)
    got_b = swap(send_k, "ctx", 1), swap(send_p, "ctx", 2)

    def back_body(g_ref, mid_ref, chip_ref, other_ref, *outs):
        for i in (0, 1):
            grad = chip_ref[i].astype(F32) + other_ref[1 - i].astype(F32)
            outs[i][...] = (
                g_ref[i].astype(F32) + grad * slope_of(mid_ref[i].astype(F32))
            ).astype(BF16)

    g_mid = call(
        back_body, [((rows, bins), BF16)] * 2, (g_pair, mid, chip, other), "middle_grad"
    )
    g_mid = [g_mid[0], swap(g_mid[0], "mp", 1), g_mid[1], swap(g_mid[1], "mp", 1)]

    ykeep, ysend = call(
        output_body,
        [((2, rows, bins), F32), ((2, rows, bins), BF16)],
        (cols_b, v_b),
        "output_product",
    )
    ygot = swap(ysend, "mp", 1)

    def last_sum_body(keep_ref, got_ref, *rest):
        own_ref, send_ref = rest[-2:]
        own_ref[...] = keep_ref[0] + got_ref[0].astype(F32)
        send_ref[...] = (keep_ref[1] + got_ref[1].astype(F32)).astype(BF16)

    def last_sum(keep, got, name, after=()):
        outs = [((rows, bins), F32), ((rows, bins), BF16)]
        return call(last_sum_body, outs, (keep, got, *after), name)

    y_own, y_send = last_sum(ykeep, ygot, "out_sum")
    y_got = swap(y_send, "mp", 2)

    def out_body(mid_ref, own_ref, got_ref, out_ref):
        mixed = own_ref[...] + got_ref[...].astype(F32)
        out_ref[...] = (mid_ref[0].astype(F32) + mixed).astype(BF16)

    (second_out,) = call(out_body, [((rows, bins), BF16)], (mid, y_own, y_got), "out", final=True)

    def first_back_body(*refs):
        grads, (k_ref, p_ref, s_ref, gu_ref, send_ref) = refs[:4], refs[4:]
        m = lax.axis_index("mp")
        gv = jnp.zeros((hid, bins), F32)
        for j in range(4):
            gv = gv + dot(p_ref[:, block(m, j)], grads[j][...])
        gu = (gv * s_ref[...]).astype(BF16)
        gu_ref[...] = gu
        near_half(k_ref, gu, m, send_ref)

    gu_a, send = call(
        first_back_body,
        [(inner, BF16), ((2, rows, bins), BF16)],
        (*g_mid, tap_a, cols_a, slope_a),
        "first_backward",
    )
    keep = kept(tap_a, gu_a, "entry_keep")
    keep_ap, send_p, own_bk = call(
        first_proj_body,
        [(two, F32), (three, BF16), (one, F32)],
        (v_a, *g_mid, keep_b[0], got_b[0]),
        "first_proj",
        pack,
    )
    got_p = swap(send_p, "ctx", 2)
    keep_ak, send_k, own_bp = call(
        first_taps_body,
        [(two, F32), (three, BF16), (one, F32)],
        (z_a, gu_a, keep_b[1], got_b[1]),
        "first_taps",
    )
    got_k = swap(send_k, "ctx", 1)
    got = swap(send, "mp", 1)
    e_own, e_send = last_sum(keep, got, "entry_sum")
    e_got = swap(e_send, "mp", 2)

    def entry_body(g_ref, x_ref, own_ref, got_ref, out_ref):
        grad = own_ref[...] + got_ref[...].astype(F32)
        out_ref[...] = (
            g_ref[...].astype(F32) + grad * slope_of(x_ref[...].astype(F32))
        ).astype(BF16)

    (entry,) = call(entry_body, [((rows, bins), BF16)], (g_mid[0], x_own, e_own, e_got), "entry", final=True)

    half = [(one, F32), (one[1:], BF16)]
    own_ap, send_p = call(half_body, half, (keep_ap, got_p), "proj_half")
    last_p = swap(send_p, "ctx", 1)
    own_ak, send_k = call(half_body, half, (keep_ak, got_k, own_ap), "taps_half")
    last_k = swap(send_k, "ctx", 2)
    taps_b_grad, point_b_grad = total(2, planes[0], own_bk, own_bp, got_p, got_k, "second_total")
    taps_a_grad, point_a_grad = total(Ellipsis, planes[1], own_ak, own_ap, last_k, last_p, "first_total")
    return second_out, entry, taps_a_grad, point_a_grad, taps_b_grad, point_b_grad


def solution(mesh):
    sizes = dict(mesh.shape)

    def shards(x, *rest):
        span = x.shape[1] * sizes["ctx"]
        fast = (
            min(FIRST_DILATION, SECOND_DILATION) >= span
            and sizes["mp"] == 4
            and sizes["ctx"] == 4
        )
        return (fast_shards if fast else general_shards)(x, *rest)

    return jax.shard_map(
        shards,
        mesh=mesh,
        in_specs=(
            P("mp", ("groups", "ctx")),
            P(None, "mp", None),
            P(None, "mp"),
            P(None, "mp", None),
            P(None, "mp"),
            P("mp", "ctx", "groups"),
        ),
        out_specs=(
            P("mp", ("groups", "ctx")),
            P("mp", ("groups", "ctx")),
            P("groups", "mp", "ctx"),
            P(("groups", "ctx"), "mp"),
            P("groups", "mp", "ctx"),
            P(("groups", "ctx"), "mp"),
        ),
        check_vma=False,
    )
```

```python
import functools

import jax
import jax.numpy as jnp
from jax import lax
from jax.experimental import pallas as pl
from jax.experimental.pallas import tpu as pltpu
from jax.sharding import PartitionSpec as P

FIRST_DILATION = 1024
SECOND_DILATION = 2048
F32 = jnp.float32
BF16 = jnp.bfloat16
ROOT = 0.7978845608028654
CUBIC = 0.044715


def shifted(value, axis, by):
    length = lax.axis_size(axis)
    pairs = [(i, i + by) for i in range(length) if 0 <= i + by < length]
    return lax.ppermute(value, axis, pairs)


def gelu_slope(values):
    return jax.jvp(jax.nn.gelu, (values,), (jnp.ones_like(values),))[1]


def contract_first(left, right):
    return lax.dot_general(
        left, right, (((0,), (0,)), ((), ())), preferred_element_type=jnp.float32
    )


def contract_last(left, right):
    return lax.dot_general(
        left, right, (((1,), (1,)), ((), ())), preferred_element_type=jnp.float32
    )


def hop_steps(activations, dilation):
    return dilation // activations.shape[1]


def residual_block_forward(activations, conv_weight, point_weight, dilation):
    hop_count = hop_steps(activations, dilation)
    squash_part = jax.nn.gelu(activations.astype(jnp.float32)).astype(jnp.bfloat16)
    squashed = lax.all_gather(squash_part, "mp", axis=0, tiled=True)
    earlier = shifted(squashed, "ctx", hop_count)
    later = shifted(squashed, "ctx", -hop_count)
    pre_act = jnp.dot(conv_weight[0], earlier, preferred_element_type=jnp.float32)
    pre_act = pre_act + jnp.dot(conv_weight[1], squashed, preferred_element_type=jnp.float32)
    pre_act = pre_act + jnp.dot(conv_weight[2], later, preferred_element_type=jnp.float32)
    hidden = jax.nn.gelu(pre_act).astype(jnp.bfloat16)
    mixed = lax.psum_scatter(
        jnp.dot(point_weight, hidden, preferred_element_type=jnp.float32).astype(jnp.bfloat16),
        "mp",
        scatter_dimension=0,
        tiled=True,
    ).astype(jnp.float32)
    result = (activations.astype(jnp.float32) + mixed).astype(jnp.bfloat16)
    return (result, squashed, pre_act, hidden)


def residual_block_backward(
    incoming_gradient, activations, squashed, pre_act, hidden, conv_weight, point_weight, dilation
):
    hop_count = hop_steps(activations, dilation)
    upstream_full = lax.all_gather(incoming_gradient, "mp", axis=0, tiled=True)
    grad_hidden = contract_first(point_weight, upstream_full)
    grad_pre = (grad_hidden * gelu_slope(pre_act)).astype(jnp.bfloat16)
    grad_later = shifted(grad_pre, "ctx", -hop_count)
    grad_earlier = shifted(grad_pre, "ctx", hop_count)
    moved = (grad_later, grad_pre, grad_earlier)
    grad_conv = jnp.stack([contract_last(part, squashed) for part in moved])
    grad_point = contract_last(upstream_full, hidden)
    total = contract_first(conv_weight[0], moved[0])
    total = total + contract_first(conv_weight[1], moved[1])
    grad_squash = lax.psum_scatter(
        (total + contract_first(conv_weight[2], moved[2])).astype(jnp.bfloat16),
        "mp",
        scatter_dimension=0,
        tiled=True,
    ).astype(jnp.float32)
    previous = (
        incoming_gradient.astype(jnp.float32)
        + grad_squash * gelu_slope(activations.astype(jnp.float32))
    ).astype(jnp.bfloat16)
    return (previous, grad_conv, grad_point)


def reduce_block(grad_conv, grad_point):
    return (
        lax.psum_scatter(
            grad_conv.astype(jnp.bfloat16), "ctx", scatter_dimension=2, tiled=True
        ).astype(jnp.float32),
        lax.psum_scatter(
            grad_point.astype(jnp.bfloat16), "ctx", scatter_dimension=0, tiled=True
        ).astype(jnp.float32),
    )


def general_shards(x, taps_a, point_a, taps_b, point_b, grad_heads):
    regrouped = lax.all_to_all(grad_heads, "ctx", split_axis=2, concat_axis=1, tiled=True)
    gradient = regrouped.reshape(regrouped.shape[0] * regrouped.shape[1], regrouped.shape[2])
    middle, z_a, u_a, v_a = residual_block_forward(x, taps_a, point_a, FIRST_DILATION)
    result, z_b, u_b, v_b = residual_block_forward(middle, taps_b, point_b, SECOND_DILATION)
    gradient, conv_b, proj_b = residual_block_backward(
        gradient, middle, z_b, u_b, v_b, taps_b, point_b, SECOND_DILATION
    )
    conv_b, proj_b = reduce_block(conv_b, proj_b)
    gradient, conv_a, proj_a = residual_block_backward(
        gradient, x, z_a, u_a, v_a, taps_a, point_a, FIRST_DILATION
    )
    conv_a, proj_a = reduce_block(conv_a, proj_a)
    return result, gradient, conv_a, proj_a, conv_b, proj_b


def swap(value, axis, bits):
    size = lax.axis_size(axis)
    return lax.ppermute(value, axis, [(i, i ^ bits) for i in range(size)])


def dot(left, right, dims=((1,), (0,))):
    return lax.dot_general(left, right, (dims, ((), ())), preferred_element_type=F32)


def gelu(s):
    return 0.5 * s * (1.0 + jnp.tanh(ROOT * (s + CUBIC * (s * s * s))))


def gelu_and_slope(s):
    sq = s * s
    t = jnp.tanh(ROOT * (s + CUBIC * (s * sq)))
    half = 0.5 * (1.0 + t)
    slope = half + 0.5 * s * (1.0 - t * t) * (ROOT * (1.0 + 3.0 * CUBIC * sq))
    return s * half, slope


def slope_of(s):
    return gelu_and_slope(s)[1]


VMEM = pl.BlockSpec(memory_space=pltpu.VMEM)


def call(body, outs, args, name, scratch=(), final=False, alias=None):
    struct = jax.ShapeDtypeStruct if final else pltpu.VMEM
    return pl.pallas_call(
        body,
        out_shape=[struct(s, d) for s, d in outs],
        in_specs=[VMEM] * len(args),
        out_specs=[VMEM] * len(outs),
        scratch_shapes=scratch,
        input_output_aliases=alias or {},
        compiler_params=pltpu.CompilerParams(vmem_limit_bytes=16 << 20),
        name=name,
    )(*[pltpu.with_memory_space_constraint(a, pltpu.VMEM) for a in args])


def fast_shards(x, taps_a, point_a, taps_b, point_b, grad_heads):
    rows, bins = x.shape
    hid, chans = taps_a.shape[1], taps_a.shape[2]
    heads, val, _ = grad_heads.shape
    def block(m, j):
        return pl.ds(pl.multiple_of((m ^ j) * rows, rows), rows)

    x_far = swap(x, "mp", 2)
    x_near = swap(x, "mp", 1)

    raw_far = swap(grad_heads, "mp", 2)

    def load_body(x_ref, ta, tb, ca, cb, g_ref, *rest):
        outs, sems = rest[:-1], rest[-1]
        sources = [x_ref, ta.at[1], tb.at[1], ca, cb, g_ref]
        copies = [
            pltpu.make_async_copy(source, out, sems.at[i])
            for i, (source, out) in enumerate(zip(sources, outs))
        ]
        for copy in copies:
            copy.start()
        for copy in copies:
            copy.wait()

    x_own, tap_a, tap_b, cols_a, cols_b, raw_own = pl.pallas_call(
        load_body,
        out_shape=[pltpu.VMEM((rows, bins), BF16)]
        + [pltpu.VMEM((hid, chans), BF16)] * 4
        + [pltpu.VMEM(grad_heads.shape, BF16)],
        in_specs=[pl.BlockSpec(memory_space=pltpu.HBM)] * 6,
        out_specs=[VMEM] * 6,
        scratch_shapes=[pltpu.SemaphoreType.DMA((6,))],
        compiler_params=pltpu.CompilerParams(vmem_limit_bytes=16 << 20),
        name="load",
    )(
        *[
            pltpu.with_memory_space_constraint(source, pltpu.HBM)
            for source in (x, taps_a, taps_b, point_a.T, point_b.T, grad_heads)
        ]
    )

    def conv(refs, js, m, k_ref, z_ref, u):
        for ref, j in zip(refs, js):
            z = gelu(ref[...].astype(F32)).astype(BF16)
            z_ref[j] = z
            part = dot(k_ref[:, block(m, j)], z)
            u = part if u is None else u + part
        return u

    stack = ((4, rows, bins), BF16)
    inner = (hid, bins)

    def near_forward_body(x0, k_ref, z_ref, u_ref):
        u_ref[...] = conv((x0,), (0,), lax.axis_index("mp"), k_ref, z_ref, None)

    z_a, u_a = call(
        near_forward_body, [stack, (inner, F32)], (x_own, tap_a), "near_forward"
    )
    x_far, u_a = lax.optimization_barrier((x_far, u_a))
    x_cross = swap(x_far, "mp", 1)

    def split_body(own_ref, far_ref, *outs):
        c = lax.axis_index("ctx")
        for k in range(4):
            at = pl.ds(pl.multiple_of((c ^ k) * bins, bins), bins)
            for i, ref in enumerate((own_ref, far_ref)):
                outs[k][i] = ref[:, :, at]

    piece = ((2, heads, val, bins), BF16)
    pieces = call(split_body, [piece] * 4, (raw_own, raw_far), "split_grad")
    pieces = [pieces[0]] + [swap(pieces[k], "ctx", k) for k in (1, 2, 3)]

    def join_body(*refs):
        c = lax.axis_index("ctx")
        out = refs[4]
        for k in range(4):
            out[:, :, c ^ k] = refs[k][...]

    (g_pair,) = call(join_body, [((2, heads, 4, val, bins), BF16)], pieces, "join_grad")
    g_pair = g_pair.reshape(2, rows, bins)
    g_near = swap(g_pair, "mp", 1)

    def near_half(w_ref, v, m, send_ref):
        for i, j in enumerate((1, 3)):
            send_ref[i] = dot(w_ref[:, block(m, j)], v, ((0,), (0,))).astype(BF16)

    def own_half(w_ref, v, m, keep_ref):
        for i, j in enumerate((0, 2)):
            keep_ref[i] = dot(w_ref[:, block(m, j)], v, ((0,), (0,)))

    def keep_body(w_ref, v_ref, keep_ref):
        own_half(w_ref, v_ref[...], lax.axis_index("mp"), keep_ref)

    def kept(w, v, name):
        return call(keep_body, [((2, rows, bins), F32)], (w, v), name)[0]

    def more_forward_body(x1, x2, k_ref, u_in, zin_ref, z_ref, u_ref):
        m = lax.axis_index("mp")
        u_ref[...] = conv((x1, x2), (1, 2), m, k_ref, z_ref, u_in[...])

    z_a, u_a = call(
        more_forward_body,
        [stack, (inner, F32)],
        (x_near, x_far, tap_a, u_a, z_a),
        "more_forward",
        alias={4: 0},
    )

    def first_body(x3, k_ref, p_ref, _, u_ref, zin_ref, z_ref, v_ref, s_ref, send_ref):
        m = lax.axis_index("mp")
        u = conv((x3,), (3,), m, k_ref, z_ref, u_ref[...])
        v, slope = gelu_and_slope(u)
        v = v.astype(BF16)
        v_ref[...] = v
        s_ref[...] = slope
        near_half(p_ref, v, m, send_ref)

    z_a, v_a, slope_a, send = call(
        first_body,
        [stack, (inner, BF16), (inner, F32), ((2, rows, bins), BF16)],
        (x_cross, tap_a, cols_a, raw_far, u_a, z_a),
        "first_forward",
        alias={5: 0},
    )
    keep = kept(cols_a, v_a, "mix_keep")
    got = swap(send, "mp", 1)

    def mix_body(keep_ref, got_ref, out_ref):
        out_ref[...] = (keep_ref[...] + got_ref[...].astype(F32)).astype(BF16)

    (chip,) = call(mix_body, [((2, rows, bins), BF16)], (keep, got), "mix_sum")
    other = swap(chip, "mp", 2)

    def middle_body(x0, x2, chip_ref, other_ref, out_ref):
        for i, ref in enumerate((x0, x2)):
            mixed = chip_ref[i].astype(F32) + other_ref[1 - i].astype(F32)
            out_ref[i] = (ref[...].astype(F32) + mixed).astype(BF16)

    (mid,) = call(
        middle_body, [((2, rows, bins), BF16)], (x_own, x_far, chip, other), "middle"
    )
    mid_near = swap(mid, "mp", 1)

    def own_block_body(a_ref, g_ref, k_ref, p_ref, z_ref, u_ref, gv_ref):
        m = lax.axis_index("mp")
        parts = (a_ref.at[0], a_ref.at[1])
        u_ref[...] = conv(parts, (0, 2), m, k_ref, z_ref, None)
        gv = dot(p_ref[:, block(m, 0)], g_ref[0])
        gv_ref[...] = gv + dot(p_ref[:, block(m, 2)], g_ref[1])

    z_b, u_b, gv_b = call(
        own_block_body,
        [stack, (inner, F32), (inner, F32)],
        (mid, g_pair, tap_b, cols_b),
        "own_block",
    )

    def second_body(
        b_ref, g_ref, k_ref, p_ref, u_ref, gv_ref, zin_ref, z_ref, v_ref, gu_ref, send_ref
    ):
        m = lax.axis_index("mp")
        u = conv((b_ref.at[0], b_ref.at[1]), (1, 3), m, k_ref, z_ref, u_ref[...])
        v, slope = gelu_and_slope(u)
        v_ref[...] = v.astype(BF16)
        gv = gv_ref[...] + dot(p_ref[:, block(m, 1)], g_ref[0])
        gv = gv + dot(p_ref[:, block(m, 3)], g_ref[1])
        gu = (gv * slope).astype(BF16)
        gu_ref[...] = gu
        near_half(k_ref, gu, m, send_ref)

    z_b, v_b, gu_b, send = call(
        second_body,
        [stack, (inner, BF16), (inner, BF16), ((2, rows, bins), BF16)],
        (mid_near, g_near, tap_b, cols_b, u_b, gv_b, z_b),
        "second_block",
        alias={6: 0},
    )
    keep = kept(tap_b, gu_b, "squash_keep")

    def output_body(p_ref, v_ref, keep_ref, send_ref):
        m = lax.axis_index("mp")
        near_half(p_ref, v_ref[...], m, send_ref)
        own_half(p_ref, v_ref[...], m, keep_ref)

    def place(k):
        return lax.axis_index("mp") ^ lax.axis_index("ctx") ^ k

    def taps_pieces(z_ref, gu_ref, keep, send):
        for i in (0, 1):
            send[i] = dot(gu_ref[...], z_ref[place(1 + 2 * i)], ((1,), (1,))).astype(BF16)
        for i in (0, 1):
            keep[i] = dot(gu_ref[...], z_ref[place(2 * i)], ((1,), (1,)))

    def proj_pieces(v_ref, g_ref, keep, send):
        for i in (0, 1):
            send[i] = dot(v_ref[...], g_ref[place(2 + i)], ((1,), (1,))).astype(BF16)
        for i in (0, 1):
            keep[i] = dot(v_ref[...], g_ref[place(i)], ((1,), (1,)))

    one, two, three = ((n, hid, rows) for n in (1, 2, 3))

    def second_weight_body(z_ref, gu_ref, v_ref, ga_ref, gb_ref, *rest):
        keep_k, keep_p, send_k, send_p, g_ref = rest
        for i in range(4):
            g_ref[i] = (ga_ref, gb_ref)[i & 1][i >> 1]
        proj_pieces(v_ref, g_ref, keep_p, send_p)
        taps_pieces(z_ref, gu_ref, keep_k, send_k)

    def half_sum(keep, got, own):
        own[0] = keep[0] + got[0].astype(F32)
        return (keep[1] + got[1].astype(F32)).astype(BF16)

    def first_proj_body(v_ref, g0, g1, g2, g3, keep_b, got_b, keep, send, own, g_ref):
        for i, ref in enumerate((g0, g1, g2, g3)):
            g_ref[i] = ref[...]
        send[2] = half_sum(keep_b, got_b, own)
        proj_pieces(v_ref, g_ref, keep, send)

    def first_taps_body(z_ref, gu_ref, keep_b, got_b, keep, send, own):
        send[2] = half_sum(keep_b, got_b, own)
        taps_pieces(z_ref, gu_ref, keep, send)

    def half_body(keep, got, *rest):
        own, send = rest[-2:]
        send[...] = half_sum(keep, got, own)

    plane = ((3, hid, rows), F32)
    hbm = pl.BlockSpec(memory_space=pltpu.HBM)

    def zero_body(*refs):
        outs, (zero, sems) = refs[:2], refs[2:]
        zero[...] = jnp.zeros((hid, rows), F32)
        copies = [
            pltpu.make_async_copy(zero, out.at[tap], sems.at[2 * i + tap // 2])
            for i, out in enumerate(outs)
            for tap in (0, 2)
        ]
        for copy in copies:
            copy.start()
        for copy in copies:
            copy.wait()

    def total_body(place, _, own_k, own_p, got_k, got_p, taps_ref, proj_ref, k, p, sems):
        k[...] = own_k[0] + got_k[place].astype(F32)
        first = pltpu.make_async_copy(k, taps_ref.at[1], sems.at[0])
        first.start()
        p[...] = own_p[0] + got_p[place].astype(F32)
        second = pltpu.make_async_copy(p, proj_ref, sems.at[1])
        second.start()
        first.wait()
        second.wait()

    def total(place, planes, own_k, own_p, got_k, got_p, name):
        taps, proj = pl.pallas_call(
            functools.partial(total_body, place),
            out_shape=[jax.ShapeDtypeStruct(*plane), jax.ShapeDtypeStruct((hid, rows), F32)],
            in_specs=[hbm] + [VMEM] * 4,
            out_specs=[hbm, hbm],
            scratch_shapes=[pltpu.VMEM((hid, rows), F32)] * 2 + [pltpu.SemaphoreType.DMA((2,))],
            input_output_aliases={0: 0},
            compiler_params=pltpu.CompilerParams(vmem_limit_bytes=16 << 20),
            name=name,
        )(
            pltpu.with_memory_space_constraint(planes, pltpu.HBM),
            *[
                pltpu.with_memory_space_constraint(a, pltpu.VMEM)
                for a in (own_k, own_p, got_k, got_p)
            ],
        )
        return taps, proj.T

    planes = pl.pallas_call(
        zero_body,
        out_shape=[pltpu.HBM(*plane)] * 2,
        in_specs=[],
        out_specs=[hbm, hbm],
        scratch_shapes=[pltpu.VMEM((hid, rows), F32), pltpu.SemaphoreType.DMA((4,))],
        compiler_params=pltpu.CompilerParams(vmem_limit_bytes=16 << 20),
        name="zero_planes",
    )()

    pack = [pltpu.VMEM((4, rows, bins), BF16)]
    *keep_b, send_k, send_p = call(
        second_weight_body,
        [(two, F32), (two, F32), (two, BF16), (two, BF16)],
        (z_b, gu_b, v_b, g_pair, g_near),
        "second_weights",
        pack,
    )
    got = swap(send, "mp", 1)

    def squash_body(keep_ref, got_ref, _, out_ref):
        mix_body(keep_ref, got_ref, out_ref)

    (chip,) = call(squash_body, [((2, rows, bins), BF16)], (keep, got, keep_b[0]), "squash_sum")
    other = swap(chip, "mp", 2)
    got_b = swap(send_k, "ctx", 1), swap(send_p, "ctx", 2)

    def back_body(g_ref, mid_ref, chip_ref, other_ref, *outs):
        for i in (0, 1):
            grad = chip_ref[i].astype(F32) + other_ref[1 - i].astype(F32)
            outs[i][...] = (
                g_ref[i].astype(F32) + grad * slope_of(mid_ref[i].astype(F32))
            ).astype(BF16)

    g_mid = call(
        back_body, [((rows, bins), BF16)] * 2, (g_pair, mid, chip, other), "middle_grad"
    )
    g_mid = [g_mid[0], swap(g_mid[0], "mp", 1), g_mid[1], swap(g_mid[1], "mp", 1)]

    ykeep, ysend = call(
        output_body,
        [((2, rows, bins), F32), ((2, rows, bins), BF16)],
        (cols_b, v_b),
        "output_product",
    )
    ygot = swap(ysend, "mp", 1)

    def last_sum_body(keep_ref, got_ref, *rest):
        own_ref, send_ref = rest[-2:]
        own_ref[...] = keep_ref[0] + got_ref[0].astype(F32)
        send_ref[...] = (keep_ref[1] + got_ref[1].astype(F32)).astype(BF16)

    def last_sum(keep, got, name, after=()):
        outs = [((rows, bins), F32), ((rows, bins), BF16)]
        return call(last_sum_body, outs, (keep, got, *after), name)

    y_own, y_send = last_sum(ykeep, ygot, "out_sum")
    y_got = swap(y_send, "mp", 2)

    def out_body(mid_ref, own_ref, got_ref, out_ref):
        mixed = own_ref[...] + got_ref[...].astype(F32)
        out_ref[...] = (mid_ref[0].astype(F32) + mixed).astype(BF16)

    (second_out,) = call(out_body, [((rows, bins), BF16)], (mid, y_own, y_got), "out", final=True)

    def first_back_body(*refs):
        grads, (k_ref, p_ref, s_ref, gu_ref, send_ref) = refs[:4], refs[4:]
        m = lax.axis_index("mp")
        gv = jnp.zeros((hid, bins), F32)
        for j in range(4):
            gv = gv + dot(p_ref[:, block(m, j)], grads[j][...])
        gu = (gv * s_ref[...]).astype(BF16)
        gu_ref[...] = gu
        near_half(k_ref, gu, m, send_ref)

    gu_a, send = call(
        first_back_body,
        [(inner, BF16), ((2, rows, bins), BF16)],
        (*g_mid, tap_a, cols_a, slope_a),
        "first_backward",
    )
    keep = kept(tap_a, gu_a, "entry_keep")
    keep_ap, send_p, own_bk = call(
        first_proj_body,
        [(two, F32), (three, BF16), (one, F32)],
        (v_a, *g_mid, keep_b[0], got_b[0]),
        "first_proj",
        pack,
    )
    got_p = swap(send_p, "ctx", 2)
    keep_ak, send_k, own_bp = call(
        first_taps_body,
        [(two, F32), (three, BF16), (one, F32)],
        (z_a, gu_a, keep_b[1], got_b[1]),
        "first_taps",
    )
    got_k = swap(send_k, "ctx", 1)
    got = swap(send, "mp", 1)
    e_own, e_send = last_sum(keep, got, "entry_sum")
    e_got = swap(e_send, "mp", 2)

    def entry_body(g_ref, x_ref, own_ref, got_ref, out_ref):
        grad = own_ref[...] + got_ref[...].astype(F32)
        out_ref[...] = (
            g_ref[...].astype(F32) + grad * slope_of(x_ref[...].astype(F32))
        ).astype(BF16)

    (entry,) = call(entry_body, [((rows, bins), BF16)], (g_mid[0], x_own, e_own, e_got), "entry", final=True)

    half = [(one, F32), (one[1:], BF16)]
    own_ap, send_p = call(half_body, half, (keep_ap, got_p), "proj_half")
    last_p = swap(send_p, "ctx", 1)
    own_ak, send_k = call(half_body, half, (keep_ak, got_k, own_ap), "taps_half")
    last_k = swap(send_k, "ctx", 2)
    taps_b_grad, point_b_grad = total(2, planes[0], own_bk, own_bp, got_p, got_k, "second_total")
    taps_a_grad, point_a_grad = total(Ellipsis, planes[1], own_ak, own_ap, last_k, last_p, "first_total")
    return second_out, entry, taps_a_grad, point_a_grad, taps_b_grad, point_b_grad


def solution(mesh):
    sizes = dict(mesh.shape)

    def shards(x, *rest):
        span = x.shape[1] * sizes["ctx"]
        fast = (
            min(FIRST_DILATION, SECOND_DILATION) >= span
            and sizes["mp"] == 4
            and sizes["ctx"] == 4
        )
        return (fast_shards if fast else general_shards)(x, *rest)

    return jax.shard_map(
        shards,
        mesh=mesh,
        in_specs=(
            P("mp", ("groups", "ctx")),
            P(None, "mp", None),
            P(None, "mp"),
            P(None, "mp", None),
            P(None, "mp"),
            P("mp", "ctx", "groups"),
        ),
        out_specs=(
            P("mp", ("groups", "ctx")),
            P("mp", ("groups", "ctx")),
            P("groups", "mp", "ctx"),
            P(("groups", "ctx"), "mp"),
            P("groups", "mp", "ctx"),
            P(("groups", "ctx"), "mp"),
        ),
        check_vma=False,
    )
```

```python
import functools

import jax
import jax.numpy as jnp
from jax import lax
from jax.experimental import pallas as pl
from jax.experimental.pallas import tpu as pltpu
from jax.sharding import PartitionSpec as P

FIRST_DILATION = 1024
SECOND_DILATION = 2048
F32 = jnp.float32
BF16 = jnp.bfloat16
ROOT = 0.7978845608028654
CUBIC = 0.044715


def shifted(value, axis, by):
    length = lax.axis_size(axis)
    pairs = [(i, i + by) for i in range(length) if 0 <= i + by < length]
    return lax.ppermute(value, axis, pairs)


def gelu_slope(values):
    return jax.jvp(jax.nn.gelu, (values,), (jnp.ones_like(values),))[1]


def contract_first(left, right):
    return lax.dot_general(
        left, right, (((0,), (0,)), ((), ())), preferred_element_type=jnp.float32
    )


def contract_last(left, right):
    return lax.dot_general(
        left, right, (((1,), (1,)), ((), ())), preferred_element_type=jnp.float32
    )


def hop_steps(activations, dilation):
    return dilation // activations.shape[1]


def residual_block_forward(activations, conv_weight, point_weight, dilation):
    hop_count = hop_steps(activations, dilation)
    squash_part = jax.nn.gelu(activations.astype(jnp.float32)).astype(jnp.bfloat16)
    squashed = lax.all_gather(squash_part, "mp", axis=0, tiled=True)
    earlier = shifted(squashed, "ctx", hop_count)
    later = shifted(squashed, "ctx", -hop_count)
    pre_act = jnp.dot(conv_weight[0], earlier, preferred_element_type=jnp.float32)
    pre_act = pre_act + jnp.dot(conv_weight[1], squashed, preferred_element_type=jnp.float32)
    pre_act = pre_act + jnp.dot(conv_weight[2], later, preferred_element_type=jnp.float32)
    hidden = jax.nn.gelu(pre_act).astype(jnp.bfloat16)
    mixed = lax.psum_scatter(
        jnp.dot(point_weight, hidden, preferred_element_type=jnp.float32).astype(jnp.bfloat16),
        "mp",
        scatter_dimension=0,
        tiled=True,
    ).astype(jnp.float32)
    result = (activations.astype(jnp.float32) + mixed).astype(jnp.bfloat16)
    return (result, squashed, pre_act, hidden)


def residual_block_backward(
    incoming_gradient, activations, squashed, pre_act, hidden, conv_weight, point_weight, dilation
):
    hop_count = hop_steps(activations, dilation)
    upstream_full = lax.all_gather(incoming_gradient, "mp", axis=0, tiled=True)
    grad_hidden = contract_first(point_weight, upstream_full)
    grad_pre = (grad_hidden * gelu_slope(pre_act)).astype(jnp.bfloat16)
    grad_later = shifted(grad_pre, "ctx", -hop_count)
    grad_earlier = shifted(grad_pre, "ctx", hop_count)
    moved = (grad_later, grad_pre, grad_earlier)
    grad_conv = jnp.stack([contract_last(part, squashed) for part in moved])
    grad_point = contract_last(upstream_full, hidden)
    total = contract_first(conv_weight[0], moved[0])
    total = total + contract_first(conv_weight[1], moved[1])
    grad_squash = lax.psum_scatter(
        (total + contract_first(conv_weight[2], moved[2])).astype(jnp.bfloat16),
        "mp",
        scatter_dimension=0,
        tiled=True,
    ).astype(jnp.float32)
    previous = (
        incoming_gradient.astype(jnp.float32)
        + grad_squash * gelu_slope(activations.astype(jnp.float32))
    ).astype(jnp.bfloat16)
    return (previous, grad_conv, grad_point)


def reduce_block(grad_conv, grad_point):
    return (
        lax.psum_scatter(
            grad_conv.astype(jnp.bfloat16), "ctx", scatter_dimension=2, tiled=True
        ).astype(jnp.float32),
        lax.psum_scatter(
            grad_point.astype(jnp.bfloat16), "ctx", scatter_dimension=0, tiled=True
        ).astype(jnp.float32),
    )


def general_shards(x, taps_a, point_a, taps_b, point_b, grad_heads):
    regrouped = lax.all_to_all(grad_heads, "ctx", split_axis=2, concat_axis=1, tiled=True)
    gradient = regrouped.reshape(regrouped.shape[0] * regrouped.shape[1], regrouped.shape[2])
    middle, z_a, u_a, v_a = residual_block_forward(x, taps_a, point_a, FIRST_DILATION)
    result, z_b, u_b, v_b = residual_block_forward(middle, taps_b, point_b, SECOND_DILATION)
    gradient, conv_b, proj_b = residual_block_backward(
        gradient, middle, z_b, u_b, v_b, taps_b, point_b, SECOND_DILATION
    )
    conv_b, proj_b = reduce_block(conv_b, proj_b)
    gradient, conv_a, proj_a = residual_block_backward(
        gradient, x, z_a, u_a, v_a, taps_a, point_a, FIRST_DILATION
    )
    conv_a, proj_a = reduce_block(conv_a, proj_a)
    return result, gradient, conv_a, proj_a, conv_b, proj_b


def swap(value, axis, bits):
    size = lax.axis_size(axis)
    return lax.ppermute(value, axis, [(i, i ^ bits) for i in range(size)])


def dot(left, right, dims=((1,), (0,))):
    return lax.dot_general(left, right, (dims, ((), ())), preferred_element_type=F32)


def gelu(s):
    return 0.5 * s * (1.0 + jnp.tanh(ROOT * (s + CUBIC * (s * s * s))))


def gelu_and_slope(s):
    sq = s * s
    t = jnp.tanh(ROOT * (s + CUBIC * (s * sq)))
    half = 0.5 * (1.0 + t)
    slope = half + 0.5 * s * (1.0 - t * t) * (ROOT * (1.0 + 3.0 * CUBIC * sq))
    return s * half, slope


def slope_of(s):
    return gelu_and_slope(s)[1]


VMEM = pl.BlockSpec(memory_space=pltpu.VMEM)


def call(body, outs, args, name, scratch=(), final=False, alias=None):
    struct = jax.ShapeDtypeStruct if final else pltpu.VMEM
    return pl.pallas_call(
        body,
        out_shape=[struct(s, d) for s, d in outs],
        in_specs=[VMEM] * len(args),
        out_specs=[VMEM] * len(outs),
        scratch_shapes=scratch,
        input_output_aliases=alias or {},
        compiler_params=pltpu.CompilerParams(vmem_limit_bytes=16 << 20),
        name=name,
    )(*[pltpu.with_memory_space_constraint(a, pltpu.VMEM) for a in args])


def fast_shards(x, taps_a, point_a, taps_b, point_b, grad_heads):
    rows, bins = x.shape
    hid, chans = taps_a.shape[1], taps_a.shape[2]
    heads, val, _ = grad_heads.shape
    def block(m, j):
        return pl.ds(pl.multiple_of((m ^ j) * rows, rows), rows)

    x_far = swap(x, "mp", 2)

    raw_far = swap(grad_heads, "mp", 2)

    def load_body(x_ref, ta, tb, ca, cb, g_ref, *rest):
        outs, sems = rest[:-1], rest[-1]
        sources = [x_ref, ta.at[1], tb.at[1], ca, cb, g_ref]
        copies = [
            pltpu.make_async_copy(source, out, sems.at[i])
            for i, (source, out) in enumerate(zip(sources, outs))
        ]
        for copy in copies:
            copy.start()
        for copy in copies:
            copy.wait()

    x_own, tap_a, tap_b, cols_a, cols_b, raw_own = pl.pallas_call(
        load_body,
        out_shape=[pltpu.VMEM((rows, bins), BF16)]
        + [pltpu.VMEM((hid, chans), BF16)] * 4
        + [pltpu.VMEM(grad_heads.shape, BF16)],
        in_specs=[pl.BlockSpec(memory_space=pltpu.HBM)] * 6,
        out_specs=[VMEM] * 6,
        scratch_shapes=[pltpu.SemaphoreType.DMA((6,))],
        compiler_params=pltpu.CompilerParams(vmem_limit_bytes=16 << 20),
        name="load",
    )(
        *[
            pltpu.with_memory_space_constraint(source, pltpu.HBM)
            for source in (x, taps_a, taps_b, point_a.T, point_b.T, grad_heads)
        ]
    )

    def conv(refs, js, m, k_ref, z_ref, u):
        for ref, j in zip(refs, js):
            z = gelu(ref[...].astype(F32)).astype(BF16)
            z_ref[j] = z
            part = dot(k_ref[:, block(m, j)], z)
            u = part if u is None else u + part
        return u

    stack = ((4, rows, bins), BF16)
    inner = (hid, bins)

    def near_forward_body(x_ref, k_ref, z_ref, u_ref):
        z = gelu(x_ref[...].astype(F32)).astype(BF16)
        z_ref[...] = z
        u_ref[...] = dot(k_ref[:, block(lax.axis_index("mp"), 0)], z)

    def far_forward_body(x_ref, k_ref, u_in, z_ref, u_ref):
        z = gelu(x_ref[...].astype(F32)).astype(BF16)
        z_ref[...] = z
        u_ref[...] = u_in[...] + dot(k_ref[:, block(lax.axis_index("mp"), 2)], z)

    half_z = [((rows, bins), BF16), (inner, F32)]
    z_own, u_a = call(near_forward_body, half_z, (x_own, tap_a), "near_forward")
    x_far, u_a = lax.optimization_barrier((x_far, u_a))
    z_far, u_a = call(far_forward_body, half_z, (x_far, tap_a, u_a), "far_forward")
    z_near, z_cross = swap(z_own, "mp", 1), swap(z_far, "mp", 1)

    def split_body(own_ref, far_ref, *outs):
        c = lax.axis_index("ctx")
        for k in range(4):
            at = pl.ds(pl.multiple_of((c ^ k) * bins, bins), bins)
            for i, ref in enumerate((own_ref, far_ref)):
                outs[k][i] = ref[:, :, at]

    piece = ((2, heads, val, bins), BF16)
    pieces = call(split_body, [piece] * 4, (raw_own, raw_far), "split_grad")
    pieces = [pieces[0]] + [swap(pieces[k], "ctx", k) for k in (1, 2, 3)]

    def join_body(*refs):
        c = lax.axis_index("ctx")
        out = refs[4]
        for k in range(4):
            out[:, :, c ^ k] = refs[k][...]

    (g_pair,) = call(join_body, [((2, heads, 4, val, bins), BF16)], pieces, "join_grad")
    g_pair = g_pair.reshape(2, rows, bins)
    g_near = swap(g_pair, "mp", 1)

    def near_half(w_ref, v, m, send_ref):
        for i, j in enumerate((1, 3)):
            send_ref[i] = dot(w_ref[:, block(m, j)], v, ((0,), (0,))).astype(BF16)

    def own_half(w_ref, v, m, keep_ref):
        for i, j in enumerate((0, 2)):
            keep_ref[i] = dot(w_ref[:, block(m, j)], v, ((0,), (0,)))

    def keep_body(w_ref, v_ref, keep_ref):
        own_half(w_ref, v_ref[...], lax.axis_index("mp"), keep_ref)

    def kept(w, v, name):
        return call(keep_body, [((2, rows, bins), F32)], (w, v), name)[0]

    def first_body(z1, z3, k_ref, p_ref, _, u_ref, v_ref, s_ref, send_ref):
        m = lax.axis_index("mp")
        u = u_ref[...] + dot(k_ref[:, block(m, 1)], z1[...])
        u = u + dot(k_ref[:, block(m, 3)], z3[...])
        v, slope = gelu_and_slope(u)
        v = v.astype(BF16)
        v_ref[...] = v
        s_ref[...] = slope
        near_half(p_ref, v, m, send_ref)

    v_a, slope_a, send = call(
        first_body,
        [(inner, BF16), (inner, F32), ((2, rows, bins), BF16)],
        (z_near, z_cross, tap_a, cols_a, raw_far, u_a),
        "first_forward",
    )
    keep = kept(cols_a, v_a, "mix_keep")
    got = swap(send, "mp", 1)

    def mix_body(keep_ref, got_ref, out_ref):
        out_ref[...] = (keep_ref[...] + got_ref[...].astype(F32)).astype(BF16)

    (chip,) = call(mix_body, [((2, rows, bins), BF16)], (keep, got), "mix_sum")
    other = swap(chip, "mp", 2)

    def middle_body(x0, x2, chip_ref, other_ref, out_ref):
        for i, ref in enumerate((x0, x2)):
            mixed = chip_ref[i].astype(F32) + other_ref[1 - i].astype(F32)
            out_ref[i] = (ref[...].astype(F32) + mixed).astype(BF16)

    (mid,) = call(
        middle_body, [((2, rows, bins), BF16)], (x_own, x_far, chip, other), "middle"
    )
    mid_near = swap(mid, "mp", 1)

    def own_block_body(a_ref, g_ref, k_ref, p_ref, z_ref, u_ref, gv_ref):
        m = lax.axis_index("mp")
        parts = (a_ref.at[0], a_ref.at[1])
        u_ref[...] = conv(parts, (0, 2), m, k_ref, z_ref, None)
        gv = dot(p_ref[:, block(m, 0)], g_ref[0])
        gv_ref[...] = gv + dot(p_ref[:, block(m, 2)], g_ref[1])

    z_b, u_b, gv_b = call(
        own_block_body,
        [stack, (inner, F32), (inner, F32)],
        (mid, g_pair, tap_b, cols_b),
        "own_block",
    )

    def second_body(
        b_ref, g_ref, k_ref, p_ref, u_ref, gv_ref, zin_ref, z_ref, v_ref, gu_ref, send_ref
    ):
        m = lax.axis_index("mp")
        u = conv((b_ref.at[0], b_ref.at[1]), (1, 3), m, k_ref, z_ref, u_ref[...])
        v, slope = gelu_and_slope(u)
        v_ref[...] = v.astype(BF16)
        gv = gv_ref[...] + dot(p_ref[:, block(m, 1)], g_ref[0])
        gv = gv + dot(p_ref[:, block(m, 3)], g_ref[1])
        gu = (gv * slope).astype(BF16)
        gu_ref[...] = gu
        near_half(k_ref, gu, m, send_ref)

    z_b, v_b, gu_b, send = call(
        second_body,
        [stack, (inner, BF16), (inner, BF16), ((2, rows, bins), BF16)],
        (mid_near, g_near, tap_b, cols_b, u_b, gv_b, z_b),
        "second_block",
        alias={6: 0},
    )
    keep = kept(tap_b, gu_b, "squash_keep")

    def output_body(p_ref, v_ref, keep_ref, send_ref):
        m = lax.axis_index("mp")
        near_half(p_ref, v_ref[...], m, send_ref)
        own_half(p_ref, v_ref[...], m, keep_ref)

    def place(k):
        return lax.axis_index("mp") ^ lax.axis_index("ctx") ^ k

    def taps_pieces(z_ref, gu_ref, keep, send):
        for i in (0, 1):
            send[i] = dot(gu_ref[...], z_ref[place(1 + 2 * i)], ((1,), (1,))).astype(BF16)
        for i in (0, 1):
            keep[i] = dot(gu_ref[...], z_ref[place(2 * i)], ((1,), (1,)))

    def proj_pieces(v_ref, g_ref, keep, send):
        for i in (0, 1):
            send[i] = dot(v_ref[...], g_ref[place(2 + i)], ((1,), (1,))).astype(BF16)
        for i in (0, 1):
            keep[i] = dot(v_ref[...], g_ref[place(i)], ((1,), (1,)))

    one, two, three = ((n, hid, rows) for n in (1, 2, 3))

    def second_weight_body(z_ref, gu_ref, v_ref, ga_ref, gb_ref, *rest):
        keep_k, keep_p, send_k, send_p, g_ref = rest
        for i in range(4):
            g_ref[i] = (ga_ref, gb_ref)[i & 1][i >> 1]
        proj_pieces(v_ref, g_ref, keep_p, send_p)
        taps_pieces(z_ref, gu_ref, keep_k, send_k)

    def half_sum(keep, got, own):
        own[0] = keep[0] + got[0].astype(F32)
        return (keep[1] + got[1].astype(F32)).astype(BF16)

    def first_proj_body(v_ref, g0, g1, g2, g3, keep_b, got_b, keep, send, own, g_ref):
        for i, ref in enumerate((g0, g1, g2, g3)):
            g_ref[i] = ref[...]
        send[2] = half_sum(keep_b, got_b, own)
        proj_pieces(v_ref, g_ref, keep, send)

    def first_taps_body(z0, z1, z2, z3, gu_ref, keep_b, got_b, keep, send, own, z_ref):
        for i, ref in enumerate((z0, z1, z2, z3)):
            z_ref[i] = ref[...]
        send[2] = half_sum(keep_b, got_b, own)
        taps_pieces(z_ref, gu_ref, keep, send)

    def half_body(keep, got, *rest):
        own, send = rest[-2:]
        send[...] = half_sum(keep, got, own)

    plane = ((3, hid, rows), F32)
    hbm = pl.BlockSpec(memory_space=pltpu.HBM)

    def zero_body(*refs):
        outs, (zero, sems) = refs[:2], refs[2:]
        zero[...] = jnp.zeros((hid, rows), F32)
        copies = [
            pltpu.make_async_copy(zero, out.at[tap], sems.at[2 * i + tap // 2])
            for i, out in enumerate(outs)
            for tap in (0, 2)
        ]
        for copy in copies:
            copy.start()
        for copy in copies:
            copy.wait()

    def total_body(place, _, own_k, own_p, got_k, got_p, taps_ref, proj_ref, k, p, sems):
        k[...] = own_k[0] + got_k[place].astype(F32)
        first = pltpu.make_async_copy(k, taps_ref.at[1], sems.at[0])
        first.start()
        p[...] = own_p[0] + got_p[place].astype(F32)
        second = pltpu.make_async_copy(p, proj_ref, sems.at[1])
        second.start()
        first.wait()
        second.wait()

    def total(place, planes, own_k, own_p, got_k, got_p, name):
        taps, proj = pl.pallas_call(
            functools.partial(total_body, place),
            out_shape=[jax.ShapeDtypeStruct(*plane), jax.ShapeDtypeStruct((hid, rows), F32)],
            in_specs=[hbm] + [VMEM] * 4,
            out_specs=[hbm, hbm],
            scratch_shapes=[pltpu.VMEM((hid, rows), F32)] * 2 + [pltpu.SemaphoreType.DMA((2,))],
            input_output_aliases={0: 0},
            compiler_params=pltpu.CompilerParams(vmem_limit_bytes=16 << 20),
            name=name,
        )(
            pltpu.with_memory_space_constraint(planes, pltpu.HBM),
            *[
                pltpu.with_memory_space_constraint(a, pltpu.VMEM)
                for a in (own_k, own_p, got_k, got_p)
            ],
        )
        return taps, proj.T

    planes = pl.pallas_call(
        zero_body,
        out_shape=[pltpu.HBM(*plane)] * 2,
        in_specs=[],
        out_specs=[hbm, hbm],
        scratch_shapes=[pltpu.VMEM((hid, rows), F32), pltpu.SemaphoreType.DMA((4,))],
        compiler_params=pltpu.CompilerParams(vmem_limit_bytes=16 << 20),
        name="zero_planes",
    )()

    pack = [pltpu.VMEM((4, rows, bins), BF16)]
    *keep_b, send_k, send_p = call(
        second_weight_body,
        [(two, F32), (two, F32), (two, BF16), (two, BF16)],
        (z_b, gu_b, v_b, g_pair, g_near),
        "second_weights",
        pack,
    )
    got = swap(send, "mp", 1)

    def squash_body(keep_ref, got_ref, _, out_ref):
        mix_body(keep_ref, got_ref, out_ref)

    (chip,) = call(squash_body, [((2, rows, bins), BF16)], (keep, got, keep_b[0]), "squash_sum")
    other = swap(chip, "mp", 2)
    got_b = swap(send_k, "ctx", 1), swap(send_p, "ctx", 2)

    def back_body(g_ref, mid_ref, chip_ref, other_ref, *outs):
        for i in (0, 1):
            grad = chip_ref[i].astype(F32) + other_ref[1 - i].astype(F32)
            outs[i][...] = (
                g_ref[i].astype(F32) + grad * slope_of(mid_ref[i].astype(F32))
            ).astype(BF16)

    g_mid = call(
        back_body, [((rows, bins), BF16)] * 2, (g_pair, mid, chip, other), "middle_grad"
    )
    g_mid = [g_mid[0], swap(g_mid[0], "mp", 1), g_mid[1], swap(g_mid[1], "mp", 1)]

    ykeep, ysend = call(
        output_body,
        [((2, rows, bins), F32), ((2, rows, bins), BF16)],
        (cols_b, v_b),
        "output_product",
    )
    ygot = swap(ysend, "mp", 1)

    def last_sum_body(keep_ref, got_ref, *rest):
        own_ref, send_ref = rest[-2:]
        own_ref[...] = keep_ref[0] + got_ref[0].astype(F32)
        send_ref[...] = (keep_ref[1] + got_ref[1].astype(F32)).astype(BF16)

    def last_sum(keep, got, name, after=()):
        outs = [((rows, bins), F32), ((rows, bins), BF16)]
        return call(last_sum_body, outs, (keep, got, *after), name)

    y_own, y_send = last_sum(ykeep, ygot, "out_sum")
    y_got = swap(y_send, "mp", 2)

    def out_body(mid_ref, own_ref, got_ref, out_ref):
        mixed = own_ref[...] + got_ref[...].astype(F32)
        out_ref[...] = (mid_ref[0].astype(F32) + mixed).astype(BF16)

    (second_out,) = call(out_body, [((rows, bins), BF16)], (mid, y_own, y_got), "out", final=True)

    def first_back_body(*refs):
        grads, (k_ref, p_ref, s_ref, gu_ref, send_ref) = refs[:4], refs[4:]
        m = lax.axis_index("mp")
        gv = jnp.zeros((hid, bins), F32)
        for j in range(4):
            gv = gv + dot(p_ref[:, block(m, j)], grads[j][...])
        gu = (gv * s_ref[...]).astype(BF16)
        gu_ref[...] = gu
        near_half(k_ref, gu, m, send_ref)

    gu_a, send = call(
        first_back_body,
        [(inner, BF16), ((2, rows, bins), BF16)],
        (*g_mid, tap_a, cols_a, slope_a),
        "first_backward",
    )
    keep = kept(tap_a, gu_a, "entry_keep")
    keep_ap, send_p, own_bk = call(
        first_proj_body,
        [(two, F32), (three, BF16), (one, F32)],
        (v_a, *g_mid, keep_b[0], got_b[0]),
        "first_proj",
        pack,
    )
    got_p = swap(send_p, "ctx", 2)
    keep_ak, send_k, own_bp = call(
        first_taps_body,
        [(two, F32), (three, BF16), (one, F32)],
        (z_own, z_near, z_far, z_cross, gu_a, keep_b[1], got_b[1]),
        "first_taps",
        pack,
    )
    got_k = swap(send_k, "ctx", 1)
    got = swap(send, "mp", 1)
    e_own, e_send = last_sum(keep, got, "entry_sum")
    e_got = swap(e_send, "mp", 2)

    def entry_body(g_ref, x_ref, own_ref, got_ref, out_ref):
        grad = own_ref[...] + got_ref[...].astype(F32)
        out_ref[...] = (
            g_ref[...].astype(F32) + grad * slope_of(x_ref[...].astype(F32))
        ).astype(BF16)

    (entry,) = call(entry_body, [((rows, bins), BF16)], (g_mid[0], x_own, e_own, e_got), "entry", final=True)

    half = [(one, F32), (one[1:], BF16)]
    own_ap, send_p = call(half_body, half, (keep_ap, got_p), "proj_half")
    last_p = swap(send_p, "ctx", 1)
    own_ak, send_k = call(half_body, half, (keep_ak, got_k, own_ap), "taps_half")
    last_k = swap(send_k, "ctx", 2)
    taps_b_grad, point_b_grad = total(2, planes[0], own_bk, own_bp, got_p, got_k, "second_total")
    taps_a_grad, point_a_grad = total(Ellipsis, planes[1], own_ak, own_ap, last_k, last_p, "first_total")
    return second_out, entry, taps_a_grad, point_a_grad, taps_b_grad, point_b_grad


def solution(mesh):
    sizes = dict(mesh.shape)

    def shards(x, *rest):
        span = x.shape[1] * sizes["ctx"]
        fast = (
            min(FIRST_DILATION, SECOND_DILATION) >= span
            and sizes["mp"] == 4
            and sizes["ctx"] == 4
        )
        return (fast_shards if fast else general_shards)(x, *rest)

    return jax.shard_map(
        shards,
        mesh=mesh,
        in_specs=(
            P("mp", ("groups", "ctx")),
            P(None, "mp", None),
            P(None, "mp"),
            P(None, "mp", None),
            P(None, "mp"),
            P("mp", "ctx", "groups"),
        ),
        out_specs=(
            P("mp", ("groups", "ctx")),
            P("mp", ("groups", "ctx")),
            P("groups", "mp", "ctx"),
            P(("groups", "ctx"), "mp"),
            P("groups", "mp", "ctx"),
            P(("groups", "ctx"), "mp"),
        ),
        check_vma=False,
    )
```

```python
import functools

import jax
import jax.numpy as jnp
from jax import lax
from jax.experimental import pallas as pl
from jax.experimental.pallas import tpu as pltpu
from jax.sharding import PartitionSpec as P

FIRST_DILATION = 1024
SECOND_DILATION = 2048
F32 = jnp.float32
BF16 = jnp.bfloat16
ROOT = 0.7978845608028654
CUBIC = 0.044715


def shifted(value, axis, by):
    length = lax.axis_size(axis)
    pairs = [(i, i + by) for i in range(length) if 0 <= i + by < length]
    return lax.ppermute(value, axis, pairs)


def gelu_slope(values):
    return jax.jvp(jax.nn.gelu, (values,), (jnp.ones_like(values),))[1]


def contract_first(left, right):
    return lax.dot_general(
        left, right, (((0,), (0,)), ((), ())), preferred_element_type=jnp.float32
    )


def contract_last(left, right):
    return lax.dot_general(
        left, right, (((1,), (1,)), ((), ())), preferred_element_type=jnp.float32
    )


def hop_steps(activations, dilation):
    return dilation // activations.shape[1]


def residual_block_forward(activations, conv_weight, point_weight, dilation):
    hop_count = hop_steps(activations, dilation)
    squash_part = jax.nn.gelu(activations.astype(jnp.float32)).astype(jnp.bfloat16)
    squashed = lax.all_gather(squash_part, "mp", axis=0, tiled=True)
    earlier = shifted(squashed, "ctx", hop_count)
    later = shifted(squashed, "ctx", -hop_count)
    pre_act = jnp.dot(conv_weight[0], earlier, preferred_element_type=jnp.float32)
    pre_act = pre_act + jnp.dot(conv_weight[1], squashed, preferred_element_type=jnp.float32)
    pre_act = pre_act + jnp.dot(conv_weight[2], later, preferred_element_type=jnp.float32)
    hidden = jax.nn.gelu(pre_act).astype(jnp.bfloat16)
    mixed = lax.psum_scatter(
        jnp.dot(point_weight, hidden, preferred_element_type=jnp.float32).astype(jnp.bfloat16),
        "mp",
        scatter_dimension=0,
        tiled=True,
    ).astype(jnp.float32)
    result = (activations.astype(jnp.float32) + mixed).astype(jnp.bfloat16)
    return (result, squashed, pre_act, hidden)


def residual_block_backward(
    incoming_gradient, activations, squashed, pre_act, hidden, conv_weight, point_weight, dilation
):
    hop_count = hop_steps(activations, dilation)
    upstream_full = lax.all_gather(incoming_gradient, "mp", axis=0, tiled=True)
    grad_hidden = contract_first(point_weight, upstream_full)
    grad_pre = (grad_hidden * gelu_slope(pre_act)).astype(jnp.bfloat16)
    grad_later = shifted(grad_pre, "ctx", -hop_count)
    grad_earlier = shifted(grad_pre, "ctx", hop_count)
    moved = (grad_later, grad_pre, grad_earlier)
    grad_conv = jnp.stack([contract_last(part, squashed) for part in moved])
    grad_point = contract_last(upstream_full, hidden)
    total = contract_first(conv_weight[0], moved[0])
    total = total + contract_first(conv_weight[1], moved[1])
    grad_squash = lax.psum_scatter(
        (total + contract_first(conv_weight[2], moved[2])).astype(jnp.bfloat16),
        "mp",
        scatter_dimension=0,
        tiled=True,
    ).astype(jnp.float32)
    previous = (
        incoming_gradient.astype(jnp.float32)
        + grad_squash * gelu_slope(activations.astype(jnp.float32))
    ).astype(jnp.bfloat16)
    return (previous, grad_conv, grad_point)


def reduce_block(grad_conv, grad_point):
    return (
        lax.psum_scatter(
            grad_conv.astype(jnp.bfloat16), "ctx", scatter_dimension=2, tiled=True
        ).astype(jnp.float32),
        lax.psum_scatter(
            grad_point.astype(jnp.bfloat16), "ctx", scatter_dimension=0, tiled=True
        ).astype(jnp.float32),
    )


def general_shards(x, taps_a, point_a, taps_b, point_b, grad_heads):
    regrouped = lax.all_to_all(grad_heads, "ctx", split_axis=2, concat_axis=1, tiled=True)
    gradient = regrouped.reshape(regrouped.shape[0] * regrouped.shape[1], regrouped.shape[2])
    middle, z_a, u_a, v_a = residual_block_forward(x, taps_a, point_a, FIRST_DILATION)
    result, z_b, u_b, v_b = residual_block_forward(middle, taps_b, point_b, SECOND_DILATION)
    gradient, conv_b, proj_b = residual_block_backward(
        gradient, middle, z_b, u_b, v_b, taps_b, point_b, SECOND_DILATION
    )
    conv_b, proj_b = reduce_block(conv_b, proj_b)
    gradient, conv_a, proj_a = residual_block_backward(
        gradient, x, z_a, u_a, v_a, taps_a, point_a, FIRST_DILATION
    )
    conv_a, proj_a = reduce_block(conv_a, proj_a)
    return result, gradient, conv_a, proj_a, conv_b, proj_b


def swap(value, axis, bits):
    size = lax.axis_size(axis)
    return lax.ppermute(value, axis, [(i, i ^ bits) for i in range(size)])


def dot(left, right, dims=((1,), (0,))):
    return lax.dot_general(left, right, (dims, ((), ())), preferred_element_type=F32)


def gelu(s):
    return 0.5 * s * (1.0 + jnp.tanh(ROOT * (s + CUBIC * (s * s * s))))


def gelu_and_slope(s):
    sq = s * s
    t = jnp.tanh(ROOT * (s + CUBIC * (s * sq)))
    half = 0.5 * (1.0 + t)
    slope = half + 0.5 * s * (1.0 - t * t) * (ROOT * (1.0 + 3.0 * CUBIC * sq))
    return s * half, slope


def slope_of(s):
    return gelu_and_slope(s)[1]


VMEM = pl.BlockSpec(memory_space=pltpu.VMEM)


def call(body, outs, args, name, scratch=(), final=False, alias=None):
    struct = jax.ShapeDtypeStruct if final else pltpu.VMEM
    return pl.pallas_call(
        body,
        out_shape=[struct(s, d) for s, d in outs],
        in_specs=[VMEM] * len(args),
        out_specs=[VMEM] * len(outs),
        scratch_shapes=scratch,
        input_output_aliases=alias or {},
        compiler_params=pltpu.CompilerParams(vmem_limit_bytes=16 << 20),
        name=name,
    )(*[pltpu.with_memory_space_constraint(a, pltpu.VMEM) for a in args])


def fast_shards(x, taps_a, point_a, taps_b, point_b, grad_heads):
    rows, bins = x.shape
    hid, chans = taps_a.shape[1], taps_a.shape[2]
    heads, val, _ = grad_heads.shape
    def block(m, j):
        return pl.ds(pl.multiple_of((m ^ j) * rows, rows), rows)

    x_far = swap(x, "mp", 2)

    raw_far = swap(grad_heads, "mp", 2)

    def load_body(x_ref, ta, tb, ca, cb, g_ref, *rest):
        outs, sems = rest[:-1], rest[-1]
        sources = [x_ref, ta.at[1], tb.at[1], ca, cb, g_ref]
        copies = [
            pltpu.make_async_copy(source, out, sems.at[i])
            for i, (source, out) in enumerate(zip(sources, outs))
        ]
        for copy in copies:
            copy.start()
        for copy in copies:
            copy.wait()

    x_own, tap_a, tap_b, cols_a, cols_b, raw_own = pl.pallas_call(
        load_body,
        out_shape=[pltpu.VMEM((rows, bins), BF16)]
        + [pltpu.VMEM((hid, chans), BF16)] * 4
        + [pltpu.VMEM(grad_heads.shape, BF16)],
        in_specs=[pl.BlockSpec(memory_space=pltpu.HBM)] * 6,
        out_specs=[VMEM] * 6,
        scratch_shapes=[pltpu.SemaphoreType.DMA((6,))],
        compiler_params=pltpu.CompilerParams(vmem_limit_bytes=16 << 20),
        name="load",
    )(
        *[
            pltpu.with_memory_space_constraint(source, pltpu.HBM)
            for source in (x, taps_a, taps_b, point_a.T, point_b.T, grad_heads)
        ]
    )

    def conv(refs, js, m, k_ref, z_ref, u):
        for ref, j in zip(refs, js):
            z = gelu(ref[...].astype(F32)).astype(BF16)
            z_ref[j] = z
            part = dot(k_ref[:, block(m, j)], z)
            u = part if u is None else u + part
        return u

    stack = ((4, rows, bins), BF16)
    inner = (hid, bins)

    def near_forward_body(x_ref, k_ref, z_ref, u_ref):
        z = gelu(x_ref[...].astype(F32)).astype(BF16)
        z_ref[...] = z
        u_ref[...] = dot(k_ref[:, block(lax.axis_index("mp"), 0)], z)

    def far_forward_body(x_ref, k_ref, u_in, z_ref, u_ref):
        z = gelu(x_ref[...].astype(F32)).astype(BF16)
        z_ref[...] = z
        u_ref[...] = u_in[...] + dot(k_ref[:, block(lax.axis_index("mp"), 2)], z)

    half_z = [((rows, bins), BF16), (inner, F32)]
    z_own, u_a = call(near_forward_body, half_z, (x_own, tap_a), "near_forward")
    x_far, u_a = lax.optimization_barrier((x_far, u_a))
    z_far, u_a = call(far_forward_body, half_z, (x_far, tap_a, u_a), "far_forward")
    z_near, z_cross = swap(z_own, "mp", 1), swap(z_far, "mp", 1)

    def split_body(own_ref, far_ref, *outs):
        c = lax.axis_index("ctx")
        for k in range(4):
            at = pl.ds(pl.multiple_of((c ^ k) * bins, bins), bins)
            for i, ref in enumerate((own_ref, far_ref)):
                outs[k][i] = ref[:, :, at]

    piece = ((2, heads, val, bins), BF16)
    pieces = call(split_body, [piece] * 4, (raw_own, raw_far), "split_grad")
    pieces = [pieces[0]] + [swap(pieces[k], "ctx", k) for k in (1, 2, 3)]

    def join_body(*refs):
        c = lax.axis_index("ctx")
        out = refs[4]
        for k in range(4):
            out[:, :, c ^ k] = refs[k][...]

    (g_pair,) = call(join_body, [((2, heads, 4, val, bins), BF16)], pieces, "join_grad")
    g_pair = g_pair.reshape(2, rows, bins)
    g_near = swap(g_pair, "mp", 1)

    def near_half(w_ref, v, m, send_ref):
        for i, j in enumerate((1, 3)):
            send_ref[i] = dot(w_ref[:, block(m, j)], v, ((0,), (0,))).astype(BF16)

    def own_half(w_ref, v, m, keep_ref):
        for i, j in enumerate((0, 2)):
            keep_ref[i] = dot(w_ref[:, block(m, j)], v, ((0,), (0,)))

    def keep_body(w_ref, v_ref, keep_ref):
        own_half(w_ref, v_ref[...], lax.axis_index("mp"), keep_ref)

    def kept(w, v, name):
        return call(keep_body, [((2, rows, bins), F32)], (w, v), name)[0]

    def first_body(z1, z3, k_ref, p_ref, _, u_ref, v_ref, s_ref, send_ref):
        m = lax.axis_index("mp")
        u = u_ref[...] + dot(k_ref[:, block(m, 1)], z1[...])
        u = u + dot(k_ref[:, block(m, 3)], z3[...])
        v, slope = gelu_and_slope(u)
        v = v.astype(BF16)
        v_ref[...] = v
        s_ref[...] = slope
        near_half(p_ref, v, m, send_ref)

    v_a, slope_a, send = call(
        first_body,
        [(inner, BF16), (inner, F32), ((2, rows, bins), BF16)],
        (z_near, z_cross, tap_a, cols_a, raw_far, u_a),
        "first_forward",
    )
    keep = kept(cols_a, v_a, "mix_keep")
    got = swap(send, "mp", 1)

    def mix_body(keep_ref, got_ref, out_ref):
        out_ref[...] = (keep_ref[...] + got_ref[...].astype(F32)).astype(BF16)

    (chip,) = call(mix_body, [((2, rows, bins), BF16)], (keep, got), "mix_sum")
    other = swap(chip, "mp", 2)

    def middle_body(x0, x2, chip_ref, other_ref, out_ref):
        for i, ref in enumerate((x0, x2)):
            mixed = chip_ref[i].astype(F32) + other_ref[1 - i].astype(F32)
            out_ref[i] = (ref[...].astype(F32) + mixed).astype(BF16)

    (mid,) = call(
        middle_body, [((2, rows, bins), BF16)], (x_own, x_far, chip, other), "middle"
    )
    mid_near = swap(mid, "mp", 1)

    def own_block_body(a_ref, g_ref, k_ref, p_ref, z_ref, u_ref, gv_ref):
        m = lax.axis_index("mp")
        parts = (a_ref.at[0], a_ref.at[1])
        u_ref[...] = conv(parts, (0, 2), m, k_ref, z_ref, None)
        gv = dot(p_ref[:, block(m, 0)], g_ref[0])
        gv_ref[...] = gv + dot(p_ref[:, block(m, 2)], g_ref[1])

    z_b, u_b, gv_b = call(
        own_block_body,
        [stack, (inner, F32), (inner, F32)],
        (mid, g_pair, tap_b, cols_b),
        "own_block",
    )

    def second_body(
        b_ref, g_ref, k_ref, p_ref, u_ref, gv_ref, zin_ref, z_ref, v_ref, gu_ref, send_ref
    ):
        m = lax.axis_index("mp")
        u = conv((b_ref.at[0], b_ref.at[1]), (1, 3), m, k_ref, z_ref, u_ref[...])
        v, slope = gelu_and_slope(u)
        v_ref[...] = v.astype(BF16)
        gv = gv_ref[...] + dot(p_ref[:, block(m, 1)], g_ref[0])
        gv = gv + dot(p_ref[:, block(m, 3)], g_ref[1])
        gu = (gv * slope).astype(BF16)
        gu_ref[...] = gu
        near_half(k_ref, gu, m, send_ref)

    z_b, v_b, gu_b, send = call(
        second_body,
        [stack, (inner, BF16), (inner, BF16), ((2, rows, bins), BF16)],
        (mid_near, g_near, tap_b, cols_b, u_b, gv_b, z_b),
        "second_block",
        alias={6: 0},
    )
    keep = kept(tap_b, gu_b, "squash_keep")

    def output_body(p_ref, v_ref, keep_ref, send_ref):
        m = lax.axis_index("mp")
        near_half(p_ref, v_ref[...], m, send_ref)
        own_half(p_ref, v_ref[...], m, keep_ref)

    def place(k):
        return lax.axis_index("mp") ^ lax.axis_index("ctx") ^ k

    def taps_pieces(z_ref, gu_ref, keep, send):
        for i in (0, 1):
            send[i] = dot(gu_ref[...], z_ref[place(1 + 2 * i)], ((1,), (1,))).astype(BF16)
        for i in (0, 1):
            keep[i] = dot(gu_ref[...], z_ref[place(2 * i)], ((1,), (1,)))

    def proj_pieces(v_ref, g_ref, keep, send):
        for i in (0, 1):
            send[i] = dot(v_ref[...], g_ref[place(2 + i)], ((1,), (1,))).astype(BF16)
        for i in (0, 1):
            keep[i] = dot(v_ref[...], g_ref[place(i)], ((1,), (1,)))

    one, two, three = ((n, hid, rows) for n in (1, 2, 3))

    def second_weight_body(z_ref, gu_ref, v_ref, ga_ref, gb_ref, *rest):
        keep_k, keep_p, send_k, send_p, g_ref = rest
        for i in range(4):
            g_ref[i] = (ga_ref, gb_ref)[i & 1][i >> 1]
        proj_pieces(v_ref, g_ref, keep_p, send_p)
        taps_pieces(z_ref, gu_ref, keep_k, send_k)

    def half_sum(keep, got, own):
        own[0] = keep[0] + got[0].astype(F32)
        return (keep[1] + got[1].astype(F32)).astype(BF16)

    def first_proj_body(v_ref, g0, g1, g2, g3, keep_b, got_b, keep, send, own, g_ref):
        for i, ref in enumerate((g0, g1, g2, g3)):
            g_ref[i] = ref[...]
        send[2] = half_sum(keep_b, got_b, own)
        proj_pieces(v_ref, g_ref, keep, send)

    def first_taps_body(z0, z1, z2, z3, gu_ref, keep_b, got_b, keep, send, own, z_ref):
        for i, ref in enumerate((z0, z1, z2, z3)):
            z_ref[i] = ref[...]
        send[2] = half_sum(keep_b, got_b, own)
        taps_pieces(z_ref, gu_ref, keep, send)

    def half_body(keep, got, *rest):
        own, send = rest[-2:]
        send[...] = half_sum(keep, got, own)

    plane = ((3, hid, rows), F32)
    hbm = pl.BlockSpec(memory_space=pltpu.HBM)

    def zero_body(*refs):
        outs, (zero, sems) = refs[:2], refs[2:]
        zero[...] = jnp.zeros((hid, rows), F32)
        copies = [
            pltpu.make_async_copy(zero, out.at[tap], sems.at[2 * i + tap // 2])
            for i, out in enumerate(outs)
            for tap in (0, 2)
        ]
        for copy in copies:
            copy.start()
        for copy in copies:
            copy.wait()

    def total_body(place, _, own_k, own_p, got_k, got_p, taps_ref, proj_ref, k, p, sems):
        k[...] = own_k[0] + got_k[place].astype(F32)
        first = pltpu.make_async_copy(k, taps_ref.at[1], sems.at[0])
        first.start()
        p[...] = own_p[0] + got_p[place].astype(F32)
        second = pltpu.make_async_copy(p, proj_ref, sems.at[1])
        second.start()
        first.wait()
        second.wait()

    def total(place, planes, own_k, own_p, got_k, got_p, name):
        taps, proj = pl.pallas_call(
            functools.partial(total_body, place),
            out_shape=[jax.ShapeDtypeStruct(*plane), jax.ShapeDtypeStruct((hid, rows), F32)],
            in_specs=[hbm] + [VMEM] * 4,
            out_specs=[hbm, hbm],
            scratch_shapes=[pltpu.VMEM((hid, rows), F32)] * 2 + [pltpu.SemaphoreType.DMA((2,))],
            input_output_aliases={0: 0},
            compiler_params=pltpu.CompilerParams(vmem_limit_bytes=16 << 20),
            name=name,
        )(
            pltpu.with_memory_space_constraint(planes, pltpu.HBM),
            *[
                pltpu.with_memory_space_constraint(a, pltpu.VMEM)
                for a in (own_k, own_p, got_k, got_p)
            ],
        )
        return taps, proj.T

    planes = pl.pallas_call(
        zero_body,
        out_shape=[pltpu.HBM(*plane)] * 2,
        in_specs=[],
        out_specs=[hbm, hbm],
        scratch_shapes=[pltpu.VMEM((hid, rows), F32), pltpu.SemaphoreType.DMA((4,))],
        compiler_params=pltpu.CompilerParams(vmem_limit_bytes=16 << 20),
        name="zero_planes",
    )()

    pack = [pltpu.VMEM((4, rows, bins), BF16)]
    *keep_b, send_k, send_p = call(
        second_weight_body,
        [(two, F32), (two, F32), (two, BF16), (two, BF16)],
        (z_b, gu_b, v_b, g_pair, g_near),
        "second_weights",
        pack,
    )
    got = swap(send, "mp", 1)

    def squash_body(keep_ref, got_ref, _, out_ref):
        mix_body(keep_ref, got_ref, out_ref)

    (chip,) = call(squash_body, [((2, rows, bins), BF16)], (keep, got, keep_b[0]), "squash_sum")
    other = swap(chip, "mp", 2)
    got_b = swap(send_k, "ctx", 1), swap(send_p, "ctx", 2)

    def back_body(g_ref, mid_ref, chip_ref, other_ref, *outs):
        for i in (0, 1):
            grad = chip_ref[i].astype(F32) + other_ref[1 - i].astype(F32)
            outs[i][...] = (
                g_ref[i].astype(F32) + grad * slope_of(mid_ref[i].astype(F32))
            ).astype(BF16)

    g_mid = call(
        back_body, [((rows, bins), BF16)] * 2, (g_pair, mid, chip, other), "middle_grad"
    )
    g_mid = [g_mid[0], swap(g_mid[0], "mp", 1), g_mid[1], swap(g_mid[1], "mp", 1)]

    ykeep, ysend = call(
        output_body,
        [((2, rows, bins), F32), ((2, rows, bins), BF16)],
        (cols_b, v_b),
        "output_product",
    )
    ygot = swap(ysend, "mp", 1)

    def last_sum_body(keep_ref, got_ref, *rest):
        own_ref, send_ref = rest[-2:]
        own_ref[...] = keep_ref[0] + got_ref[0].astype(F32)
        send_ref[...] = (keep_ref[1] + got_ref[1].astype(F32)).astype(BF16)

    def last_sum(keep, got, name, after=()):
        outs = [((rows, bins), F32), ((rows, bins), BF16)]
        return call(last_sum_body, outs, (keep, got, *after), name)

    y_own, y_send = last_sum(ykeep, ygot, "out_sum")
    y_got = swap(y_send, "mp", 2)

    def out_body(mid_ref, own_ref, got_ref, out_ref):
        mixed = own_ref[...] + got_ref[...].astype(F32)
        out_ref[...] = (mid_ref[0].astype(F32) + mixed).astype(BF16)

    (second_out,) = call(out_body, [((rows, bins), BF16)], (mid, y_own, y_got), "out", final=True)

    def first_back_body(*refs):
        grads, (k_ref, p_ref, s_ref, gu_ref, send_ref) = refs[:4], refs[4:]
        m = lax.axis_index("mp")
        gv = jnp.zeros((hid, bins), F32)
        for j in range(4):
            gv = gv + dot(p_ref[:, block(m, j)], grads[j][...])
        gu = (gv * s_ref[...]).astype(BF16)
        gu_ref[...] = gu
        near_half(k_ref, gu, m, send_ref)

    gu_a, send = call(
        first_back_body,
        [(inner, BF16), ((2, rows, bins), BF16)],
        (*g_mid, tap_a, cols_a, slope_a),
        "first_backward",
    )
    keep = kept(tap_a, gu_a, "entry_keep")
    keep_ap, send_p, own_bk = call(
        first_proj_body,
        [(two, F32), (three, BF16), (one, F32)],
        (v_a, *g_mid, keep_b[0], got_b[0]),
        "first_proj",
        pack,
    )
    got_p = swap(send_p, "ctx", 2)
    keep_ak, send_k, own_bp = call(
        first_taps_body,
        [(two, F32), (three, BF16), (one, F32)],
        (z_own, z_near, z_far, z_cross, gu_a, keep_b[1], got_b[1]),
        "first_taps",
        pack,
    )
    got_k = swap(send_k, "ctx", 1)
    got = swap(send, "mp", 1)
    e_own, e_send = last_sum(keep, got, "entry_sum", (keep_ak,))
    e_got = swap(e_send, "mp", 2)

    def entry_body(g_ref, x_ref, own_ref, got_ref, out_ref):
        grad = own_ref[...] + got_ref[...].astype(F32)
        out_ref[...] = (
            g_ref[...].astype(F32) + grad * slope_of(x_ref[...].astype(F32))
        ).astype(BF16)

    (entry,) = call(entry_body, [((rows, bins), BF16)], (g_mid[0], x_own, e_own, e_got), "entry", final=True)

    half = [(one, F32), (one[1:], BF16)]
    own_ap, send_p = call(half_body, half, (keep_ap, got_p), "proj_half")
    last_p = swap(send_p, "ctx", 1)
    own_ak, send_k = call(half_body, half, (keep_ak, got_k, own_ap), "taps_half")
    last_k = swap(send_k, "ctx", 2)
    taps_b_grad, point_b_grad = total(2, planes[0], own_bk, own_bp, got_p, got_k, "second_total")
    taps_a_grad, point_a_grad = total(Ellipsis, planes[1], own_ak, own_ap, last_k, last_p, "first_total")
    return second_out, entry, taps_a_grad, point_a_grad, taps_b_grad, point_b_grad


def solution(mesh):
    sizes = dict(mesh.shape)

    def shards(x, *rest):
        span = x.shape[1] * sizes["ctx"]
        fast = (
            min(FIRST_DILATION, SECOND_DILATION) >= span
            and sizes["mp"] == 4
            and sizes["ctx"] == 4
        )
        return (fast_shards if fast else general_shards)(x, *rest)

    return jax.shard_map(
        shards,
        mesh=mesh,
        in_specs=(
            P("mp", ("groups", "ctx")),
            P(None, "mp", None),
            P(None, "mp"),
            P(None, "mp", None),
            P(None, "mp"),
            P("mp", "ctx", "groups"),
        ),
        out_specs=(
            P("mp", ("groups", "ctx")),
            P("mp", ("groups", "ctx")),
            P("groups", "mp", "ctx"),
            P(("groups", "ctx"), "mp"),
            P("groups", "mp", "ctx"),
            P(("groups", "ctx"), "mp"),
        ),
        check_vma=False,
    )
```
